512 devices in a mesh: ep: 8 (over y), etp: 64 (over z, x, core).
Axes of the slice: x: 4, y: 8, z: 8, core: 2. Of those that a mesh axis runs over, the one named last changes fastest.
Arguments:
- tokens: bfloat16 [384, 3072], P('ep', 'etp'), may hold values from -6 to 6
- routes: int32 [384, 2], P('ep'), may hold values from 0 to 7, as said below
- route_gates: float32 [384, 2], P('ep'), may hold values from 0.1 to 0.9
- cotangent: bfloat16 [384, 3072], P('ep', 'etp'), may hold values from -1.5 to 1.5
- w_gate: bfloat16 [8, 3072, 8192], P('ep', None, 'etp'), may hold values from -0.109375 to 0.109375
- w_up: bfloat16 [8, 3072, 8192], P('ep', None, 'etp'), may hold values from -0.109375 to 0.109375
- w_down: bfloat16 [8, 8192, 3072], P('ep', 'etp'), may hold values from -0.1875 to 0.1875
Outputs:
- mixed: bfloat16 [384, 3072], P('ep', 'etp')
- grad_gates: float32 [384, 2], P('ep')
- grad_w_gate: bfloat16 [8, 3072, 8192], P('ep', None, 'etp')
- grad_w_up: bfloat16 [8, 3072, 8192], P('ep', None, 'etp')
- grad_w_down: bfloat16 [8, 8192, 3072], P('ep', 'etp')
The draws below stay inside these ranges and needn't reach their ends.
Inputs may be any that keep to these rules, and one draw needn't show every extreme that they name: `routes`: within each aligned block of 48 rows (the tokens of one index of ep) the two experts of a row differ and no expert is named by more than 24 rows; one expert, the same in every block, is named by exactly 24 rows of each block.
All inputs are finite; a program needn't handle non-finite values.
Results may differ from the reference program's by a relative error of at most 0.0058.
Values may be sent and summed in bfloat16 or wider, within the bound.
A program may use at most 64 MiB of HBM per device.

```python
import jax
import jax.numpy as jnp

D = 3072
FF = 8192
EXPERTS = 8
TOP = 2
TOK_EP = 48
CAP = 24
TOKENS = 384


def draw_routes(key, part):
    block_count = TOKENS // TOK_EP
    slot_share = CAP // 3
    others = EXPERTS - 1
    rest_rows = TOK_EP - CAP
    hot_expert = jax.random.randint(jax.random.fold_in(key, 7), (), 0, EXPERTS)

    def lift_past(values):
        return values + (values >= hot_expert).astype(jnp.int32)

    def one_block(block_index):
        block_key = jax.random.fold_in(key, block_index + 11)
        key_one, key_two, key_three, key_four, key_five = jax.random.split(block_key, 5)
        pool_a = jax.random.permutation(key_one, others * slot_share)[:CAP] // slot_share
        pool_b = jax.random.permutation(key_two, others * slot_share)[:rest_rows] // slot_share
        shift_by = jax.random.randint(key_three, (), 1, others)
        second_b = (pool_b + shift_by) % others
        first_pick = jnp.concatenate([jnp.full((CAP,), hot_expert, jnp.int32), lift_past(pool_b.astype(jnp.int32))])
        second_pick = jnp.concatenate([lift_past(pool_a.astype(jnp.int32)), lift_past(second_b.astype(jnp.int32))])
        swap_cols = jax.random.randint(key_four, (TOK_EP,), 0, 2)
        column_one = jnp.where(swap_cols == 1, second_pick, first_pick)
        column_two = jnp.where(swap_cols == 1, first_pick, second_pick)
        row_order = jax.random.permutation(key_five, TOK_EP)
        return jnp.stack([column_one, column_two], axis=1)[row_order]
    blocks = jax.vmap(one_block)(jnp.arange(block_count, dtype=jnp.int32))
    return blocks.reshape(TOKENS, 2).astype(jnp.int32)


def strengthened(result, own_key, source, target, shards_of, factor):
    def block_of(dim):
        return (jnp.arange(result.shape[dim]) // (result.shape[dim] // shards_of)).reshape((-1,) + (1,) * (result.ndim - 1 - dim))

    near = jax.random.permutation(own_key, shards_of)[block_of(target)]
    far = (block_of(target) + shards_of // 2) % shards_of
    return jnp.where((block_of(source) == near) | (block_of(source) == far), factor * result, result)


def block_levels(stream_key, dims, shards, low, top_value):
    loudness, own = 1.0, jax.random.fold_in(stream_key, 6)
    for dim, shards_of in shards:
        draws = jnp.exp(jax.random.uniform(jax.random.fold_in(own, dim), (shards_of,), jnp.float32, low / len(shards), top_value / len(shards)))
        loudness = loudness * jnp.repeat(draws, dims[dim] // shards_of).reshape([-1 if axis == dim else 1 for axis in range(len(dims))])
    return loudness


def bell_draw(stream_key, shape, scale, bound, shards=(), held_as=jnp.bfloat16):
    array = scale * jax.random.normal(stream_key, shape, jnp.float32)
    if shards:
        array = array * block_levels(stream_key, shape, shards, -0.22, 0.18)
    return jnp.clip(array, -bound, bound).astype(held_as)


def heavy_noise(rng, shape, spread, limit, shards, heavy, kind=jnp.bfloat16):
    result = spread * jax.random.normal(rng, shape, jnp.float32)
    if shards:
        result = result * block_levels(rng, shape, shards, -0.22, 0.18)
    return jnp.clip(strengthened(result, jax.random.fold_in(rng, 3), *heavy), -limit, limit).astype(kind)


def setup_inputs(seed: int = 0) -> dict:
    splits = jax.random.split(jax.random.key(seed), 8)
    tokens = bell_draw(splits[0], (TOKENS, D), 1.0, 6.0, ((0, 8), (1, 64)))
    routes = draw_routes(jax.random.fold_in(splits[7], 71), 0)
    route_gates = jnp.clip(0.1 + 0.79999997 * jax.random.uniform(splits[2], (TOKENS, TOP), jnp.float32) ** block_levels(splits[2], (TOKENS, TOP), ((0, 8),), -0.2, 0.2), 0.1, 0.9)
    cotangent = bell_draw(splits[3], (TOKENS, D), 0.25, 1.5, ((0, 8), (1, 64)))
    w_gate = bell_draw(splits[4], (EXPERTS, D, FF), D ** -0.5, 0.109375, ((0, 8), (2, 64)))
    w_up = bell_draw(splits[5], (EXPERTS, D, FF), D ** -0.5, 0.109375, ((0, 8), (2, 64)))
    w_down = heavy_noise(splits[6], (EXPERTS, FF, D), FF ** -0.5, 0.1875, ((0, 8), (1, 64)), (1, 2, 64, 4.0))
    return {"tokens": tokens, "routes": routes, "route_gates": route_gates, "cotangent": cotangent, "w_gate": w_gate, "w_up": w_up, "w_down": w_down}


def reference(tokens, routes, route_gates, cotangent, w_gate, w_up, w_down):
    block_count = TOKENS // TOK_EP
    flat_ids = routes.reshape(-1).astype(jnp.int32)
    pair_count = flat_ids.shape[0]
    onehot = (flat_ids[:, None] == jnp.arange(EXPERTS, dtype=jnp.int32)[None, :]).astype(jnp.int32)
    blocked = onehot.reshape(block_count, 2 * TOK_EP, EXPERTS)
    before = (jnp.cumsum(blocked, axis=1) - blocked).reshape(pair_count, EXPERTS)
    slot_id = jnp.sum(before * onehot, axis=1).astype(jnp.int32)
    position = (jnp.arange(pair_count, dtype=jnp.int32) // (2 * TOK_EP)).astype(jnp.int32) * CAP + slot_id
    slot_rows = block_count * CAP
    x_pad = jnp.concatenate([tokens, jnp.zeros((1, D), tokens.dtype)], axis=0)
    dy_pad = jnp.concatenate([cotangent, jnp.zeros((1, D), cotangent.dtype)], axis=0)
    gate_flat = jnp.concatenate([route_gates.reshape(-1).astype(jnp.float32), jnp.zeros((1,), jnp.float32)])
    mixed_acc = jnp.zeros((TOKENS + 1, D), jnp.float32)
    grad_acc = jnp.zeros((pair_count + 1,), jnp.float32)
    grads_gate, grads_up, grads_down = [], [], []
    for expert in range(EXPERTS):
        target = jnp.where(flat_ids == expert, position, slot_rows).astype(jnp.int32)
        slot_table = jnp.full((slot_rows,), pair_count, jnp.int32).at[target].set(
            jnp.arange(pair_count, dtype=jnp.int32), mode="drop")
        token_of_slot = (slot_table // 2).astype(jnp.int32)
        slot_gate = gate_flat[slot_table][:, None]
        rows_x = x_pad[token_of_slot]
        rows_dy = (slot_gate * dy_pad[token_of_slot].astype(jnp.float32)).astype(jnp.bfloat16)
        gate_pre = jnp.dot(rows_x, w_gate[expert], preferred_element_type=jnp.float32)
        up_pre = jnp.dot(rows_x, w_up[expert], preferred_element_type=jnp.float32)
        sigma = jax.nn.sigmoid(gate_pre)
        hidden = (jax.nn.silu(gate_pre) * up_pre).astype(jnp.bfloat16)
        expert_out = jnp.dot(hidden, w_down[expert], preferred_element_type=jnp.float32)
        mixed_acc = mixed_acc.at[token_of_slot].add(slot_gate * expert_out)
        inner = jnp.sum(expert_out * dy_pad[token_of_slot].astype(jnp.float32), axis=1)
        grad_acc = grad_acc.at[slot_table].add(inner)
        d_hidden = jnp.dot(rows_dy, w_down[expert].T, preferred_element_type=jnp.float32)
        d_up = (d_hidden * jax.nn.silu(gate_pre)).astype(jnp.bfloat16)
        d_gate = (d_hidden * up_pre * sigma * (1.0 + gate_pre * (1.0 - sigma))).astype(jnp.bfloat16)
        grads_down.append(jnp.dot(hidden.T, rows_dy, preferred_element_type=jnp.float32).astype(jnp.bfloat16))
        grads_gate.append(jnp.dot(rows_x.T, d_gate, preferred_element_type=jnp.float32).astype(jnp.bfloat16))
        grads_up.append(jnp.dot(rows_x.T, d_up, preferred_element_type=jnp.float32).astype(jnp.bfloat16))
    mixed = mixed_acc[:TOKENS].astype(jnp.bfloat16)
    grad_gates = grad_acc[:pair_count].reshape(TOKENS, 2)
    return (mixed, grad_gates, jnp.stack(grads_gate), jnp.stack(grads_up), jnp.stack(grads_down))
```

```python
import jax
import jax.numpy as jnp
import numpy as np
from jax import lax
from jax.sharding import Mesh
from jax.sharding import PartitionSpec as P

EXPERTS = 8
CAP = 24
SUB = ("z", "x", "core")


def sub_sizes(etp):
    if etp % 8 == 0:
        return (etp // 8, 4, 2)
    return (etp, 1, 1)


def per_device(tokens, routes, route_gates, cotangent, w_gate, w_up, w_down):
    ep_count = lax.axis_size("ep")
    nz, nx, nc = lax.axis_size("z"), lax.axis_size("x"), lax.axis_size("core")
    tok_count, width = tokens.shape
    flat_ids = routes.reshape(-1)
    pair_count = flat_ids.shape[0]
    onehot = (flat_ids[:, None] == jnp.arange(EXPERTS, dtype=jnp.int32)[None, :]).astype(jnp.int32)
    before = jnp.cumsum(onehot, axis=0) - onehot
    slot_id = jnp.sum(before * onehot, axis=1)
    target = flat_ids * CAP + slot_id
    slot_table = (
        jnp.full((EXPERTS * CAP,), pair_count, jnp.int32)
        .at[target]
        .set(jnp.arange(pair_count, dtype=jnp.int32))
    )
    token_of_slot = slot_table // 2
    gate_flat = jnp.concatenate([route_gates.reshape(-1), jnp.zeros((1,), jnp.float32)])
    slot_gate = gate_flat[slot_table]
    xc = jnp.concatenate([tokens, cotangent], axis=1)
    xc_pad = jnp.concatenate([xc, jnp.zeros((1, 2 * width), jnp.bfloat16)], axis=0)
    sent = xc_pad[token_of_slot].reshape(ep_count, CAP, 2 * width)
    recv = lax.all_to_all(sent, "ep", 0, 0, tiled=True)
    gates_recv = lax.all_to_all(slot_gate.reshape(ep_count, CAP), "ep", 0, 0, tiled=True)
    rows = ep_count * CAP
    chunk = recv.reshape(rows, 2 * width)
    g = lax.all_gather(chunk, "z", axis=0)
    g = lax.all_gather(g, "x", axis=0)
    g = lax.all_gather(g, "core", axis=0)
    g = jnp.transpose(g, (3, 2, 1, 0, 4))
    rows_x = g[..., :width].reshape(rows, -1)
    cot_rows = g[..., width:].reshape(rows, -1)
    slot_g = gates_recv.reshape(rows, 1)
    rows_dy = (slot_g * cot_rows.astype(jnp.float32)).astype(jnp.bfloat16)
    wg, wu, wd = w_gate[0], w_up[0], w_down[0]
    gate_pre = jnp.dot(rows_x, wg, preferred_element_type=jnp.float32)
    up_pre = jnp.dot(rows_x, wu, preferred_element_type=jnp.float32)
    sigma = jax.nn.sigmoid(gate_pre)
    hidden = (jax.nn.silu(gate_pre) * up_pre).astype(jnp.bfloat16)
    output_part = jnp.dot(hidden, wd, preferred_element_type=jnp.float32)
    d_hidden = lax.dot_general(rows_dy, wd, (((1,), (1,)), ((), ())), preferred_element_type=jnp.float32)
    d_up = (d_hidden * jax.nn.silu(gate_pre)).astype(jnp.bfloat16)
    d_gate = (d_hidden * up_pre * sigma * (1.0 + gate_pre * (1.0 - sigma))).astype(jnp.bfloat16)
    grad_down = lax.dot_general(hidden, rows_dy, (((0,), (0,)), ((), ())), preferred_element_type=jnp.float32)
    grad_gate_w = lax.dot_general(rows_x, d_gate, (((0,), (0,)), ((), ())), preferred_element_type=jnp.float32)
    grad_up_w = lax.dot_general(rows_x, d_up, (((0,), (0,)), ((), ())), preferred_element_type=jnp.float32)
    inner = jnp.sum(output_part * cot_rows.astype(jnp.float32), axis=1)
    part = output_part.reshape(rows, nz, nx, nc, width)
    part = jnp.transpose(part, (3, 2, 1, 0, 4))
    extra = jnp.broadcast_to(inner[None, None, None, :, None], (nc, nx, nz, rows, 1))
    part = jnp.concatenate([part, extra], axis=4)
    part = lax.psum_scatter(part, "core", scatter_dimension=0, tiled=True)
    part = lax.psum_scatter(part, "x", scatter_dimension=1, tiled=True)
    part = lax.psum_scatter(part, "z", scatter_dimension=2, tiled=True)
    back = part.reshape(ep_count, CAP, width + 1)
    returned = lax.all_to_all(back, "ep", 0, 0, tiled=True).reshape(EXPERTS * CAP, width + 1)
    pair_rows = returned[target].reshape(tok_count, 2, width + 1)
    mixed = jnp.sum(route_gates[:, :, None] * pair_rows[:, :, :width], axis=1).astype(jnp.bfloat16)
    grad_gates = pair_rows[:, :, width]
    return (
        mixed,
        grad_gates,
        grad_gate_w.astype(jnp.bfloat16)[None],
        grad_up_w.astype(jnp.bfloat16)[None],
        grad_down.astype(jnp.bfloat16)[None],
    )


def solution(mesh):
    ep = mesh.shape["ep"]
    etp = mesh.shape["etp"]
    nz, nx, nc = sub_sizes(etp)
    devs = np.asarray(mesh.devices).reshape(ep, nz, nx, nc)
    mesh2 = Mesh(devs, ("ep",) + SUB)
    in_specs = (
        P("ep", SUB),
        P("ep", None),
        P("ep", None),
        P("ep", SUB),
        P("ep", None, SUB),
        P("ep", None, SUB),
        P("ep", SUB, None),
    )
    out_specs = (
        P("ep", SUB),
        P("ep", None),
        P("ep", None, SUB),
        P("ep", None, SUB),
        P("ep", SUB, None),
    )
    return jax.shard_map(
        per_device, mesh=mesh2, in_specs=in_specs, out_specs=out_specs, check_vma=False
    )
```

```python
import functools

import jax
import jax.numpy as jnp
import numpy as np
from jax import lax
from jax.experimental import pallas as pl
from jax.experimental.pallas import tpu as pltpu
from jax.sharding import Mesh
from jax.sharding import PartitionSpec as P

EXPERTS = 8
CAP = 24
SUB = ("z", "x", "core")


def sub_sizes(etp):
    if etp % 8 == 0:
        return (etp // 8, 4, 2)
    return (etp, 1, 1)


def _gather_kernel(nz, nx, nc, chunk_ref, out_ref, sem_local, send_a, recv_a, send_b, recv_b, send_c, recv_c):
    e = lax.axis_index("ep")
    z = lax.axis_index("z")
    x = lax.axis_index("x")
    c = lax.axis_index("core")
    mesh_id = pl.DeviceIdType.MESH
    barrier = pltpu.get_barrier_semaphore()
    for d in range(1, nz):
        pl.semaphore_signal(barrier, inc=1, device_id=(e, (z + d) % nz, x, c), device_id_type=mesh_id)
    for d in range(1, nx):
        pl.semaphore_signal(barrier, inc=1, device_id=(e, z, (x + d) % nx, c), device_id_type=mesh_id)
    for d in range(1, nc):
        pl.semaphore_signal(barrier, inc=1, device_id=(e, z, x, (c + d) % nc), device_id_type=mesh_id)
    pl.semaphore_wait(barrier, (nz - 1) + (nx - 1) + (nc - 1))

    local = pltpu.make_async_copy(chunk_ref, out_ref.at[c, x, z], sem_local.at[0])
    local.start()
    sends = []
    for d in range(1, nz):
        cp = pltpu.make_async_remote_copy(
            chunk_ref, out_ref.at[c, x, z], send_a.at[d - 1], recv_a.at[d - 1],
            device_id=(e, (z + d) % nz, x, c), device_id_type=mesh_id)
        cp.start()
        sends.append(cp)
    for d in range(1, nz):
        pltpu.make_async_remote_copy(
            chunk_ref, out_ref.at[c, x, (z + nz - d) % nz], send_a.at[d - 1], recv_a.at[d - 1],
            device_id=(e, (z + nz - d) % nz, x, c), device_id_type=mesh_id).wait_recv()
    local.wait()
    for d in range(1, nx):
        cp = pltpu.make_async_remote_copy(
            out_ref.at[c, x], out_ref.at[c, x], send_b.at[d - 1], recv_b.at[d - 1],
            device_id=(e, z, (x + d) % nx, c), device_id_type=mesh_id)
        cp.start()
        sends.append(cp)
    for d in range(1, nx):
        pltpu.make_async_remote_copy(
            out_ref.at[c, (x + nx - d) % nx], out_ref.at[c, (x + nx - d) % nx], send_b.at[d - 1], recv_b.at[d - 1],
            device_id=(e, z, (x + nx - d) % nx, c), device_id_type=mesh_id).wait_recv()
    for d in range(1, nc):
        cp = pltpu.make_async_remote_copy(
            out_ref.at[c], out_ref.at[c], send_c.at[d - 1], recv_c.at[d - 1],
            device_id=(e, z, x, (c + d) % nc), device_id_type=mesh_id)
        cp.start()
        sends.append(cp)
    for d in range(1, nc):
        pltpu.make_async_remote_copy(
            out_ref.at[(c + nc - d) % nc], out_ref.at[(c + nc - d) % nc], send_c.at[d - 1], recv_c.at[d - 1],
            device_id=(e, z, x, (c + nc - d) % nc), device_id_type=mesh_id).wait_recv()
    for cp in sends:
        cp.wait_send()


def etp_gather(chunk, nz, nx, nc):
    rows, cols = chunk.shape
    vmem = pltpu.VMEM
    return pl.pallas_call(
        functools.partial(_gather_kernel, nz, nx, nc),
        out_shape=jax.ShapeDtypeStruct((nc, nx, nz, rows, cols), chunk.dtype),
        in_specs=[pl.BlockSpec(memory_space=vmem)],
        out_specs=pl.BlockSpec(memory_space=vmem),
        scratch_shapes=[
            pltpu.SemaphoreType.DMA((1,)),
            pltpu.SemaphoreType.DMA((max(nz - 1, 1),)),
            pltpu.SemaphoreType.DMA((max(nz - 1, 1),)),
            pltpu.SemaphoreType.DMA((max(nx - 1, 1),)),
            pltpu.SemaphoreType.DMA((max(nx - 1, 1),)),
            pltpu.SemaphoreType.DMA((max(nc - 1, 1),)),
            pltpu.SemaphoreType.DMA((max(nc - 1, 1),)),
        ],
        compiler_params=pltpu.CompilerParams(collective_id=0, has_side_effects=True),
    )(chunk)


def per_device(tokens, routes, route_gates, cotangent, w_gate, w_up, w_down):
    ep_count = lax.axis_size("ep")
    nz, nx, nc = lax.axis_size("z"), lax.axis_size("x"), lax.axis_size("core")
    tok_count, width = tokens.shape
    flat_ids = routes.reshape(-1)
    pair_count = flat_ids.shape[0]
    onehot = (flat_ids[:, None] == jnp.arange(EXPERTS, dtype=jnp.int32)[None, :]).astype(jnp.int32)
    before = jnp.cumsum(onehot, axis=0) - onehot
    slot_id = jnp.sum(before * onehot, axis=1)
    target = flat_ids * CAP + slot_id
    slot_table = (
        jnp.full((EXPERTS * CAP,), pair_count, jnp.int32)
        .at[target]
        .set(jnp.arange(pair_count, dtype=jnp.int32))
    )
    token_of_slot = slot_table // 2
    gate_flat = jnp.concatenate([route_gates.reshape(-1), jnp.zeros((1,), jnp.float32)])
    slot_gate = gate_flat[slot_table]
    xc = jnp.concatenate([tokens, cotangent], axis=1)
    xc_pad = jnp.concatenate([xc, jnp.zeros((1, 2 * width), jnp.bfloat16)], axis=0)
    sent = xc_pad[token_of_slot].reshape(ep_count, CAP, 2 * width)
    recv = lax.all_to_all(sent, "ep", 0, 0, tiled=True)
    gates_recv = lax.all_to_all(slot_gate.reshape(ep_count, CAP), "ep", 0, 0, tiled=True)
    rows = ep_count * CAP
    lanes = 128
    chunk = recv.reshape(rows * 2 * width // lanes, lanes)
    g = etp_gather(chunk, nz, nx, nc).reshape(nc, nx, nz, rows, 2 * width)
    g = jnp.transpose(g, (3, 2, 1, 0, 4))
    rows_x = g[..., :width].reshape(rows, -1)
    cot_rows = g[..., width:].reshape(rows, -1)
    slot_g = gates_recv.reshape(rows, 1)
    rows_dy = (slot_g * cot_rows.astype(jnp.float32)).astype(jnp.bfloat16)
    wg, wu, wd = w_gate[0], w_up[0], w_down[0]
    gate_pre = jnp.dot(rows_x, wg, preferred_element_type=jnp.float32)
    up_pre = jnp.dot(rows_x, wu, preferred_element_type=jnp.float32)
    sigma = jax.nn.sigmoid(gate_pre)
    hidden = (jax.nn.silu(gate_pre) * up_pre).astype(jnp.bfloat16)
    output_part = jnp.dot(hidden, wd, preferred_element_type=jnp.float32)
    d_hidden = lax.dot_general(rows_dy, wd, (((1,), (1,)), ((), ())), preferred_element_type=jnp.float32)
    d_up = (d_hidden * jax.nn.silu(gate_pre)).astype(jnp.bfloat16)
    d_gate = (d_hidden * up_pre * sigma * (1.0 + gate_pre * (1.0 - sigma))).astype(jnp.bfloat16)
    grad_down = lax.dot_general(hidden, rows_dy, (((0,), (0,)), ((), ())), preferred_element_type=jnp.float32)
    grad_gate_w = lax.dot_general(rows_x, d_gate, (((0,), (0,)), ((), ())), preferred_element_type=jnp.float32)
    grad_up_w = lax.dot_general(rows_x, d_up, (((0,), (0,)), ((), ())), preferred_element_type=jnp.float32)
    inner = jnp.sum(output_part * cot_rows.astype(jnp.float32), axis=1)
    part = output_part.reshape(rows, nz, nx, nc, width)
    part = jnp.transpose(part, (3, 2, 1, 0, 4))
    extra = jnp.broadcast_to(inner[None, None, None, :, None], (nc, nx, nz, rows, 1))
    part = jnp.concatenate([part, extra], axis=4)
    part = lax.psum_scatter(part, "core", scatter_dimension=0, tiled=True)
    part = lax.psum_scatter(part, "x", scatter_dimension=1, tiled=True)
    part = lax.psum_scatter(part, "z", scatter_dimension=2, tiled=True)
    back = part.reshape(ep_count, CAP, width + 1)
    returned = lax.all_to_all(back, "ep", 0, 0, tiled=True).reshape(EXPERTS * CAP, width + 1)
    pair_rows = returned[target].reshape(tok_count, 2, width + 1)
    mixed = jnp.sum(route_gates[:, :, None] * pair_rows[:, :, :width], axis=1).astype(jnp.bfloat16)
    grad_gates = pair_rows[:, :, width]
    return (
        mixed,
        grad_gates,
        grad_gate_w.astype(jnp.bfloat16)[None],
        grad_up_w.astype(jnp.bfloat16)[None],
        grad_down.astype(jnp.bfloat16)[None],
    )


def solution(mesh):
    ep = mesh.shape["ep"]
    etp = mesh.shape["etp"]
    nz, nx, nc = sub_sizes(etp)
    devs = np.asarray(mesh.devices).reshape(ep, nz, nx, nc)
    mesh2 = Mesh(devs, ("ep",) + SUB)
    in_specs = (
        P("ep", SUB),
        P("ep", None),
        P("ep", None),
        P("ep", SUB),
        P("ep", None, SUB),
        P("ep", None, SUB),
        P("ep", SUB, None),
    )
    out_specs = (
        P("ep", SUB),
        P("ep", None),
        P("ep", None, SUB),
        P("ep", None, SUB),
        P("ep", SUB, None),
    )
    return jax.shard_map(
        per_device, mesh=mesh2, in_specs=in_specs, out_specs=out_specs, check_vma=False
    )
```

```python
import functools

import jax
import jax.numpy as jnp
import numpy as np
from jax import lax
from jax.experimental import pallas as pl
from jax.experimental.pallas import tpu as pltpu
from jax.sharding import Mesh
from jax.sharding import PartitionSpec as P

EXPERTS = 8
CAP = 24
SUB = ("z", "x", "core")


def sub_sizes(etp):
    if etp % 8 == 0:
        return (etp // 8, 4, 2)
    return (etp, 1, 1)


def _gather_kernel(nz, nx, nc, chunk_ref, out_ref, sem_local, send_a, recv_a, send_b, recv_b, send_c, recv_c):
    e = lax.axis_index("ep")
    z = lax.axis_index("z")
    x = lax.axis_index("x")
    c = lax.axis_index("core")
    mesh_id = pl.DeviceIdType.MESH
    barrier = pltpu.get_barrier_semaphore()
    for d in range(1, nz):
        pl.semaphore_signal(barrier, inc=1, device_id=(e, (z + d) % nz, x, c), device_id_type=mesh_id)
    for d in range(1, nx):
        pl.semaphore_signal(barrier, inc=1, device_id=(e, z, (x + d) % nx, c), device_id_type=mesh_id)
    for d in range(1, nc):
        pl.semaphore_signal(barrier, inc=1, device_id=(e, z, x, (c + d) % nc), device_id_type=mesh_id)
    pl.semaphore_wait(barrier, (nz - 1) + (nx - 1) + (nc - 1))

    local = pltpu.make_async_copy(chunk_ref, out_ref.at[c, x, z], sem_local.at[0])
    local.start()
    sends = []
    for d in range(1, nz):
        cp = pltpu.make_async_remote_copy(
            chunk_ref, out_ref.at[c, x, z], send_a.at[d - 1], recv_a.at[d - 1],
            device_id=(e, (z + d) % nz, x, c), device_id_type=mesh_id)
        cp.start()
        sends.append(cp)
    for d in range(1, nz):
        pltpu.make_async_remote_copy(
            chunk_ref, out_ref.at[c, x, (z + nz - d) % nz], send_a.at[d - 1], recv_a.at[d - 1],
            device_id=(e, (z + nz - d) % nz, x, c), device_id_type=mesh_id).wait_recv()
    local.wait()
    for d in range(1, nx):
        cp = pltpu.make_async_remote_copy(
            out_ref.at[c, x], out_ref.at[c, x], send_b.at[d - 1], recv_b.at[d - 1],
            device_id=(e, z, (x + d) % nx, c), device_id_type=mesh_id)
        cp.start()
        sends.append(cp)
    for d in range(1, nx):
        pltpu.make_async_remote_copy(
            out_ref.at[c, (x + nx - d) % nx], out_ref.at[c, (x + nx - d) % nx], send_b.at[d - 1], recv_b.at[d - 1],
            device_id=(e, z, (x + nx - d) % nx, c), device_id_type=mesh_id).wait_recv()
    for d in range(1, nc):
        cp = pltpu.make_async_remote_copy(
            out_ref.at[c], out_ref.at[c], send_c.at[d - 1], recv_c.at[d - 1],
            device_id=(e, z, x, (c + d) % nc), device_id_type=mesh_id)
        cp.start()
        sends.append(cp)
    for d in range(1, nc):
        pltpu.make_async_remote_copy(
            out_ref.at[(c + nc - d) % nc], out_ref.at[(c + nc - d) % nc], send_c.at[d - 1], recv_c.at[d - 1],
            device_id=(e, z, x, (c + nc - d) % nc), device_id_type=mesh_id).wait_recv()
    for cp in sends:
        cp.wait_send()


def etp_gather(chunk, nz, nx, nc):
    rows, cols = chunk.shape
    vmem = pltpu.VMEM
    return pl.pallas_call(
        functools.partial(_gather_kernel, nz, nx, nc),
        out_shape=jax.ShapeDtypeStruct((nc, nx, nz, rows, cols), chunk.dtype),
        in_specs=[pl.BlockSpec(memory_space=vmem)],
        out_specs=pl.BlockSpec(memory_space=vmem),
        scratch_shapes=[
            pltpu.SemaphoreType.DMA((1,)),
            pltpu.SemaphoreType.DMA((max(nz - 1, 1),)),
            pltpu.SemaphoreType.DMA((max(nz - 1, 1),)),
            pltpu.SemaphoreType.DMA((max(nx - 1, 1),)),
            pltpu.SemaphoreType.DMA((max(nx - 1, 1),)),
            pltpu.SemaphoreType.DMA((max(nc - 1, 1),)),
            pltpu.SemaphoreType.DMA((max(nc - 1, 1),)),
        ],
        compiler_params=pltpu.CompilerParams(collective_id=0, has_side_effects=True),
    )(chunk)


def _rs_kernel(ne, nz, nx, nc, blk, part_ref, out_ref, recv_c, acc1, recv_b, acc2, recv_a, fin,
               sem_local, send_c, rsem_c, send_b, rsem_b, send_a, rsem_a, send_d, rsem_d):
    e = lax.axis_index("ep")
    z = lax.axis_index("z")
    x = lax.axis_index("x")
    c = lax.axis_index("core")
    mesh_id = pl.DeviceIdType.MESH
    barrier = pltpu.get_barrier_semaphore()
    for d in range(1, nz):
        pl.semaphore_signal(barrier, inc=1, device_id=(e, (z + d) % nz, x, c), device_id_type=mesh_id)
    for d in range(1, nx):
        pl.semaphore_signal(barrier, inc=1, device_id=(e, z, (x + d) % nx, c), device_id_type=mesh_id)
    for d in range(1, nc):
        pl.semaphore_signal(barrier, inc=1, device_id=(e, z, x, (c + d) % nc), device_id_type=mesh_id)
    for d in range(1, ne):
        pl.semaphore_signal(barrier, inc=1, device_id=((e + d) % ne, z, x, c), device_id_type=mesh_id)
    pl.semaphore_wait(barrier, (nz - 1) + (nx - 1) + (nc - 1) + (ne - 1))
    sends = []

    for d in range(1, nc):
        cp = pltpu.make_async_remote_copy(
            part_ref.at[(c + d) % nc], recv_c.at[d - 1], send_c.at[d - 1], rsem_c.at[d - 1],
            device_id=(e, z, x, (c + d) % nc), device_id_type=mesh_id)
        cp.start()
        sends.append(cp)
    for d in range(1, nc):
        pltpu.make_async_remote_copy(
            part_ref.at[c], recv_c.at[d - 1], send_c.at[d - 1], rsem_c.at[d - 1],
            device_id=(e, z, x, (c + nc - d) % nc), device_id_type=mesh_id).wait_recv()
    for i in range(nx):
        total = part_ref[c, i]
        for d in range(1, nc):
            total = total + recv_c[d - 1, i]
        acc1[i] = total

    for d in range(1, nx):
        cp = pltpu.make_async_remote_copy(
            acc1.at[(x + d) % nx], recv_b.at[d - 1], send_b.at[d - 1], rsem_b.at[d - 1],
            device_id=(e, z, (x + d) % nx, c), device_id_type=mesh_id)
        cp.start()
        sends.append(cp)
    for d in range(1, nx):
        pltpu.make_async_remote_copy(
            acc1.at[x], recv_b.at[d - 1], send_b.at[d - 1], rsem_b.at[d - 1],
            device_id=(e, z, (x + nx - d) % nx, c), device_id_type=mesh_id).wait_recv()
    total = acc1[x]
    for d in range(1, nx):
        total = total + recv_b[d - 1]
    acc2[...] = total

    for d in range(1, nz):
        cp = pltpu.make_async_remote_copy(
            acc2.at[(z + d) % nz], recv_a.at[d - 1], send_a.at[d - 1], rsem_a.at[d - 1],
            device_id=(e, (z + d) % nz, x, c), device_id_type=mesh_id)
        cp.start()
        sends.append(cp)
    for d in range(1, nz):
        pltpu.make_async_remote_copy(
            acc2.at[z], recv_a.at[d - 1], send_a.at[d - 1], rsem_a.at[d - 1],
            device_id=(e, (z + nz - d) % nz, x, c), device_id_type=mesh_id).wait_recv()
    total = acc2[z]
    for d in range(1, nz):
        total = total + recv_a[d - 1]

    pad_rows = fin.shape[1]
    for b in range(ne):
        fin[b, :blk] = total[b * blk:(b + 1) * blk]
        fin[b, blk:] = jnp.zeros((pad_rows - blk, total.shape[1]), total.dtype)
    local = pltpu.make_async_copy(fin.at[e], out_ref.at[e], sem_local.at[0])
    local.start()
    for d in range(1, ne):
        cp = pltpu.make_async_remote_copy(
            fin.at[(e + d) % ne], out_ref.at[e], send_d.at[d - 1], rsem_d.at[e],
            device_id=((e + d) % ne, z, x, c), device_id_type=mesh_id)
        cp.start()
        sends.append(cp)
    for d in range(1, ne):
        src = (e + ne - d) % ne
        pltpu.make_async_remote_copy(
            fin.at[e], out_ref.at[src], send_d.at[d - 1], rsem_d.at[src],
            device_id=(src, z, x, c), device_id_type=mesh_id).wait_recv()
    local.wait()
    for cp in sends:
        cp.wait_send()


def etp_reduce_scatter(part, ne, blk):
    nc, nx, nz, rows, lanes = part.shape
    pad_rows = -(-blk // 8) * 8
    f32 = jnp.float32
    vmem = pltpu.VMEM
    dma = pltpu.SemaphoreType.DMA
    return pl.pallas_call(
        functools.partial(_rs_kernel, ne, nz, nx, nc, blk),
        out_shape=jax.ShapeDtypeStruct((ne, pad_rows, lanes), f32),
        in_specs=[pl.BlockSpec(memory_space=vmem)],
        out_specs=pl.BlockSpec(memory_space=vmem),
        scratch_shapes=[
            pltpu.VMEM((max(nc - 1, 1), nx, nz, rows, lanes), f32),
            pltpu.VMEM((nx, nz, rows, lanes), f32),
            pltpu.VMEM((max(nx - 1, 1), nz, rows, lanes), f32),
            pltpu.VMEM((nz, rows, lanes), f32),
            pltpu.VMEM((max(nz - 1, 1), rows, lanes), f32),
            pltpu.VMEM((ne, pad_rows, lanes), f32),
            dma((1,)),
            dma((max(nc - 1, 1),)),
            dma((max(nc - 1, 1),)),
            dma((max(nx - 1, 1),)),
            dma((max(nx - 1, 1),)),
            dma((max(nz - 1, 1),)),
            dma((max(nz - 1, 1),)),
            dma((max(ne - 1, 1),)),
            dma((ne,)),
        ],
        compiler_params=pltpu.CompilerParams(collective_id=1, has_side_effects=True),
    )(part)


def per_device(tokens, routes, route_gates, cotangent, w_gate, w_up, w_down):
    ep_count = lax.axis_size("ep")
    nz, nx, nc = lax.axis_size("z"), lax.axis_size("x"), lax.axis_size("core")
    tok_count, width = tokens.shape
    flat_ids = routes.reshape(-1)
    pair_count = flat_ids.shape[0]
    onehot = (flat_ids[:, None] == jnp.arange(EXPERTS, dtype=jnp.int32)[None, :]).astype(jnp.int32)
    before = jnp.cumsum(onehot, axis=0) - onehot
    slot_id = jnp.sum(before * onehot, axis=1)
    target = flat_ids * CAP + slot_id
    slot_table = (
        jnp.full((EXPERTS * CAP,), pair_count, jnp.int32)
        .at[target]
        .set(jnp.arange(pair_count, dtype=jnp.int32))
    )
    token_of_slot = slot_table // 2
    gate_flat = jnp.concatenate([route_gates.reshape(-1), jnp.zeros((1,), jnp.float32)])
    slot_gate = gate_flat[slot_table]
    xc = jnp.concatenate([tokens, cotangent], axis=1)
    xc_pad = jnp.concatenate([xc, jnp.zeros((1, 2 * width), jnp.bfloat16)], axis=0)
    sent = xc_pad[token_of_slot].reshape(ep_count, CAP, 2 * width)
    recv = lax.all_to_all(sent, "ep", 0, 0, tiled=True)
    gates_recv = lax.all_to_all(slot_gate.reshape(ep_count, CAP), "ep", 0, 0, tiled=True)
    rows = ep_count * CAP
    lanes = 128
    chunk = recv.reshape(rows * 2 * width // lanes, lanes)
    g = etp_gather(chunk, nz, nx, nc).reshape(nc, nx, nz, rows, 2 * width)
    g = jnp.transpose(g, (3, 2, 1, 0, 4))
    rows_x = g[..., :width].reshape(rows, -1)
    cot_rows = g[..., width:].reshape(rows, -1)
    slot_g = gates_recv.reshape(rows, 1)
    rows_dy = (slot_g * cot_rows.astype(jnp.float32)).astype(jnp.bfloat16)
    wg, wu, wd = w_gate[0], w_up[0], w_down[0]
    gate_pre = jnp.dot(rows_x, wg, preferred_element_type=jnp.float32)
    up_pre = jnp.dot(rows_x, wu, preferred_element_type=jnp.float32)
    sigma = jax.nn.sigmoid(gate_pre)
    hidden = (jax.nn.silu(gate_pre) * up_pre).astype(jnp.bfloat16)
    output_part = jnp.dot(hidden, wd, preferred_element_type=jnp.float32)
    d_hidden = lax.dot_general(rows_dy, wd, (((1,), (1,)), ((), ())), preferred_element_type=jnp.float32)
    d_up = (d_hidden * jax.nn.silu(gate_pre)).astype(jnp.bfloat16)
    d_gate = (d_hidden * up_pre * sigma * (1.0 + gate_pre * (1.0 - sigma))).astype(jnp.bfloat16)
    grad_down = lax.dot_general(hidden, rows_dy, (((0,), (0,)), ((), ())), preferred_element_type=jnp.float32)
    grad_gate_w = lax.dot_general(rows_x, d_gate, (((0,), (0,)), ((), ())), preferred_element_type=jnp.float32)
    grad_up_w = lax.dot_general(rows_x, d_up, (((0,), (0,)), ((), ())), preferred_element_type=jnp.float32)
    inner = jnp.sum(output_part * cot_rows.astype(jnp.float32), axis=1)
    lanes = 128
    blk_elems = CAP * (width + 1)
    blk = -(-blk_elems // lanes)
    part = output_part.reshape(ep_count, CAP, nz, nx, nc, width)
    part = jnp.transpose(part, (4, 3, 2, 0, 1, 5))
    extra = jnp.broadcast_to(inner.reshape(1, 1, 1, ep_count, CAP, 1), (nc, nx, nz, ep_count, CAP, 1))
    part = jnp.concatenate([part, extra], axis=5).reshape(nc, nx, nz, ep_count, blk_elems)
    part = jnp.pad(part, ((0, 0),) * 4 + ((0, blk * lanes - blk_elems),))
    part = part.reshape(nc, nx, nz, ep_count * blk, lanes)
    back = etp_reduce_scatter(part, ep_count, blk)
    returned = back[:, :blk].reshape(ep_count, blk * lanes)[:, :blk_elems].reshape(EXPERTS * CAP, width + 1)
    pair_rows = returned[target].reshape(tok_count, 2, width + 1)
    mixed = jnp.sum(route_gates[:, :, None] * pair_rows[:, :, :width], axis=1).astype(jnp.bfloat16)
    grad_gates = pair_rows[:, :, width]
    return (
        mixed,
        grad_gates,
        grad_gate_w.astype(jnp.bfloat16)[None],
        grad_up_w.astype(jnp.bfloat16)[None],
        grad_down.astype(jnp.bfloat16)[None],
    )


def solution(mesh):
    ep = mesh.shape["ep"]
    etp = mesh.shape["etp"]
    nz, nx, nc = sub_sizes(etp)
    devs = np.asarray(mesh.devices).reshape(ep, nz, nx, nc)
    mesh2 = Mesh(devs, ("ep",) + SUB)
    in_specs = (
        P("ep", SUB),
        P("ep", None),
        P("ep", None),
        P("ep", SUB),
        P("ep", None, SUB),
        P("ep", None, SUB),
        P("ep", SUB, None),
    )
    out_specs = (
        P("ep", SUB),
        P("ep", None),
        P("ep", None, SUB),
        P("ep", None, SUB),
        P("ep", SUB, None),
    )
    return jax.shard_map(
        per_device, mesh=mesh2, in_specs=in_specs, out_specs=out_specs, check_vma=False
    )
```

```python
import functools

import jax
import jax.numpy as jnp
import numpy as np
from jax import lax
from jax.experimental import pallas as pl
from jax.experimental.pallas import tpu as pltpu
from jax.sharding import Mesh
from jax.sharding import PartitionSpec as P

EXPERTS = 8
CAP = 24
SUB = ("z", "x", "core")
MESH_ID = pl.DeviceIdType.MESH


def sub_sizes(etp):
    if etp % 8 == 0:
        return (etp // 8, 4, 2)
    return (etp, 1, 1)


def _coords():
    return (lax.axis_index("ep"), lax.axis_index("z"), lax.axis_index("x"), lax.axis_index("core"))


def _barrier(ne, nz, nx, nc, with_ep):
    e, z, x, c = _coords()
    barrier = pltpu.get_barrier_semaphore()
    count = 0
    for d in range(1, nz):
        pl.semaphore_signal(barrier, inc=1, device_id=(e, (z + d) % nz, x, c), device_id_type=MESH_ID)
        count += 1
    for d in range(1, nx):
        pl.semaphore_signal(barrier, inc=1, device_id=(e, z, (x + d) % nx, c), device_id_type=MESH_ID)
        count += 1
    for d in range(1, nc):
        pl.semaphore_signal(barrier, inc=1, device_id=(e, z, x, (c + d) % nc), device_id_type=MESH_ID)
        count += 1
    if with_ep:
        for d in range(1, ne):
            pl.semaphore_signal(barrier, inc=1, device_id=((e + d) % ne, z, x, c), device_id_type=MESH_ID)
            count += 1
    pl.semaphore_wait(barrier, count)


def _gather_kernel(nz, nx, nc, xa_ref, ca_ref, xo_ref, co_ref, sem_local, send_a, recv_a, send_b, recv_b, send_c, recv_c):
    e, z, x, c = _coords()
    _barrier(1, nz, nx, nc, False)
    pairs = ((xa_ref, xo_ref), (ca_ref, co_ref))
    locals_ = []
    for t, (src, out) in enumerate(pairs):
        cp = pltpu.make_async_copy(src, out.at[z, x, c], sem_local.at[t])
        cp.start()
        locals_.append(cp)
    sends = []
    for t, (src, out) in enumerate(pairs):
        for d in range(1, nz):
            cp = pltpu.make_async_remote_copy(
                src, out.at[z, x, c], send_a.at[t, d - 1], recv_a.at[t, d - 1],
                device_id=(e, (z + d) % nz, x, c), device_id_type=MESH_ID)
            cp.start()
            sends.append(cp)
    for t, (src, out) in enumerate(pairs):
        for d in range(1, nz):
            zs = (z + nz - d) % nz
            pltpu.make_async_remote_copy(
                src, out.at[zs, x, c], send_a.at[t, d - 1], recv_a.at[t, d - 1],
                device_id=(e, zs, x, c), device_id_type=MESH_ID).wait_recv()
    for cp in locals_:
        cp.wait()
    for t, (src, out) in enumerate(pairs):
        for d in range(1, nx):
            cp = pltpu.make_async_remote_copy(
                out.at[:, x, c], out.at[:, x, c], send_b.at[t, d - 1], recv_b.at[t, d - 1],
                device_id=(e, z, (x + d) % nx, c), device_id_type=MESH_ID)
            cp.start()
            sends.append(cp)
    for t, (src, out) in enumerate(pairs):
        for d in range(1, nx):
            xs = (x + nx - d) % nx
            pltpu.make_async_remote_copy(
                out.at[:, xs, c], out.at[:, xs, c], send_b.at[t, d - 1], recv_b.at[t, d - 1],
                device_id=(e, z, xs, c), device_id_type=MESH_ID).wait_recv()
    for t, (src, out) in enumerate(pairs):
        for d in range(1, nc):
            cp = pltpu.make_async_remote_copy(
                out.at[:, :, c], out.at[:, :, c], send_c.at[t, d - 1], recv_c.at[t, d - 1],
                device_id=(e, z, x, (c + d) % nc), device_id_type=MESH_ID)
            cp.start()
            sends.append(cp)
    for t, (src, out) in enumerate(pairs):
        for d in range(1, nc):
            cs = (c + nc - d) % nc
            pltpu.make_async_remote_copy(
                out.at[:, :, cs], out.at[:, :, cs], send_c.at[t, d - 1], recv_c.at[t, d - 1],
                device_id=(e, z, x, cs), device_id_type=MESH_ID).wait_recv()
    for cp in sends:
        cp.wait_send()


def etp_gather(xa, ca, nz, nx, nc):
    rows, cols = xa.shape
    vmem = pltpu.VMEM
    dma = pltpu.SemaphoreType.DMA
    shape = jax.ShapeDtypeStruct((nz, nx, nc, rows, cols), xa.dtype)
    return pl.pallas_call(
        functools.partial(_gather_kernel, nz, nx, nc),
        out_shape=(shape, shape),
        in_specs=[pl.BlockSpec(memory_space=vmem)] * 2,
        out_specs=(pl.BlockSpec(memory_space=vmem),) * 2,
        scratch_shapes=[
            dma((2,)),
            dma((2, max(nz - 1, 1))),
            dma((2, max(nz - 1, 1))),
            dma((2, max(nx - 1, 1))),
            dma((2, max(nx - 1, 1))),
            dma((2, max(nc - 1, 1))),
            dma((2, max(nc - 1, 1))),
        ],
        compiler_params=pltpu.CompilerParams(collective_id=0, has_side_effects=True),
    )(xa, ca)


def _rs_kernel(ne, nz, nx, nc, part_ref, inner_ref, out_ref, recv_c, acc1, recv_b, acc2, recv_a,
               ir_c, in1, ir_b, in2, ir_a, fin,
               sem_local, send_c, rsem_c, send_b, rsem_b, send_a, rsem_a, send_d, rsem_d):
    e, z, x, c = _coords()
    _barrier(ne, nz, nx, nc, True)
    sends = []

    def exchange(pieces, peers_of, send_sem, recv_sem):
        n = len(peers_of)
        for t, (src_of, dst) in enumerate(pieces):
            for d in range(n):
                cp = pltpu.make_async_remote_copy(
                    src_of(d), dst.at[d], send_sem.at[t, d], recv_sem.at[t, d],
                    device_id=peers_of[d][0], device_id_type=MESH_ID)
                cp.start()
                sends.append(cp)
        for t, (src_of, dst) in enumerate(pieces):
            for d in range(n):
                pltpu.make_async_remote_copy(
                    dst.at[d], dst.at[d], send_sem.at[t, d], recv_sem.at[t, d],
                    device_id=peers_of[d][1], device_id_type=MESH_ID).wait_recv()

    peers = [((e, z, x, (c + d) % nc), (e, z, x, (c + nc - d) % nc)) for d in range(1, nc)]
    exchange([(lambda d: part_ref.at[:, :, (c + d + 1) % nc], recv_c), (lambda d: inner_ref, ir_c)],
             peers, send_c, rsem_c)

    def sum_c(i, carry):
        zi = i // nx
        xi = i % nx
        total = part_ref[zi, xi, c]
        for d in range(nc - 1):
            total = total + recv_c[d, zi, xi]
        acc1[zi, xi] = total
        return carry
    lax.fori_loop(0, nz * nx, sum_c, 0)
    total = inner_ref[...]
    for d in range(nc - 1):
        total = total + ir_c[d]
    in1[...] = total

    peers = [((e, z, (x + d) % nx, c), (e, z, (x + nx - d) % nx, c)) for d in range(1, nx)]
    exchange([(lambda d: acc1.at[:, (x + d + 1) % nx], recv_b), (lambda d: in1, ir_b)],
             peers, send_b, rsem_b)

    def sum_b(zi, carry):
        total = acc1[zi, x]
        for d in range(nx - 1):
            total = total + recv_b[d, zi]
        acc2[zi] = total
        return carry
    lax.fori_loop(0, nz, sum_b, 0)
    total = in1[...]
    for d in range(nx - 1):
        total = total + ir_b[d]
    in2[...] = total

    peers = [((e, (z + d) % nz, x, c), (e, (z + nz - d) % nz, x, c)) for d in range(1, nz)]
    exchange([(lambda d: acc2.at[(z + d + 1) % nz], recv_a), (lambda d: in2, ir_a)],
             peers, send_a, rsem_a)
    total = acc2[z]
    for d in range(nz - 1):
        total = total + recv_a[d]
    itotal = in2[...]
    for d in range(nz - 1):
        itotal = itotal + ir_a[d]

    feats = total.shape[0]
    blk = fin.shape[2]
    for b in range(ne):
        fin[b, :feats, :] = total[:, b * blk:(b + 1) * blk]
        fin[b, feats:feats + 1, :] = itotal[:, b * blk:(b + 1) * blk]
        fin[b, feats + 1:, :] = jnp.zeros((fin.shape[1] - feats - 1, blk), jnp.float32)
    local = pltpu.make_async_copy(fin.at[e], out_ref.at[e], sem_local.at[0])
    local.start()
    for d in range(1, ne):
        cp = pltpu.make_async_remote_copy(
            fin.at[(e + d) % ne], out_ref.at[e], send_d.at[d - 1], rsem_d.at[e],
            device_id=((e + d) % ne, z, x, c), device_id_type=MESH_ID)
        cp.start()
        sends.append(cp)
    for d in range(1, ne):
        src = (e + ne - d) % ne
        pltpu.make_async_remote_copy(
            fin.at[e], out_ref.at[src], send_d.at[d - 1], rsem_d.at[src],
            device_id=(src, z, x, c), device_id_type=MESH_ID).wait_recv()
    local.wait()
    for cp in sends:
        cp.wait_send()


def etp_reduce_scatter(part, inner, ne, blk):
    nz, nx, nc, feats, cols = part.shape
    pad_rows = -(-(feats + 1) // 8) * 8
    f32 = jnp.float32
    vmem = pltpu.VMEM
    dma = pltpu.SemaphoreType.DMA
    mc, mx, mz = max(nc - 1, 1), max(nx - 1, 1), max(nz - 1, 1)
    return pl.pallas_call(
        functools.partial(_rs_kernel, ne, nz, nx, nc),
        out_shape=jax.ShapeDtypeStruct((ne, pad_rows, blk), f32),
        in_specs=[pl.BlockSpec(memory_space=vmem)] * 2,
        out_specs=pl.BlockSpec(memory_space=vmem),
        scratch_shapes=[
            pltpu.VMEM((mc, nz, nx, feats, cols), f32),
            pltpu.VMEM((nz, nx, feats, cols), f32),
            pltpu.VMEM((mx, nz, feats, cols), f32),
            pltpu.VMEM((nz, feats, cols), f32),
            pltpu.VMEM((mz, feats, cols), f32),
            pltpu.VMEM((mc, 1, cols), f32),
            pltpu.VMEM((1, cols), f32),
            pltpu.VMEM((mx, 1, cols), f32),
            pltpu.VMEM((1, cols), f32),
            pltpu.VMEM((mz, 1, cols), f32),
            pltpu.VMEM((ne, pad_rows, blk), f32),
            dma((1,)),
            dma((2, mc)),
            dma((2, mc)),
            dma((2, mx)),
            dma((2, mx)),
            dma((2, mz)),
            dma((2, mz)),
            dma((max(ne - 1, 1),)),
            dma((ne,)),
        ],
        compiler_params=pltpu.CompilerParams(collective_id=1, has_side_effects=True),
    )(part, inner)


def per_device(tokens, routes, route_gates, cotangent, w_gate, w_up, w_down):
    ep_count = lax.axis_size("ep")
    nz, nx, nc = lax.axis_size("z"), lax.axis_size("x"), lax.axis_size("core")
    tok_count, width = tokens.shape
    flat_ids = routes.reshape(-1)
    pair_count = flat_ids.shape[0]
    onehot = (flat_ids[:, None] == jnp.arange(EXPERTS, dtype=jnp.int32)[None, :]).astype(jnp.int32)
    before = jnp.cumsum(onehot, axis=0) - onehot
    slot_id = jnp.sum(before * onehot, axis=1)
    target = flat_ids * CAP + slot_id
    slot_table = (
        jnp.full((EXPERTS * CAP,), pair_count, jnp.int32)
        .at[target]
        .set(jnp.arange(pair_count, dtype=jnp.int32))
    )
    token_of_slot = slot_table // 2
    gate_flat = jnp.concatenate([route_gates.reshape(-1), jnp.zeros((1,), jnp.float32)])
    slot_gate = gate_flat[slot_table]
    xc = jnp.concatenate([tokens, cotangent], axis=1)
    xc_pad = jnp.concatenate([xc, jnp.zeros((1, 2 * width), jnp.bfloat16)], axis=0)
    sent = xc_pad[token_of_slot].reshape(ep_count, CAP, 2 * width)
    recv = lax.all_to_all(sent, "ep", 0, 0, tiled=True)
    gates_recv = lax.all_to_all(slot_gate.reshape(ep_count, CAP), "ep", 0, 0, tiled=True)
    rows = ep_count * CAP
    recv_t = jnp.transpose(recv, (2, 0, 1)).reshape(2 * width, rows)
    xt_all, ct_all = etp_gather(recv_t[:width], recv_t[width:], nz, nx, nc)
    feat = nz * nx * nc * width
    xt = xt_all.reshape(feat, rows)
    ct = ct_all.reshape(feat, rows)
    slot_g = gates_recv.reshape(1, rows)
    dyt = (slot_g * ct.astype(jnp.float32)).astype(jnp.bfloat16)
    wg, wu, wd = w_gate[0], w_up[0], w_down[0]
    f32 = jnp.float32

    def dims(a, b):
        return (((a,), (b,)), ((), ()))
    gate_pre = lax.dot_general(xt, wg, dims(0, 0), preferred_element_type=f32)
    up_pre = lax.dot_general(xt, wu, dims(0, 0), preferred_element_type=f32)
    sigma = jax.nn.sigmoid(gate_pre)
    hidden = (jax.nn.silu(gate_pre) * up_pre).astype(jnp.bfloat16)
    out_t = lax.dot_general(wd, hidden, dims(0, 1), preferred_element_type=f32)
    d_hidden = lax.dot_general(dyt, wd, dims(0, 1), preferred_element_type=f32)
    d_up = (d_hidden * jax.nn.silu(gate_pre)).astype(jnp.bfloat16)
    d_gate = (d_hidden * up_pre * sigma * (1.0 + gate_pre * (1.0 - sigma))).astype(jnp.bfloat16)
    grad_down = lax.dot_general(hidden, dyt, dims(0, 1), preferred_element_type=f32)
    grad_gate_w = lax.dot_general(xt, d_gate, dims(1, 0), preferred_element_type=f32)
    grad_up_w = lax.dot_general(xt, d_up, dims(1, 0), preferred_element_type=f32)
    inner = jnp.sum(out_t * ct.astype(f32), axis=0, keepdims=True)
    back = etp_reduce_scatter(out_t.reshape(nz, nx, nc, width, rows), inner, ep_count, CAP)
    returned = jnp.transpose(back, (0, 2, 1)).reshape(EXPERTS * CAP, -1)
    pair_rows = returned[target].reshape(tok_count, 2, -1)
    mixed = jnp.sum(route_gates[:, :, None] * pair_rows[:, :, :width], axis=1).astype(jnp.bfloat16)
    grad_gates = pair_rows[:, :, width]
    return (
        mixed,
        grad_gates,
        grad_gate_w.astype(jnp.bfloat16)[None],
        grad_up_w.astype(jnp.bfloat16)[None],
        grad_down.astype(jnp.bfloat16)[None],
    )


def solution(mesh):
    ep = mesh.shape["ep"]
    etp = mesh.shape["etp"]
    nz, nx, nc = sub_sizes(etp)
    devs = np.asarray(mesh.devices).reshape(ep, nz, nx, nc)
    mesh2 = Mesh(devs, ("ep",) + SUB)
    in_specs = (
        P("ep", SUB),
        P("ep", None),
        P("ep", None),
        P("ep", SUB),
        P("ep", None, SUB),
        P("ep", None, SUB),
        P("ep", SUB, None),
    )
    out_specs = (
        P("ep", SUB),
        P("ep", None),
        P("ep", None, SUB),
        P("ep", None, SUB),
        P("ep", SUB, None),
    )
    return jax.shard_map(
        per_device, mesh=mesh2, in_specs=in_specs, out_specs=out_specs, check_vma=False
    )
```

```python
import functools

import jax
import jax.numpy as jnp
import numpy as np
from jax import lax
from jax.experimental import pallas as pl
from jax.experimental.pallas import tpu as pltpu
from jax.sharding import Mesh
from jax.sharding import PartitionSpec as P

EXPERTS = 8
CAP = 24
SUB = ("z", "x", "core")
MESH_ID = pl.DeviceIdType.MESH


def sub_sizes(etp):
    if etp % 8 == 0:
        return (etp // 8, 4, 2)
    return (etp, 1, 1)


def _coords():
    return (lax.axis_index("ep"), lax.axis_index("z"), lax.axis_index("x"), lax.axis_index("core"))


def _barrier(ne, nz, nx, nc, with_ep):
    e, z, x, c = _coords()
    barrier = pltpu.get_barrier_semaphore()
    count = 0
    for d in range(1, nz):
        pl.semaphore_signal(barrier, inc=1, device_id=(e, (z + d) % nz, x, c), device_id_type=MESH_ID)
        count += 1
    for d in range(1, nx):
        pl.semaphore_signal(barrier, inc=1, device_id=(e, z, (x + d) % nx, c), device_id_type=MESH_ID)
        count += 1
    for d in range(1, nc):
        pl.semaphore_signal(barrier, inc=1, device_id=(e, z, x, (c + d) % nc), device_id_type=MESH_ID)
        count += 1
    if with_ep:
        for d in range(1, ne):
            pl.semaphore_signal(barrier, inc=1, device_id=((e + d) % ne, z, x, c), device_id_type=MESH_ID)
            count += 1
    pl.semaphore_wait(barrier, count)


def _gather_kernel(ne, nz, nx, nc, sent_ref, g_ref, xo_ref, co_ref, go_ref, rbuf, rg, xa, ca,
                   sem_local, send_0, rsem_0, send_a, recv_a, send_b, recv_b, send_c, recv_c):
    e, z, x, c = _coords()
    _barrier(ne, nz, nx, nc, True)
    sends = []
    own = [pltpu.make_async_copy(sent_ref.at[e], rbuf.at[e], sem_local.at[0]),
           pltpu.make_async_copy(g_ref.at[e], rg.at[e], sem_local.at[1])]
    for cp in own:
        cp.start()
    for t, (src, dst) in enumerate(((sent_ref, rbuf), (g_ref, rg))):
        for d in range(1, ne):
            cp = pltpu.make_async_remote_copy(
                src.at[(e + d) % ne], dst.at[e], send_0.at[t, d - 1], rsem_0.at[t, e],
                device_id=((e + d) % ne, z, x, c), device_id_type=MESH_ID)
            cp.start()
            sends.append(cp)
    for t, (src, dst) in enumerate(((sent_ref, rbuf), (g_ref, rg))):
        for d in range(1, ne):
            srce = (e + ne - d) % ne
            pltpu.make_async_remote_copy(
                src.at[e], dst.at[srce], send_0.at[t, d - 1], rsem_0.at[t, srce],
                device_id=(srce, z, x, c), device_id_type=MESH_ID).wait_recv()
    for cp in own:
        cp.wait()
    feats = xa.shape[0]
    blk = rbuf.shape[2]
    for b in range(ne):
        piece = rbuf[b]
        xa[:, b * blk:(b + 1) * blk] = piece[:feats]
        ca[:, b * blk:(b + 1) * blk] = piece[feats:]
        go_ref[:, b * blk:(b + 1) * blk] = rg[b]

    pairs = ((xa, xo_ref), (ca, co_ref))
    locals_ = []
    for t, (src, out) in enumerate(pairs):
        cp = pltpu.make_async_copy(src, out.at[z, x, c], sem_local.at[2 + t])
        cp.start()
        locals_.append(cp)
    for t, (src, out) in enumerate(pairs):
        for d in range(1, nz):
            cp = pltpu.make_async_remote_copy(
                src, out.at[z, x, c], send_a.at[t, d - 1], recv_a.at[t, d - 1],
                device_id=(e, (z + d) % nz, x, c), device_id_type=MESH_ID)
            cp.start()
            sends.append(cp)
    for t, (src, out) in enumerate(pairs):
        for d in range(1, nz):
            zs = (z + nz - d) % nz
            pltpu.make_async_remote_copy(
                src, out.at[zs, x, c], send_a.at[t, d - 1], recv_a.at[t, d - 1],
                device_id=(e, zs, x, c), device_id_type=MESH_ID).wait_recv()
    for cp in locals_:
        cp.wait()
    for t, (src, out) in enumerate(pairs):
        for d in range(1, nx):
            cp = pltpu.make_async_remote_copy(
                out.at[:, x, c], out.at[:, x, c], send_b.at[t, d - 1], recv_b.at[t, d - 1],
                device_id=(e, z, (x + d) % nx, c), device_id_type=MESH_ID)
            cp.start()
            sends.append(cp)
    for t, (src, out) in enumerate(pairs):
        for d in range(1, nx):
            xs = (x + nx - d) % nx
            pltpu.make_async_remote_copy(
                out.at[:, xs, c], out.at[:, xs, c], send_b.at[t, d - 1], recv_b.at[t, d - 1],
                device_id=(e, z, xs, c), device_id_type=MESH_ID).wait_recv()
    for t, (src, out) in enumerate(pairs):
        for d in range(1, nc):
            cp = pltpu.make_async_remote_copy(
                out.at[:, :, c], out.at[:, :, c], send_c.at[t, d - 1], recv_c.at[t, d - 1],
                device_id=(e, z, x, (c + d) % nc), device_id_type=MESH_ID)
            cp.start()
            sends.append(cp)
    for t, (src, out) in enumerate(pairs):
        for d in range(1, nc):
            cs = (c + nc - d) % nc
            pltpu.make_async_remote_copy(
                out.at[:, :, cs], out.at[:, :, cs], send_c.at[t, d - 1], recv_c.at[t, d - 1],
                device_id=(e, z, x, cs), device_id_type=MESH_ID).wait_recv()
    for cp in sends:
        cp.wait_send()


def ep_etp_gather(sent, gsend, nz, nx, nc):
    ne, two_feats, blk = sent.shape
    feats = two_feats // 2
    cols = ne * blk
    vmem = pltpu.VMEM
    dma = pltpu.SemaphoreType.DMA
    shape = jax.ShapeDtypeStruct((nz, nx, nc, feats, cols), sent.dtype)
    return pl.pallas_call(
        functools.partial(_gather_kernel, ne, nz, nx, nc),
        out_shape=(shape, shape, jax.ShapeDtypeStruct((1, cols), gsend.dtype)),
        in_specs=[pl.BlockSpec(memory_space=vmem)] * 2,
        out_specs=(pl.BlockSpec(memory_space=vmem),) * 3,
        scratch_shapes=[
            pltpu.VMEM((ne, two_feats, blk), sent.dtype),
            pltpu.VMEM((ne, 1, blk), gsend.dtype),
            pltpu.VMEM((feats, cols), sent.dtype),
            pltpu.VMEM((feats, cols), sent.dtype),
            dma((4,)),
            dma((2, max(ne - 1, 1))),
            dma((2, ne)),
            dma((2, max(nz - 1, 1))),
            dma((2, max(nz - 1, 1))),
            dma((2, max(nx - 1, 1))),
            dma((2, max(nx - 1, 1))),
            dma((2, max(nc - 1, 1))),
            dma((2, max(nc - 1, 1))),
        ],
        compiler_params=pltpu.CompilerParams(collective_id=0, has_side_effects=True),
    )(sent, gsend)


def _rs_kernel(ne, nz, nx, nc, part_ref, inner_ref, out_ref, recv_c, acc1, recv_b, acc2, recv_a,
               ir_c, in1, ir_b, in2, ir_a, fin,
               sem_local, send_c, rsem_c, send_b, rsem_b, send_a, rsem_a, send_d, rsem_d):
    e, z, x, c = _coords()
    _barrier(ne, nz, nx, nc, True)
    sends = []

    def exchange(pieces, peers_of, send_sem, recv_sem):
        n = len(peers_of)
        for t, (src_of, dst) in enumerate(pieces):
            for d in range(n):
                cp = pltpu.make_async_remote_copy(
                    src_of(d), dst.at[d], send_sem.at[t, d], recv_sem.at[t, d],
                    device_id=peers_of[d][0], device_id_type=MESH_ID)
                cp.start()
                sends.append(cp)
        for t, (src_of, dst) in enumerate(pieces):
            for d in range(n):
                pltpu.make_async_remote_copy(
                    dst.at[d], dst.at[d], send_sem.at[t, d], recv_sem.at[t, d],
                    device_id=peers_of[d][1], device_id_type=MESH_ID).wait_recv()

    peers = [((e, z, x, (c + d) % nc), (e, z, x, (c + nc - d) % nc)) for d in range(1, nc)]
    exchange([(lambda d: part_ref.at[:, :, (c + d + 1) % nc], recv_c), (lambda d: inner_ref, ir_c)],
             peers, send_c, rsem_c)

    def sum_c(i, carry):
        zi = i // nx
        xi = i % nx
        total = part_ref[zi, xi, c]
        for d in range(nc - 1):
            total = total + recv_c[d, zi, xi]
        acc1[zi, xi] = total
        return carry
    lax.fori_loop(0, nz * nx, sum_c, 0)
    total = inner_ref[...]
    for d in range(nc - 1):
        total = total + ir_c[d]
    in1[...] = total

    peers = [((e, z, (x + d) % nx, c), (e, z, (x + nx - d) % nx, c)) for d in range(1, nx)]
    exchange([(lambda d: acc1.at[:, (x + d + 1) % nx], recv_b), (lambda d: in1, ir_b)],
             peers, send_b, rsem_b)

    def sum_b(zi, carry):
        total = acc1[zi, x]
        for d in range(nx - 1):
            total = total + recv_b[d, zi]
        acc2[zi] = total
        return carry
    lax.fori_loop(0, nz, sum_b, 0)
    total = in1[...]
    for d in range(nx - 1):
        total = total + ir_b[d]
    in2[...] = total

    peers = [((e, (z + d) % nz, x, c), (e, (z + nz - d) % nz, x, c)) for d in range(1, nz)]
    exchange([(lambda d: acc2.at[(z + d + 1) % nz], recv_a), (lambda d: in2, ir_a)],
             peers, send_a, rsem_a)
    total = acc2[z]
    for d in range(nz - 1):
        total = total + recv_a[d]
    itotal = in2[...]
    for d in range(nz - 1):
        itotal = itotal + ir_a[d]

    feats = total.shape[0]
    blk = fin.shape[2]
    for b in range(ne):
        fin[b, :feats, :] = total[:, b * blk:(b + 1) * blk]
        fin[b, feats:feats + 1, :] = itotal[:, b * blk:(b + 1) * blk]
        fin[b, feats + 1:, :] = jnp.zeros((fin.shape[1] - feats - 1, blk), jnp.float32)
    local = pltpu.make_async_copy(fin.at[e], out_ref.at[e], sem_local.at[0])
    local.start()
    for d in range(1, ne):
        cp = pltpu.make_async_remote_copy(
            fin.at[(e + d) % ne], out_ref.at[e], send_d.at[d - 1], rsem_d.at[e],
            device_id=((e + d) % ne, z, x, c), device_id_type=MESH_ID)
        cp.start()
        sends.append(cp)
    for d in range(1, ne):
        src = (e + ne - d) % ne
        pltpu.make_async_remote_copy(
            fin.at[e], out_ref.at[src], send_d.at[d - 1], rsem_d.at[src],
            device_id=(src, z, x, c), device_id_type=MESH_ID).wait_recv()
    local.wait()
    for cp in sends:
        cp.wait_send()


def etp_reduce_scatter(part, inner, ne, blk):
    nz, nx, nc, feats, cols = part.shape
    pad_rows = -(-(feats + 1) // 8) * 8
    f32 = jnp.float32
    vmem = pltpu.VMEM
    dma = pltpu.SemaphoreType.DMA
    mc, mx, mz = max(nc - 1, 1), max(nx - 1, 1), max(nz - 1, 1)
    return pl.pallas_call(
        functools.partial(_rs_kernel, ne, nz, nx, nc),
        out_shape=jax.ShapeDtypeStruct((ne, pad_rows, blk), f32),
        in_specs=[pl.BlockSpec(memory_space=vmem)] * 2,
        out_specs=pl.BlockSpec(memory_space=vmem),
        scratch_shapes=[
            pltpu.VMEM((mc, nz, nx, feats, cols), f32),
            pltpu.VMEM((nz, nx, feats, cols), f32),
            pltpu.VMEM((mx, nz, feats, cols), f32),
            pltpu.VMEM((nz, feats, cols), f32),
            pltpu.VMEM((mz, feats, cols), f32),
            pltpu.VMEM((mc, 1, cols), f32),
            pltpu.VMEM((1, cols), f32),
            pltpu.VMEM((mx, 1, cols), f32),
            pltpu.VMEM((1, cols), f32),
            pltpu.VMEM((mz, 1, cols), f32),
            pltpu.VMEM((ne, pad_rows, blk), f32),
            dma((1,)),
            dma((2, mc)),
            dma((2, mc)),
            dma((2, mx)),
            dma((2, mx)),
            dma((2, mz)),
            dma((2, mz)),
            dma((max(ne - 1, 1),)),
            dma((ne,)),
        ],
        compiler_params=pltpu.CompilerParams(collective_id=1, has_side_effects=True),
    )(part, inner)


def per_device(tokens, routes, route_gates, cotangent, w_gate, w_up, w_down):
    ep_count = lax.axis_size("ep")
    nz, nx, nc = lax.axis_size("z"), lax.axis_size("x"), lax.axis_size("core")
    tok_count, width = tokens.shape
    flat_ids = routes.reshape(-1)
    pair_count = flat_ids.shape[0]
    onehot = (flat_ids[:, None] == jnp.arange(EXPERTS, dtype=jnp.int32)[None, :]).astype(jnp.int32)
    before = jnp.cumsum(onehot, axis=0) - onehot
    slot_id = jnp.sum(before * onehot, axis=1)
    target = flat_ids * CAP + slot_id
    slot_table = (
        jnp.full((EXPERTS * CAP,), pair_count, jnp.int32)
        .at[target]
        .set(jnp.arange(pair_count, dtype=jnp.int32))
    )
    token_of_slot = slot_table // 2
    gate_flat = jnp.concatenate([route_gates.reshape(-1), jnp.zeros((1,), jnp.float32)])
    slot_gate = gate_flat[slot_table]
    xc = jnp.concatenate([tokens, cotangent], axis=1)
    xc_pad = jnp.concatenate([xc, jnp.zeros((1, 2 * width), jnp.bfloat16)], axis=0)
    sent = jnp.transpose(xc_pad[token_of_slot].reshape(ep_count, CAP, 2 * width), (0, 2, 1))
    gsend = slot_gate.reshape(ep_count, 1, CAP)
    rows = ep_count * CAP
    xt_all, ct_all, gates_recv = ep_etp_gather(sent, gsend, nz, nx, nc)
    feat = nz * nx * nc * width
    xt = xt_all.reshape(feat, rows)
    ct = ct_all.reshape(feat, rows)
    slot_g = gates_recv.reshape(1, rows)
    dyt = (slot_g * ct.astype(jnp.float32)).astype(jnp.bfloat16)
    wg, wu, wd = w_gate[0], w_up[0], w_down[0]
    f32 = jnp.float32

    def dims(a, b):
        return (((a,), (b,)), ((), ()))
    gate_pre = lax.dot_general(xt, wg, dims(0, 0), preferred_element_type=f32)
    up_pre = lax.dot_general(xt, wu, dims(0, 0), preferred_element_type=f32)
    sigma = jax.nn.sigmoid(gate_pre)
    hidden = (jax.nn.silu(gate_pre) * up_pre).astype(jnp.bfloat16)
    out_t = lax.dot_general(wd, hidden, dims(0, 1), preferred_element_type=f32)
    d_hidden = lax.dot_general(dyt, wd, dims(0, 1), preferred_element_type=f32)
    d_up = (d_hidden * jax.nn.silu(gate_pre)).astype(jnp.bfloat16)
    d_gate = (d_hidden * up_pre * sigma * (1.0 + gate_pre * (1.0 - sigma))).astype(jnp.bfloat16)
    grad_down = lax.dot_general(hidden, dyt, dims(0, 1), preferred_element_type=f32)
    grad_gate_w = lax.dot_general(xt, d_gate, dims(1, 0), preferred_element_type=f32)
    grad_up_w = lax.dot_general(xt, d_up, dims(1, 0), preferred_element_type=f32)
    inner = jnp.sum(out_t * ct.astype(f32), axis=0, keepdims=True)
    back = etp_reduce_scatter(out_t.reshape(nz, nx, nc, width, rows), inner, ep_count, CAP)
    returned = jnp.transpose(back, (0, 2, 1)).reshape(EXPERTS * CAP, -1)
    pair_rows = returned[target].reshape(tok_count, 2, -1)
    mixed = jnp.sum(route_gates[:, :, None] * pair_rows[:, :, :width], axis=1).astype(jnp.bfloat16)
    grad_gates = pair_rows[:, :, width]
    return (
        mixed,
        grad_gates,
        grad_gate_w.astype(jnp.bfloat16)[None],
        grad_up_w.astype(jnp.bfloat16)[None],
        grad_down.astype(jnp.bfloat16)[None],
    )


def solution(mesh):
    ep = mesh.shape["ep"]
    etp = mesh.shape["etp"]
    nz, nx, nc = sub_sizes(etp)
    devs = np.asarray(mesh.devices).reshape(ep, nz, nx, nc)
    mesh2 = Mesh(devs, ("ep",) + SUB)
    in_specs = (
        P("ep", SUB),
        P("ep", None),
        P("ep", None),
        P("ep", SUB),
        P("ep", None, SUB),
        P("ep", None, SUB),
        P("ep", SUB, None),
    )
    out_specs = (
        P("ep", SUB),
        P("ep", None),
        P("ep", None, SUB),
        P("ep", None, SUB),
        P("ep", SUB, None),
    )
    return jax.shard_map(
        per_device, mesh=mesh2, in_specs=in_specs, out_specs=out_specs, check_vma=False
    )
```

```python
import functools

import jax
import jax.numpy as jnp
import numpy as np
from jax import lax
from jax.experimental import pallas as pl
from jax.experimental.pallas import tpu as pltpu
from jax.sharding import Mesh
from jax.sharding import PartitionSpec as P

EXPERTS = 8
CAP = 24
SUB = ("z", "x", "core")
MESH_ID = pl.DeviceIdType.MESH


def sub_sizes(etp):
    if etp % 8 == 0:
        return (etp // 8, 4, 2)
    return (etp, 1, 1)


def _coords():
    return (lax.axis_index("ep"), lax.axis_index("z"), lax.axis_index("x"), lax.axis_index("core"))


def _barrier(ne, nz, nx, nc, with_ep):
    e, z, x, c = _coords()
    barrier = pltpu.get_barrier_semaphore()
    count = 0
    for d in range(1, nz):
        pl.semaphore_signal(barrier, inc=1, device_id=(e, (z + d) % nz, x, c), device_id_type=MESH_ID)
        count += 1
    for d in range(1, nx):
        pl.semaphore_signal(barrier, inc=1, device_id=(e, z, (x + d) % nx, c), device_id_type=MESH_ID)
        count += 1
    for d in range(1, nc):
        pl.semaphore_signal(barrier, inc=1, device_id=(e, z, x, (c + d) % nc), device_id_type=MESH_ID)
        count += 1
    if with_ep:
        for d in range(1, ne):
            pl.semaphore_signal(barrier, inc=1, device_id=((e + d) % ne, z, x, c), device_id_type=MESH_ID)
            count += 1
    pl.semaphore_wait(barrier, count)


def _gather_kernel(ne, nz, nx, nc, sent_ref, g_ref, xo_ref, go_ref, rbuf, rg, xa,
                   sem_local, send_0, rsem_0, send_a, recv_a, send_b, recv_b, send_c, recv_c):
    e, z, x, c = _coords()
    _barrier(ne, nz, nx, nc, True)
    sends = []
    own = [pltpu.make_async_copy(sent_ref.at[e], rbuf.at[e], sem_local.at[0]),
           pltpu.make_async_copy(g_ref.at[e], rg.at[e], sem_local.at[1])]
    for cp in own:
        cp.start()
    for t, (src, dst) in enumerate(((sent_ref, rbuf), (g_ref, rg))):
        for d in range(1, ne):
            cp = pltpu.make_async_remote_copy(
                src.at[(e + d) % ne], dst.at[e], send_0.at[t, d - 1], rsem_0.at[t, e],
                device_id=((e + d) % ne, z, x, c), device_id_type=MESH_ID)
            cp.start()
            sends.append(cp)
    for t, (src, dst) in enumerate(((sent_ref, rbuf), (g_ref, rg))):
        for d in range(1, ne):
            srce = (e + ne - d) % ne
            pltpu.make_async_remote_copy(
                src.at[e], dst.at[srce], send_0.at[t, d - 1], rsem_0.at[t, srce],
                device_id=(srce, z, x, c), device_id_type=MESH_ID).wait_recv()
    for cp in own:
        cp.wait()
    feats = xa.shape[0]
    blk = rbuf.shape[2]
    cols = ne * blk
    for b in range(ne):
        piece = rbuf[b]
        xa[:, b * blk:(b + 1) * blk] = piece[:feats]
        xa[:, cols + b * blk:cols + (b + 1) * blk] = piece[feats:]
        go_ref[:, b * blk:(b + 1) * blk] = rg[b]

    pairs = ((xa, xo_ref),)
    locals_ = []
    for t, (src, out) in enumerate(pairs):
        cp = pltpu.make_async_copy(src, out.at[z, x, c], sem_local.at[2 + t])
        cp.start()
        locals_.append(cp)
    for t, (src, out) in enumerate(pairs):
        for d in range(1, nz):
            cp = pltpu.make_async_remote_copy(
                src, out.at[z, x, c], send_a.at[t, d - 1], recv_a.at[t, d - 1],
                device_id=(e, (z + d) % nz, x, c), device_id_type=MESH_ID)
            cp.start()
            sends.append(cp)
    for t, (src, out) in enumerate(pairs):
        for d in range(1, nz):
            zs = (z + nz - d) % nz
            pltpu.make_async_remote_copy(
                src, out.at[zs, x, c], send_a.at[t, d - 1], recv_a.at[t, d - 1],
                device_id=(e, zs, x, c), device_id_type=MESH_ID).wait_recv()
    for cp in locals_:
        cp.wait()
    for t, (src, out) in enumerate(pairs):
        for d in range(1, nx):
            cp = pltpu.make_async_remote_copy(
                out.at[:, x, c], out.at[:, x, c], send_b.at[t, d - 1], recv_b.at[t, d - 1],
                device_id=(e, z, (x + d) % nx, c), device_id_type=MESH_ID)
            cp.start()
            sends.append(cp)
    for t, (src, out) in enumerate(pairs):
        for d in range(1, nx):
            xs = (x + nx - d) % nx
            pltpu.make_async_remote_copy(
                out.at[:, xs, c], out.at[:, xs, c], send_b.at[t, d - 1], recv_b.at[t, d - 1],
                device_id=(e, z, xs, c), device_id_type=MESH_ID).wait_recv()
    for t, (src, out) in enumerate(pairs):
        for d in range(1, nc):
            cp = pltpu.make_async_remote_copy(
                out.at[:, :, c], out.at[:, :, c], send_c.at[t, d - 1], recv_c.at[t, d - 1],
                device_id=(e, z, x, (c + d) % nc), device_id_type=MESH_ID)
            cp.start()
            sends.append(cp)
    for t, (src, out) in enumerate(pairs):
        for d in range(1, nc):
            cs = (c + nc - d) % nc
            pltpu.make_async_remote_copy(
                out.at[:, :, cs], out.at[:, :, cs], send_c.at[t, d - 1], recv_c.at[t, d - 1],
                device_id=(e, z, x, cs), device_id_type=MESH_ID).wait_recv()
    for cp in sends:
        cp.wait_send()


def ep_etp_gather(sent, gsend, nz, nx, nc):
    ne, two_feats, blk = sent.shape
    feats = two_feats // 2
    cols = ne * blk
    vmem = pltpu.VMEM
    dma = pltpu.SemaphoreType.DMA
    shape = jax.ShapeDtypeStruct((nz, nx, nc, feats, 2 * cols), sent.dtype)
    return pl.pallas_call(
        functools.partial(_gather_kernel, ne, nz, nx, nc),
        out_shape=(shape, jax.ShapeDtypeStruct((1, cols), gsend.dtype)),
        in_specs=[pl.BlockSpec(memory_space=vmem)] * 2,
        out_specs=(pl.BlockSpec(memory_space=vmem),) * 2,
        scratch_shapes=[
            pltpu.VMEM((ne, two_feats, blk), sent.dtype),
            pltpu.VMEM((ne, 1, blk), gsend.dtype),
            pltpu.VMEM((feats, 2 * cols), sent.dtype),
            dma((4,)),
            dma((2, max(ne - 1, 1))),
            dma((2, ne)),
            dma((2, max(nz - 1, 1))),
            dma((2, max(nz - 1, 1))),
            dma((2, max(nx - 1, 1))),
            dma((2, max(nx - 1, 1))),
            dma((2, max(nc - 1, 1))),
            dma((2, max(nc - 1, 1))),
        ],
        compiler_params=pltpu.CompilerParams(collective_id=0, has_side_effects=True),
    )(sent, gsend)


def _rs_kernel(ne, nz, nx, nc, part_ref, inner_ref, out_ref, recv_c, acc1, recv_b, acc2, recv_a,
               ir_c, in1, ir_b, in2, ir_a, fin,
               sem_local, send_c, rsem_c, send_b, rsem_b, send_a, rsem_a, send_d, rsem_d):
    e, z, x, c = _coords()
    _barrier(ne, nz, nx, nc, True)
    sends = []

    def exchange(pieces, peers_of, send_sem, recv_sem):
        n = len(peers_of)
        for t, (src_of, dst) in enumerate(pieces):
            for d in range(n):
                cp = pltpu.make_async_remote_copy(
                    src_of(d), dst.at[d], send_sem.at[t, d], recv_sem.at[t, d],
                    device_id=peers_of[d][0], device_id_type=MESH_ID)
                cp.start()
                sends.append(cp)
        for t, (src_of, dst) in enumerate(pieces):
            for d in range(n):
                pltpu.make_async_remote_copy(
                    dst.at[d], dst.at[d], send_sem.at[t, d], recv_sem.at[t, d],
                    device_id=peers_of[d][1], device_id_type=MESH_ID).wait_recv()

    peers = [((e, z, x, (c + d) % nc), (e, z, x, (c + nc - d) % nc)) for d in range(1, nc)]
    exchange([(lambda d: part_ref.at[:, :, (c + d + 1) % nc], recv_c), (lambda d: inner_ref, ir_c)],
             peers, send_c, rsem_c)

    def sum_c(i, carry):
        zi = i // nx
        xi = i % nx
        total = part_ref[zi, xi, c]
        for d in range(nc - 1):
            total = total + recv_c[d, zi, xi]
        acc1[zi, xi] = total
        return carry
    lax.fori_loop(0, nz * nx, sum_c, 0)
    total = inner_ref[...]
    for d in range(nc - 1):
        total = total + ir_c[d]
    in1[...] = total

    peers = [((e, z, (x + d) % nx, c), (e, z, (x + nx - d) % nx, c)) for d in range(1, nx)]
    exchange([(lambda d: acc1.at[:, (x + d + 1) % nx], recv_b), (lambda d: in1, ir_b)],
             peers, send_b, rsem_b)

    def sum_b(zi, carry):
        total = acc1[zi, x]
        for d in range(nx - 1):
            total = total + recv_b[d, zi]
        acc2[zi] = total
        return carry
    lax.fori_loop(0, nz, sum_b, 0)
    total = in1[...]
    for d in range(nx - 1):
        total = total + ir_b[d]
    in2[...] = total

    peers = [((e, (z + d) % nz, x, c), (e, (z + nz - d) % nz, x, c)) for d in range(1, nz)]
    exchange([(lambda d: acc2.at[(z + d + 1) % nz], recv_a), (lambda d: in2, ir_a)],
             peers, send_a, rsem_a)
    total = acc2[z]
    for d in range(nz - 1):
        total = total + recv_a[d]
    itotal = in2[...]
    for d in range(nz - 1):
        itotal = itotal + ir_a[d]

    half = total.shape[0]
    feats = 2 * half
    blk = fin.shape[2]
    cols = ne * blk
    for b in range(ne):
        fin[b, :half, :] = total[:, b * blk:(b + 1) * blk]
        fin[b, half:feats, :] = total[:, cols + b * blk:cols + (b + 1) * blk]
        fin[b, feats:feats + 1, :] = itotal[:, b * blk:(b + 1) * blk]
        fin[b, feats + 1:, :] = jnp.zeros((fin.shape[1] - feats - 1, blk), jnp.float32)
    local = pltpu.make_async_copy(fin.at[e], out_ref.at[e], sem_local.at[0])
    local.start()
    for d in range(1, ne):
        cp = pltpu.make_async_remote_copy(
            fin.at[(e + d) % ne], out_ref.at[e], send_d.at[d - 1], rsem_d.at[e],
            device_id=((e + d) % ne, z, x, c), device_id_type=MESH_ID)
        cp.start()
        sends.append(cp)
    for d in range(1, ne):
        src = (e + ne - d) % ne
        pltpu.make_async_remote_copy(
            fin.at[e], out_ref.at[src], send_d.at[d - 1], rsem_d.at[src],
            device_id=(src, z, x, c), device_id_type=MESH_ID).wait_recv()
    local.wait()
    for cp in sends:
        cp.wait_send()


def etp_reduce_scatter(part, inner, ne, blk):
    nz, nx, nc, feats, cols = part.shape
    pad_rows = -(-(2 * feats + 1) // 8) * 8
    f32 = jnp.float32
    vmem = pltpu.VMEM
    dma = pltpu.SemaphoreType.DMA
    mc, mx, mz = max(nc - 1, 1), max(nx - 1, 1), max(nz - 1, 1)
    return pl.pallas_call(
        functools.partial(_rs_kernel, ne, nz, nx, nc),
        out_shape=jax.ShapeDtypeStruct((ne, pad_rows, blk), f32),
        in_specs=[pl.BlockSpec(memory_space=vmem)] * 2,
        out_specs=pl.BlockSpec(memory_space=vmem),
        scratch_shapes=[
            pltpu.VMEM((mc, nz, nx, feats, cols), f32),
            pltpu.VMEM((nz, nx, feats, cols), f32),
            pltpu.VMEM((mx, nz, feats, cols), f32),
            pltpu.VMEM((nz, feats, cols), f32),
            pltpu.VMEM((mz, feats, cols), f32),
            pltpu.VMEM((mc, 1, cols // 2), f32),
            pltpu.VMEM((1, cols // 2), f32),
            pltpu.VMEM((mx, 1, cols // 2), f32),
            pltpu.VMEM((1, cols // 2), f32),
            pltpu.VMEM((mz, 1, cols // 2), f32),
            pltpu.VMEM((ne, pad_rows, blk), f32),
            dma((1,)),
            dma((2, mc)),
            dma((2, mc)),
            dma((2, mx)),
            dma((2, mx)),
            dma((2, mz)),
            dma((2, mz)),
            dma((max(ne - 1, 1),)),
            dma((ne,)),
        ],
        compiler_params=pltpu.CompilerParams(collective_id=1, has_side_effects=True),
    )(part, inner)


def per_device(tokens, routes, route_gates, cotangent, w_gate, w_up, w_down):
    ep_count = lax.axis_size("ep")
    nz, nx, nc = lax.axis_size("z"), lax.axis_size("x"), lax.axis_size("core")
    tok_count, width = tokens.shape
    flat_ids = routes.reshape(-1)
    pair_count = flat_ids.shape[0]
    onehot = (flat_ids[:, None] == jnp.arange(EXPERTS, dtype=jnp.int32)[None, :]).astype(jnp.int32)
    before = jnp.cumsum(onehot, axis=0) - onehot
    slot_id = jnp.sum(before * onehot, axis=1)
    target = flat_ids * CAP + slot_id
    slot_table = (
        jnp.full((EXPERTS * CAP,), pair_count, jnp.int32)
        .at[target]
        .set(jnp.arange(pair_count, dtype=jnp.int32))
    )
    token_of_slot = slot_table // 2
    gate_flat = jnp.concatenate([route_gates.reshape(-1), jnp.zeros((1,), jnp.float32)])
    slot_gate = gate_flat[slot_table]
    xc = jnp.concatenate([tokens, cotangent], axis=1)
    xc_pad = jnp.concatenate([xc, jnp.zeros((1, 2 * width), jnp.bfloat16)], axis=0)
    sent = jnp.transpose(xc_pad[token_of_slot].reshape(ep_count, CAP, 2 * width), (0, 2, 1))
    gsend = slot_gate.reshape(ep_count, 1, CAP)
    rows = ep_count * CAP
    xc_all, gates_recv = ep_etp_gather(sent, gsend, nz, nx, nc)
    feat = nz * nx * nc * width
    xt = xc_all[..., :rows].reshape(feat, rows)
    ct = xc_all[..., rows:].reshape(feat, rows)
    slot_g = gates_recv.reshape(1, rows)
    dyt = (slot_g * ct.astype(jnp.float32)).astype(jnp.bfloat16)
    wg, wu, wd = w_gate[0], w_up[0], w_down[0]
    f32 = jnp.float32

    def dims(a, b):
        return (((a,), (b,)), ((), ()))
    gate_pre = lax.dot_general(xt, wg, dims(0, 0), preferred_element_type=f32)
    up_pre = lax.dot_general(xt, wu, dims(0, 0), preferred_element_type=f32)
    sigma = jax.nn.sigmoid(gate_pre)
    hidden = (jax.nn.silu(gate_pre) * up_pre).astype(jnp.bfloat16)
    out_t = lax.dot_general(wd, hidden, dims(0, 1), preferred_element_type=f32)
    d_hidden = lax.dot_general(dyt, wd, dims(0, 1), preferred_element_type=f32)
    d_up = (d_hidden * jax.nn.silu(gate_pre)).astype(jnp.bfloat16)
    d_gate = (d_hidden * up_pre * sigma * (1.0 + gate_pre * (1.0 - sigma))).astype(jnp.bfloat16)
    grad_down = lax.dot_general(hidden, dyt, dims(0, 1), preferred_element_type=f32)
    grad_gate_w = lax.dot_general(xt, d_gate, dims(1, 0), preferred_element_type=f32)
    grad_up_w = lax.dot_general(xt, d_up, dims(1, 0), preferred_element_type=f32)
    inner = jnp.sum(out_t * ct.astype(f32), axis=0, keepdims=True)
    part = out_t.reshape(nz, nx, nc, width // 2, 2 * rows)
    back = etp_reduce_scatter(part, inner, ep_count, CAP)
    half = width // 2
    feats_back = back[:, :width].reshape(EXPERTS, 2, half, CAP)
    feats_back = jnp.transpose(feats_back, (0, 3, 2, 1)).reshape(EXPERTS * CAP, width)
    inner_back = back[:, width].reshape(EXPERTS * CAP)
    pair_rows = feats_back[target].reshape(tok_count, 2, width)
    mixed = jnp.sum(route_gates[:, :, None] * pair_rows, axis=1).astype(jnp.bfloat16)
    grad_gates = inner_back[target].reshape(tok_count, 2)
    return (
        mixed,
        grad_gates,
        grad_gate_w.astype(jnp.bfloat16)[None],
        grad_up_w.astype(jnp.bfloat16)[None],
        grad_down.astype(jnp.bfloat16)[None],
    )


def solution(mesh):
    ep = mesh.shape["ep"]
    etp = mesh.shape["etp"]
    nz, nx, nc = sub_sizes(etp)
    devs = np.asarray(mesh.devices).reshape(ep, nz, nx, nc)
    mesh2 = Mesh(devs, ("ep",) + SUB)
    in_specs = (
        P("ep", SUB),
        P("ep", None),
        P("ep", None),
        P("ep", SUB),
        P("ep", None, SUB),
        P("ep", None, SUB),
        P("ep", SUB, None),
    )
    out_specs = (
        P("ep", SUB),
        P("ep", None),
        P("ep", None, SUB),
        P("ep", None, SUB),
        P("ep", SUB, None),
    )
    return jax.shard_map(
        per_device, mesh=mesh2, in_specs=in_specs, out_specs=out_specs, check_vma=False
    )
```

```python
import functools

import jax
import jax.numpy as jnp
import numpy as np
from jax import lax
from jax.experimental import pallas as pl
from jax.experimental.pallas import tpu as pltpu
from jax.sharding import Mesh
from jax.sharding import PartitionSpec as P

EXPERTS = 8
CAP = 24
SUB = ("z", "x", "core")
MESH_ID = pl.DeviceIdType.MESH


def sub_sizes(etp):
    if etp % 8 == 0:
        return (etp // 8, 4, 2)
    return (etp, 1, 1)


def _coords():
    return (lax.axis_index("ep"), lax.axis_index("z"), lax.axis_index("x"), lax.axis_index("core"))


def _barrier(ne, nz, nx, nc, with_ep):
    e, z, x, c = _coords()
    barrier = pltpu.get_barrier_semaphore()
    count = 0
    for d in range(1, nz):
        pl.semaphore_signal(barrier, inc=1, device_id=(e, (z + d) % nz, x, c), device_id_type=MESH_ID)
        count += 1
    for d in range(1, nx):
        pl.semaphore_signal(barrier, inc=1, device_id=(e, z, (x + d) % nx, c), device_id_type=MESH_ID)
        count += 1
    for d in range(1, nc):
        pl.semaphore_signal(barrier, inc=1, device_id=(e, z, x, (c + d) % nc), device_id_type=MESH_ID)
        count += 1
    if with_ep:
        for d in range(1, ne):
            pl.semaphore_signal(barrier, inc=1, device_id=((e + d) % ne, z, x, c), device_id_type=MESH_ID)
            count += 1
    pl.semaphore_wait(barrier, count)


def _gather_kernel(ne, nz, nx, nc, sent_ref, g_ref, xo_ref, go_ref, rbuf, rg, xa,
                   sem_local, send_0, rsem_0, send_a, recv_a, send_b, recv_b, send_c, recv_c):
    e, z, x, c = _coords()
    _barrier(ne, nz, nx, nc, True)
    sends = []
    own = [pltpu.make_async_copy(sent_ref.at[e], rbuf.at[e], sem_local.at[0]),
           pltpu.make_async_copy(g_ref.at[e], rg.at[e], sem_local.at[1])]
    for cp in own:
        cp.start()
    for t, (src, dst) in enumerate(((sent_ref, rbuf), (g_ref, rg))):
        for d in range(1, ne):
            cp = pltpu.make_async_remote_copy(
                src.at[(e + d) % ne], dst.at[e], send_0.at[t, d - 1], rsem_0.at[t, e],
                device_id=((e + d) % ne, z, x, c), device_id_type=MESH_ID)
            cp.start()
            sends.append(cp)
    for t, (src, dst) in enumerate(((sent_ref, rbuf), (g_ref, rg))):
        for d in range(1, ne):
            srce = (e + ne - d) % ne
            pltpu.make_async_remote_copy(
                src.at[e], dst.at[srce], send_0.at[t, d - 1], rsem_0.at[t, srce],
                device_id=(srce, z, x, c), device_id_type=MESH_ID).wait_recv()
    for cp in own:
        cp.wait()
    feats = xa.shape[0]
    blk = rbuf.shape[2]
    cols = ne * blk
    for b in range(ne):
        piece = rbuf[b]
        xa[:, b * blk:(b + 1) * blk] = piece[:feats]
        xa[:, cols + b * blk:cols + (b + 1) * blk] = piece[feats:]
        go_ref[:, b * blk:(b + 1) * blk] = rg[b]

    out = xo_ref
    local = pltpu.make_async_copy(xa, out.at[z, x, c], sem_local.at[2])
    local.start()
    for d in range(1, nz):
        cp = pltpu.make_async_remote_copy(
            xa, out.at[z, x, c], send_a.at[d - 1], recv_a.at[d - 1],
            device_id=(e, (z + d) % nz, x, c), device_id_type=MESH_ID)
        cp.start()
        sends.append(cp)

    def forward(src, zz, xs, to_x):
        if to_x:
            for dx in range(1, nx):
                cp = pltpu.make_async_remote_copy(
                    src, out.at[zz, x, c], send_b.at[dx - 1, zz], recv_b.at[dx - 1, zz],
                    device_id=(e, z, (x + dx) % nx, c), device_id_type=MESH_ID)
                cp.start()
                sends.append(cp)
        for dc in range(1, nc):
            cp = pltpu.make_async_remote_copy(
                src, out.at[zz, xs, c], send_c.at[dc - 1, xs, zz], recv_c.at[dc - 1, xs, zz],
                device_id=(e, z, x, (c + dc) % nc), device_id_type=MESH_ID)
            cp.start()
            sends.append(cp)

    forward(xa, z, x, True)
    for d in range(1, nz):
        zs = (z + nz - d) % nz
        pltpu.make_async_remote_copy(
            xa, out.at[zs, x, c], send_a.at[d - 1], recv_a.at[d - 1],
            device_id=(e, zs, x, c), device_id_type=MESH_ID).wait_recv()
        forward(out.at[zs, x, c], zs, x, True)
    for dx in range(1, nx):
        xs = (x + nx - dx) % nx
        for zz in range(nz):
            pltpu.make_async_remote_copy(
                xa, out.at[zz, xs, c], send_b.at[dx - 1, zz], recv_b.at[dx - 1, zz],
                device_id=(e, z, xs, c), device_id_type=MESH_ID).wait_recv()
            forward(out.at[zz, xs, c], zz, xs, False)
    for dc in range(1, nc):
        cs = (c + nc - dc) % nc
        for xx in range(nx):
            for zz in range(nz):
                pltpu.make_async_remote_copy(
                    xa, out.at[zz, xx, cs], send_c.at[dc - 1, xx, zz], recv_c.at[dc - 1, xx, zz],
                    device_id=(e, z, x, cs), device_id_type=MESH_ID).wait_recv()
    local.wait()
    for cp in sends:
        cp.wait_send()


def ep_etp_gather(sent, gsend, nz, nx, nc):
    ne, two_feats, blk = sent.shape
    feats = two_feats // 2
    cols = ne * blk
    vmem = pltpu.VMEM
    dma = pltpu.SemaphoreType.DMA
    shape = jax.ShapeDtypeStruct((nz, nx, nc, feats, 2 * cols), sent.dtype)
    return pl.pallas_call(
        functools.partial(_gather_kernel, ne, nz, nx, nc),
        out_shape=(shape, jax.ShapeDtypeStruct((1, cols), gsend.dtype)),
        in_specs=[pl.BlockSpec(memory_space=vmem)] * 2,
        out_specs=(pl.BlockSpec(memory_space=vmem),) * 2,
        scratch_shapes=[
            pltpu.VMEM((ne, two_feats, blk), sent.dtype),
            pltpu.VMEM((ne, 1, blk), gsend.dtype),
            pltpu.VMEM((feats, 2 * cols), sent.dtype),
            dma((3,)),
            dma((2, max(ne - 1, 1))),
            dma((2, ne)),
            dma((max(nz - 1, 1),)),
            dma((max(nz - 1, 1),)),
            dma((max(nx - 1, 1), nz)),
            dma((max(nx - 1, 1), nz)),
            dma((max(nc - 1, 1), nx, nz)),
            dma((max(nc - 1, 1), nx, nz)),
        ],
        compiler_params=pltpu.CompilerParams(collective_id=0, has_side_effects=True),
    )(sent, gsend)


def _rs_kernel(ne, nz, nx, nc, part_ref, inner_ref, out_ref, recv_c, acc1, recv_b, acc2, recv_a,
               ir_c, in1, ir_b, in2, ir_a, fin,
               sem_local, send_c, rsem_c, send_b, rsem_b, send_a, rsem_a, send_d, rsem_d):
    e, z, x, c = _coords()
    _barrier(ne, nz, nx, nc, True)
    sends = []

    def exchange(pieces, peers_of, send_sem, recv_sem):
        n = len(peers_of)
        for t, (src_of, dst) in enumerate(pieces):
            for d in range(n):
                cp = pltpu.make_async_remote_copy(
                    src_of(d), dst.at[d], send_sem.at[t, d], recv_sem.at[t, d],
                    device_id=peers_of[d][0], device_id_type=MESH_ID)
                cp.start()
                sends.append(cp)
        for t, (src_of, dst) in enumerate(pieces):
            for d in range(n):
                pltpu.make_async_remote_copy(
                    dst.at[d], dst.at[d], send_sem.at[t, d], recv_sem.at[t, d],
                    device_id=peers_of[d][1], device_id_type=MESH_ID).wait_recv()

    peers = [((e, z, x, (c + d) % nc), (e, z, x, (c + nc - d) % nc)) for d in range(1, nc)]
    exchange([(lambda d: part_ref.at[:, :, (c + d + 1) % nc], recv_c), (lambda d: inner_ref, ir_c)],
             peers, send_c, rsem_c)

    def sum_c(i, carry):
        zi = i // nx
        xi = i % nx
        total = part_ref[zi, xi, c]
        for d in range(nc - 1):
            total = total + recv_c[d, zi, xi]
        acc1[zi, xi] = total
        return carry
    lax.fori_loop(0, nz * nx, sum_c, 0)
    total = inner_ref[...]
    for d in range(nc - 1):
        total = total + ir_c[d]
    in1[...] = total

    peers = [((e, z, (x + d) % nx, c), (e, z, (x + nx - d) % nx, c)) for d in range(1, nx)]
    exchange([(lambda d: acc1.at[:, (x + d + 1) % nx], recv_b), (lambda d: in1, ir_b)],
             peers, send_b, rsem_b)

    def sum_b(zi, carry):
        total = acc1[zi, x]
        for d in range(nx - 1):
            total = total + recv_b[d, zi]
        acc2[zi] = total
        return carry
    lax.fori_loop(0, nz, sum_b, 0)
    total = in1[...]
    for d in range(nx - 1):
        total = total + ir_b[d]
    in2[...] = total

    peers = [((e, (z + d) % nz, x, c), (e, (z + nz - d) % nz, x, c)) for d in range(1, nz)]
    exchange([(lambda d: acc2.at[(z + d + 1) % nz], recv_a), (lambda d: in2, ir_a)],
             peers, send_a, rsem_a)
    total = acc2[z]
    for d in range(nz - 1):
        total = total + recv_a[d]
    itotal = in2[...]
    for d in range(nz - 1):
        itotal = itotal + ir_a[d]

    half = total.shape[0]
    feats = 2 * half
    blk = fin.shape[2]
    cols = ne * blk
    for b in range(ne):
        fin[b, :half, :] = total[:, b * blk:(b + 1) * blk]
        fin[b, half:feats, :] = total[:, cols + b * blk:cols + (b + 1) * blk]
        fin[b, feats:feats + 1, :] = itotal[:, b * blk:(b + 1) * blk]
        fin[b, feats + 1:, :] = jnp.zeros((fin.shape[1] - feats - 1, blk), jnp.float32)
    local = pltpu.make_async_copy(fin.at[e], out_ref.at[e], sem_local.at[0])
    local.start()
    for d in range(1, ne):
        cp = pltpu.make_async_remote_copy(
            fin.at[(e + d) % ne], out_ref.at[e], send_d.at[d - 1], rsem_d.at[e],
            device_id=((e + d) % ne, z, x, c), device_id_type=MESH_ID)
        cp.start()
        sends.append(cp)
    for d in range(1, ne):
        src = (e + ne - d) % ne
        pltpu.make_async_remote_copy(
            fin.at[e], out_ref.at[src], send_d.at[d - 1], rsem_d.at[src],
            device_id=(src, z, x, c), device_id_type=MESH_ID).wait_recv()
    local.wait()
    for cp in sends:
        cp.wait_send()


def etp_reduce_scatter(part, inner, ne, blk):
    nz, nx, nc, feats, cols = part.shape
    pad_rows = -(-(2 * feats + 1) // 8) * 8
    f32 = jnp.float32
    vmem = pltpu.VMEM
    dma = pltpu.SemaphoreType.DMA
    mc, mx, mz = max(nc - 1, 1), max(nx - 1, 1), max(nz - 1, 1)
    return pl.pallas_call(
        functools.partial(_rs_kernel, ne, nz, nx, nc),
        out_shape=jax.ShapeDtypeStruct((ne, pad_rows, blk), f32),
        in_specs=[pl.BlockSpec(memory_space=vmem)] * 2,
        out_specs=pl.BlockSpec(memory_space=vmem),
        scratch_shapes=[
            pltpu.VMEM((mc, nz, nx, feats, cols), f32),
            pltpu.VMEM((nz, nx, feats, cols), f32),
            pltpu.VMEM((mx, nz, feats, cols), f32),
            pltpu.VMEM((nz, feats, cols), f32),
            pltpu.VMEM((mz, feats, cols), f32),
            pltpu.VMEM((mc, 1, cols // 2), f32),
            pltpu.VMEM((1, cols // 2), f32),
            pltpu.VMEM((mx, 1, cols // 2), f32),
            pltpu.VMEM((1, cols // 2), f32),
            pltpu.VMEM((mz, 1, cols // 2), f32),
            pltpu.VMEM((ne, pad_rows, blk), f32),
            dma((1,)),
            dma((2, mc)),
            dma((2, mc)),
            dma((2, mx)),
            dma((2, mx)),
            dma((2, mz)),
            dma((2, mz)),
            dma((max(ne - 1, 1),)),
            dma((ne,)),
        ],
        compiler_params=pltpu.CompilerParams(collective_id=1, has_side_effects=True),
    )(part, inner)


def per_device(tokens, routes, route_gates, cotangent, w_gate, w_up, w_down):
    ep_count = lax.axis_size("ep")
    nz, nx, nc = lax.axis_size("z"), lax.axis_size("x"), lax.axis_size("core")
    tok_count, width = tokens.shape
    flat_ids = routes.reshape(-1)
    pair_count = flat_ids.shape[0]
    onehot = (flat_ids[:, None] == jnp.arange(EXPERTS, dtype=jnp.int32)[None, :]).astype(jnp.int32)
    before = jnp.cumsum(onehot, axis=0) - onehot
    slot_id = jnp.sum(before * onehot, axis=1)
    target = flat_ids * CAP + slot_id
    slot_table = (
        jnp.full((EXPERTS * CAP,), pair_count, jnp.int32)
        .at[target]
        .set(jnp.arange(pair_count, dtype=jnp.int32))
    )
    token_of_slot = slot_table // 2
    gate_flat = jnp.concatenate([route_gates.reshape(-1), jnp.zeros((1,), jnp.float32)])
    slot_gate = gate_flat[slot_table]
    xc = jnp.concatenate([tokens, cotangent], axis=1)
    xc_pad = jnp.concatenate([xc, jnp.zeros((1, 2 * width), jnp.bfloat16)], axis=0)
    sent = jnp.transpose(xc_pad[token_of_slot].reshape(ep_count, CAP, 2 * width), (0, 2, 1))
    gsend = slot_gate.reshape(ep_count, 1, CAP)
    rows = ep_count * CAP
    xc_all, gates_recv = ep_etp_gather(sent, gsend, nz, nx, nc)
    feat = nz * nx * nc * width
    xt = xc_all[..., :rows].reshape(feat, rows)
    ct = xc_all[..., rows:].reshape(feat, rows)
    slot_g = gates_recv.reshape(1, rows)
    dyt = (slot_g * ct.astype(jnp.float32)).astype(jnp.bfloat16)
    wg, wu, wd = w_gate[0], w_up[0], w_down[0]
    f32 = jnp.float32

    def dims(a, b):
        return (((a,), (b,)), ((), ()))
    gate_pre = lax.dot_general(xt, wg, dims(0, 0), preferred_element_type=f32)
    up_pre = lax.dot_general(xt, wu, dims(0, 0), preferred_element_type=f32)
    sigma = jax.nn.sigmoid(gate_pre)
    hidden = (jax.nn.silu(gate_pre) * up_pre).astype(jnp.bfloat16)
    out_t = lax.dot_general(wd, hidden, dims(0, 1), preferred_element_type=f32)
    d_hidden = lax.dot_general(dyt, wd, dims(0, 1), preferred_element_type=f32)
    d_up = (d_hidden * jax.nn.silu(gate_pre)).astype(jnp.bfloat16)
    d_gate = (d_hidden * up_pre * sigma * (1.0 + gate_pre * (1.0 - sigma))).astype(jnp.bfloat16)
    grad_down = lax.dot_general(hidden, dyt, dims(0, 1), preferred_element_type=f32)
    grad_gate_w = lax.dot_general(xt, d_gate, dims(1, 0), preferred_element_type=f32)
    grad_up_w = lax.dot_general(xt, d_up, dims(1, 0), preferred_element_type=f32)
    inner = jnp.sum(out_t * ct.astype(f32), axis=0, keepdims=True)
    part = out_t.reshape(nz, nx, nc, width // 2, 2 * rows)
    back = etp_reduce_scatter(part, inner, ep_count, CAP)
    half = width // 2
    feats_back = back[:, :width].reshape(EXPERTS, 2, half, CAP)
    feats_back = jnp.transpose(feats_back, (0, 3, 2, 1)).reshape(EXPERTS * CAP, width)
    inner_back = back[:, width].reshape(EXPERTS * CAP)
    pair_rows = feats_back[target].reshape(tok_count, 2, width)
    mixed = jnp.sum(route_gates[:, :, None] * pair_rows, axis=1).astype(jnp.bfloat16)
    grad_gates = inner_back[target].reshape(tok_count, 2)
    return (
        mixed,
        grad_gates,
        grad_gate_w.astype(jnp.bfloat16)[None],
        grad_up_w.astype(jnp.bfloat16)[None],
        grad_down.astype(jnp.bfloat16)[None],
    )


def solution(mesh):
    ep = mesh.shape["ep"]
    etp = mesh.shape["etp"]
    nz, nx, nc = sub_sizes(etp)
    devs = np.asarray(mesh.devices).reshape(ep, nz, nx, nc)
    mesh2 = Mesh(devs, ("ep",) + SUB)
    in_specs = (
        P("ep", SUB),
        P("ep", None),
        P("ep", None),
        P("ep", SUB),
        P("ep", None, SUB),
        P("ep", None, SUB),
        P("ep", SUB, None),
    )
    out_specs = (
        P("ep", SUB),
        P("ep", None),
        P("ep", None, SUB),
        P("ep", None, SUB),
        P("ep", SUB, None),
    )
    return jax.shard_map(
        per_device, mesh=mesh2, in_specs=in_specs, out_specs=out_specs, check_vma=False
    )
```

```python
import functools

import jax
import jax.numpy as jnp
import numpy as np
from jax import lax
from jax.experimental import pallas as pl
from jax.experimental.pallas import tpu as pltpu
from jax.sharding import Mesh
from jax.sharding import PartitionSpec as P

EXPERTS = 8
CAP = 24
SUB = ("z", "x", "core")
MESH_ID = pl.DeviceIdType.MESH


def sub_sizes(etp):
    if etp % 8 == 0:
        return (etp // 8, 4, 2)
    return (etp, 1, 1)


def _coords():
    return (lax.axis_index("ep"), lax.axis_index("z"), lax.axis_index("x"), lax.axis_index("core"))


def _barrier(ne, nz, nx, nc, with_ep):
    e, z, x, c = _coords()
    barrier = pltpu.get_barrier_semaphore()
    count = 0
    for d in range(1, nz):
        pl.semaphore_signal(barrier, inc=1, device_id=(e, (z + d) % nz, x, c), device_id_type=MESH_ID)
        count += 1
    for d in range(1, nx):
        pl.semaphore_signal(barrier, inc=1, device_id=(e, z, (x + d) % nx, c), device_id_type=MESH_ID)
        count += 1
    for d in range(1, nc):
        pl.semaphore_signal(barrier, inc=1, device_id=(e, z, x, (c + d) % nc), device_id_type=MESH_ID)
        count += 1
    if with_ep:
        for d in range(1, ne):
            pl.semaphore_signal(barrier, inc=1, device_id=((e + d) % ne, z, x, c), device_id_type=MESH_ID)
            count += 1
    pl.semaphore_wait(barrier, count)


def _gather_kernel(ne, nz, nx, nc, sent_ref, g_ref, xo_ref, go_ref, rbuf, rg, xa,
                   sem_local, send_0, rsem_0, send_a, recv_a, send_b, recv_b, send_c, recv_c):
    e, z, x, c = _coords()
    _barrier(ne, nz, nx, nc, True)
    sends = []
    own = [pltpu.make_async_copy(sent_ref.at[e], rbuf.at[e], sem_local.at[0]),
           pltpu.make_async_copy(g_ref.at[e], rg.at[e], sem_local.at[1])]
    for cp in own:
        cp.start()
    for t, (src, dst) in enumerate(((sent_ref, rbuf), (g_ref, rg))):
        for d in range(1, ne):
            cp = pltpu.make_async_remote_copy(
                src.at[(e + d) % ne], dst.at[e], send_0.at[t, d - 1], rsem_0.at[t, e],
                device_id=((e + d) % ne, z, x, c), device_id_type=MESH_ID)
            cp.start()
            sends.append(cp)
    for t, (src, dst) in enumerate(((sent_ref, rbuf), (g_ref, rg))):
        for d in range(1, ne):
            srce = (e + ne - d) % ne
            pltpu.make_async_remote_copy(
                src.at[e], dst.at[srce], send_0.at[t, d - 1], rsem_0.at[t, srce],
                device_id=(srce, z, x, c), device_id_type=MESH_ID).wait_recv()
    for cp in own:
        cp.wait()
    feats = xa.shape[0]
    blk = rbuf.shape[2]
    cols = ne * blk
    for b in range(ne):
        piece = rbuf[b]
        xa[:, b * blk:(b + 1) * blk] = piece[:feats]
        xa[:, cols + b * blk:cols + (b + 1) * blk] = piece[feats:]
        go_ref[:, b * blk:(b + 1) * blk] = rg[b]

    out = xo_ref
    local = pltpu.make_async_copy(xa, out.at[z, x, c], sem_local.at[2])
    local.start()
    for d in range(1, nz):
        cp = pltpu.make_async_remote_copy(
            xa, out.at[z, x, c], send_a.at[d - 1], recv_a.at[d - 1],
            device_id=(e, (z + d) % nz, x, c), device_id_type=MESH_ID)
        cp.start()
        sends.append(cp)

    def forward(src, zz, xs, to_x):
        if to_x:
            for dx in range(1, nx):
                cp = pltpu.make_async_remote_copy(
                    src, out.at[zz, x, c], send_b.at[dx - 1, zz], recv_b.at[dx - 1, zz],
                    device_id=(e, z, (x + dx) % nx, c), device_id_type=MESH_ID)
                cp.start()
                sends.append(cp)
        for dc in range(1, nc):
            cp = pltpu.make_async_remote_copy(
                src, out.at[zz, xs, c], send_c.at[dc - 1, xs, zz], recv_c.at[dc - 1, xs, zz],
                device_id=(e, z, x, (c + dc) % nc), device_id_type=MESH_ID)
            cp.start()
            sends.append(cp)

    forward(xa, z, x, True)
    for d in range(1, nz):
        zs = (z + nz - d) % nz
        pltpu.make_async_remote_copy(
            xa, out.at[zs, x, c], send_a.at[d - 1], recv_a.at[d - 1],
            device_id=(e, zs, x, c), device_id_type=MESH_ID).wait_recv()
        forward(out.at[zs, x, c], zs, x, True)
    for dx in range(1, nx):
        xs = (x + nx - dx) % nx
        for zz in range(nz):
            pltpu.make_async_remote_copy(
                xa, out.at[zz, xs, c], send_b.at[dx - 1, zz], recv_b.at[dx - 1, zz],
                device_id=(e, z, xs, c), device_id_type=MESH_ID).wait_recv()
            forward(out.at[zz, xs, c], zz, xs, False)
    for dc in range(1, nc):
        cs = (c + nc - dc) % nc
        for xx in range(nx):
            for zz in range(nz):
                pltpu.make_async_remote_copy(
                    xa, out.at[zz, xx, cs], send_c.at[dc - 1, xx, zz], recv_c.at[dc - 1, xx, zz],
                    device_id=(e, z, x, cs), device_id_type=MESH_ID).wait_recv()
    local.wait()
    for cp in sends:
        cp.wait_send()


def ep_etp_gather(sent, gsend, nz, nx, nc):
    ne, two_feats, blk = sent.shape
    feats = two_feats // 2
    cols = ne * blk
    vmem = pltpu.VMEM
    dma = pltpu.SemaphoreType.DMA
    shape = jax.ShapeDtypeStruct((nz, nx, nc, feats, 2 * cols), sent.dtype)
    return pl.pallas_call(
        functools.partial(_gather_kernel, ne, nz, nx, nc),
        out_shape=(shape, jax.ShapeDtypeStruct((1, cols), gsend.dtype)),
        in_specs=[pl.BlockSpec(memory_space=vmem)] * 2,
        out_specs=(pl.BlockSpec(memory_space=vmem),) * 2,
        scratch_shapes=[
            pltpu.VMEM((ne, two_feats, blk), sent.dtype),
            pltpu.VMEM((ne, 1, blk), gsend.dtype),
            pltpu.VMEM((feats, 2 * cols), sent.dtype),
            dma((3,)),
            dma((2, max(ne - 1, 1))),
            dma((2, ne)),
            dma((max(nz - 1, 1),)),
            dma((max(nz - 1, 1),)),
            dma((max(nx - 1, 1), nz)),
            dma((max(nx - 1, 1), nz)),
            dma((max(nc - 1, 1), nx, nz)),
            dma((max(nc - 1, 1), nx, nz)),
        ],
        compiler_params=pltpu.CompilerParams(collective_id=0, has_side_effects=True),
    )(sent, gsend)


def _rs_kernel(ne, nz, nx, nc, part_ref, partb_ref, inner_ref, out_ref, recv_c, acc1, acc1b, recv_b, acc2, acc2b,
               recv_a, ir_c, in1, ir_b, in2, ir_a, fin,
               sem_local, send_c, rsem_c, send_b, rsem_b, send_a, rsem_a, send_d, rsem_d):
    e, z, x, c = _coords()
    _barrier(ne, nz, nx, nc, True)
    sends = []

    def exchange(pieces, peers_of, send_sem, recv_sem):
        n = len(peers_of)
        for t, (src_of, dst) in enumerate(pieces):
            for d in range(n):
                cp = pltpu.make_async_remote_copy(
                    src_of(d), dst.at[d], send_sem.at[t, d], recv_sem.at[t, d],
                    device_id=peers_of[d][0], device_id_type=MESH_ID)
                cp.start()
                sends.append(cp)
        for t, (src_of, dst) in enumerate(pieces):
            for d in range(n):
                pltpu.make_async_remote_copy(
                    dst.at[d], dst.at[d], send_sem.at[t, d], recv_sem.at[t, d],
                    device_id=peers_of[d][1], device_id_type=MESH_ID).wait_recv()

    peers = [((e, z, x, (c + d) % nc), (e, z, x, (c + nc - d) % nc)) for d in range(1, nc)]
    exchange([(lambda d: partb_ref.at[:, :, (c + d + 1) % nc], recv_c), (lambda d: inner_ref, ir_c)],
             peers, send_c, rsem_c)

    def sum_c(i, carry):
        zi = i // nx
        xi = i % nx
        total = part_ref[zi, xi, c]
        for d in range(nc - 1):
            total = total + recv_c[d, zi, xi].astype(jnp.float32)
        acc1[zi, xi] = total
        acc1b[zi, xi] = total.astype(acc1b.dtype)
        return carry
    lax.fori_loop(0, nz * nx, sum_c, 0)
    total = inner_ref[...]
    for d in range(nc - 1):
        total = total + ir_c[d]
    in1[...] = total

    peers = [((e, z, (x + d) % nx, c), (e, z, (x + nx - d) % nx, c)) for d in range(1, nx)]
    exchange([(lambda d: acc1b.at[:, (x + d + 1) % nx], recv_b), (lambda d: in1, ir_b)],
             peers, send_b, rsem_b)

    def sum_b(zi, carry):
        total = acc1[zi, x]
        for d in range(nx - 1):
            total = total + recv_b[d, zi].astype(jnp.float32)
        acc2[zi] = total
        acc2b[zi] = total.astype(acc2b.dtype)
        return carry
    lax.fori_loop(0, nz, sum_b, 0)
    total = in1[...]
    for d in range(nx - 1):
        total = total + ir_b[d]
    in2[...] = total

    peers = [((e, (z + d) % nz, x, c), (e, (z + nz - d) % nz, x, c)) for d in range(1, nz)]
    exchange([(lambda d: acc2b.at[(z + d + 1) % nz], recv_a), (lambda d: in2, ir_a)],
             peers, send_a, rsem_a)
    total = acc2[z]
    for d in range(nz - 1):
        total = total + recv_a[d].astype(jnp.float32)
    itotal = in2[...]
    for d in range(nz - 1):
        itotal = itotal + ir_a[d]

    half = total.shape[0]
    feats = 2 * half
    blk = fin.shape[2]
    cols = ne * blk
    for b in range(ne):
        fin[b, :half, :] = total[:, b * blk:(b + 1) * blk]
        fin[b, half:feats, :] = total[:, cols + b * blk:cols + (b + 1) * blk]
        fin[b, feats:feats + 1, :] = itotal[:, b * blk:(b + 1) * blk]
        fin[b, feats + 1:, :] = jnp.zeros((fin.shape[1] - feats - 1, blk), jnp.float32)
    local = pltpu.make_async_copy(fin.at[e], out_ref.at[e], sem_local.at[0])
    local.start()
    for d in range(1, ne):
        cp = pltpu.make_async_remote_copy(
            fin.at[(e + d) % ne], out_ref.at[e], send_d.at[d - 1], rsem_d.at[e],
            device_id=((e + d) % ne, z, x, c), device_id_type=MESH_ID)
        cp.start()
        sends.append(cp)
    for d in range(1, ne):
        src = (e + ne - d) % ne
        pltpu.make_async_remote_copy(
            fin.at[e], out_ref.at[src], send_d.at[d - 1], rsem_d.at[src],
            device_id=(src, z, x, c), device_id_type=MESH_ID).wait_recv()
    local.wait()
    for cp in sends:
        cp.wait_send()


def etp_reduce_scatter(part, inner, ne, blk):
    bf16 = jnp.bfloat16
    nz, nx, nc, feats, cols = part.shape
    pad_rows = -(-(2 * feats + 1) // 8) * 8
    f32 = jnp.float32
    vmem = pltpu.VMEM
    dma = pltpu.SemaphoreType.DMA
    mc, mx, mz = max(nc - 1, 1), max(nx - 1, 1), max(nz - 1, 1)
    return pl.pallas_call(
        functools.partial(_rs_kernel, ne, nz, nx, nc),
        out_shape=jax.ShapeDtypeStruct((ne, pad_rows, blk), f32),
        in_specs=[pl.BlockSpec(memory_space=vmem)] * 3,
        out_specs=pl.BlockSpec(memory_space=vmem),
        scratch_shapes=[
            pltpu.VMEM((mc, nz, nx, feats, cols), bf16),
            pltpu.VMEM((nz, nx, feats, cols), f32),
            pltpu.VMEM((nz, nx, feats, cols), bf16),
            pltpu.VMEM((mx, nz, feats, cols), bf16),
            pltpu.VMEM((nz, feats, cols), f32),
            pltpu.VMEM((nz, feats, cols), bf16),
            pltpu.VMEM((mz, feats, cols), bf16),
            pltpu.VMEM((mc, 1, cols // 2), f32),
            pltpu.VMEM((1, cols // 2), f32),
            pltpu.VMEM((mx, 1, cols // 2), f32),
            pltpu.VMEM((1, cols // 2), f32),
            pltpu.VMEM((mz, 1, cols // 2), f32),
            pltpu.VMEM((ne, pad_rows, blk), f32),
            dma((1,)),
            dma((2, mc)),
            dma((2, mc)),
            dma((2, mx)),
            dma((2, mx)),
            dma((2, mz)),
            dma((2, mz)),
            dma((max(ne - 1, 1),)),
            dma((ne,)),
        ],
        compiler_params=pltpu.CompilerParams(collective_id=1, has_side_effects=True),
    )(part, part.astype(bf16), inner)


def per_device(tokens, routes, route_gates, cotangent, w_gate, w_up, w_down):
    ep_count = lax.axis_size("ep")
    nz, nx, nc = lax.axis_size("z"), lax.axis_size("x"), lax.axis_size("core")
    tok_count, width = tokens.shape
    flat_ids = routes.reshape(-1)
    pair_count = flat_ids.shape[0]
    onehot = (flat_ids[:, None] == jnp.arange(EXPERTS, dtype=jnp.int32)[None, :]).astype(jnp.int32)
    before = jnp.cumsum(onehot, axis=0) - onehot
    slot_id = jnp.sum(before * onehot, axis=1)
    target = flat_ids * CAP + slot_id
    slot_table = (
        jnp.full((EXPERTS * CAP,), pair_count, jnp.int32)
        .at[target]
        .set(jnp.arange(pair_count, dtype=jnp.int32))
    )
    token_of_slot = slot_table // 2
    gate_flat = jnp.concatenate([route_gates.reshape(-1), jnp.zeros((1,), jnp.float32)])
    slot_gate = gate_flat[slot_table]
    xc = jnp.concatenate([tokens, cotangent], axis=1)
    xc_pad = jnp.concatenate([xc, jnp.zeros((1, 2 * width), jnp.bfloat16)], axis=0)
    sent = jnp.transpose(xc_pad[token_of_slot].reshape(ep_count, CAP, 2 * width), (0, 2, 1))
    gsend = slot_gate.reshape(ep_count, 1, CAP)
    rows = ep_count * CAP
    xc_all, gates_recv = ep_etp_gather(sent, gsend, nz, nx, nc)
    feat = nz * nx * nc * width
    xt = xc_all[..., :rows].reshape(feat, rows)
    ct = xc_all[..., rows:].reshape(feat, rows)
    slot_g = gates_recv.reshape(1, rows)
    dyt = (slot_g * ct.astype(jnp.float32)).astype(jnp.bfloat16)
    wg, wu, wd = w_gate[0], w_up[0], w_down[0]
    f32 = jnp.float32

    def dims(a, b):
        return (((a,), (b,)), ((), ()))
    gate_pre = lax.dot_general(xt, wg, dims(0, 0), preferred_element_type=f32)
    up_pre = lax.dot_general(xt, wu, dims(0, 0), preferred_element_type=f32)
    sigma = jax.nn.sigmoid(gate_pre)
    hidden = (jax.nn.silu(gate_pre) * up_pre).astype(jnp.bfloat16)
    out_t = lax.dot_general(wd, hidden, dims(0, 1), preferred_element_type=f32)
    d_hidden = lax.dot_general(dyt, wd, dims(0, 1), preferred_element_type=f32)
    d_up = (d_hidden * jax.nn.silu(gate_pre)).astype(jnp.bfloat16)
    d_gate = (d_hidden * up_pre * sigma * (1.0 + gate_pre * (1.0 - sigma))).astype(jnp.bfloat16)
    grad_down = lax.dot_general(hidden, dyt, dims(0, 1), preferred_element_type=f32)
    grad_gate_w = lax.dot_general(xt, d_gate, dims(1, 0), preferred_element_type=f32)
    grad_up_w = lax.dot_general(xt, d_up, dims(1, 0), preferred_element_type=f32)
    inner = jnp.sum(out_t * ct.astype(f32), axis=0, keepdims=True)
    part = out_t.reshape(nz, nx, nc, width // 2, 2 * rows)
    back = etp_reduce_scatter(part, inner, ep_count, CAP)
    half = width // 2
    feats_back = back[:, :width].reshape(EXPERTS, 2, half, CAP)
    feats_back = jnp.transpose(feats_back, (0, 3, 2, 1)).reshape(EXPERTS * CAP, width)
    inner_back = back[:, width].reshape(EXPERTS * CAP)
    pair_rows = feats_back[target].reshape(tok_count, 2, width)
    mixed = jnp.sum(route_gates[:, :, None] * pair_rows, axis=1).astype(jnp.bfloat16)
    grad_gates = inner_back[target].reshape(tok_count, 2)
    return (
        mixed,
        grad_gates,
        grad_gate_w.astype(jnp.bfloat16)[None],
        grad_up_w.astype(jnp.bfloat16)[None],
        grad_down.astype(jnp.bfloat16)[None],
    )


def solution(mesh):
    ep = mesh.shape["ep"]
    etp = mesh.shape["etp"]
    nz, nx, nc = sub_sizes(etp)
    devs = np.asarray(mesh.devices).reshape(ep, nz, nx, nc)
    mesh2 = Mesh(devs, ("ep",) + SUB)
    in_specs = (
        P("ep", SUB),
        P("ep", None),
        P("ep", None),
        P("ep", SUB),
        P("ep", None, SUB),
        P("ep", None, SUB),
        P("ep", SUB, None),
    )
    out_specs = (
        P("ep", SUB),
        P("ep", None),
        P("ep", None, SUB),
        P("ep", None, SUB),
        P("ep", SUB, None),
    )
    return jax.shard_map(
        per_device, mesh=mesh2, in_specs=in_specs, out_specs=out_specs, check_vma=False
    )
```

```python
import functools

import jax
import jax.numpy as jnp
import numpy as np
from jax import lax
from jax.experimental import pallas as pl
from jax.experimental.pallas import tpu as pltpu
from jax.sharding import Mesh
from jax.sharding import PartitionSpec as P

EXPERTS = 8
CAP = 24
SUB = ("z", "x", "core")
MESH_ID = pl.DeviceIdType.MESH


def sub_sizes(etp):
    if etp % 8 == 0:
        return (etp // 8, 4, 2)
    return (etp, 1, 1)


def _coords():
    return (lax.axis_index("ep"), lax.axis_index("z"), lax.axis_index("x"), lax.axis_index("core"))


def _barrier(ne, nz, nx, nc, with_ep):
    e, z, x, c = _coords()
    barrier = pltpu.get_barrier_semaphore()
    count = 0
    for d in range(1, nz):
        pl.semaphore_signal(barrier, inc=1, device_id=(e, (z + d) % nz, x, c), device_id_type=MESH_ID)
        count += 1
    for d in range(1, nx):
        pl.semaphore_signal(barrier, inc=1, device_id=(e, z, (x + d) % nx, c), device_id_type=MESH_ID)
        count += 1
    for d in range(1, nc):
        pl.semaphore_signal(barrier, inc=1, device_id=(e, z, x, (c + d) % nc), device_id_type=MESH_ID)
        count += 1
    if with_ep:
        for d in range(1, ne):
            pl.semaphore_signal(barrier, inc=1, device_id=((e + d) % ne, z, x, c), device_id_type=MESH_ID)
            count += 1
    pl.semaphore_wait(barrier, count)


def _gather_kernel(ne, nz, nx, nc, sent_ref, g_ref, xo_ref, go_ref, rbuf, rg, xa,
                   sem_local, send_0, rsem_0, send_a, recv_a, send_b, recv_b, send_c, recv_c):
    e, z, x, c = _coords()
    _barrier(ne, nz, nx, nc, True)
    sends = []
    own = [pltpu.make_async_copy(sent_ref.at[e], rbuf.at[e], sem_local.at[0]),
           pltpu.make_async_copy(g_ref.at[e], rg.at[e], sem_local.at[1])]
    for cp in own:
        cp.start()
    for t, (src, dst) in enumerate(((sent_ref, rbuf), (g_ref, rg))):
        for d in range(1, ne):
            cp = pltpu.make_async_remote_copy(
                src.at[(e + d) % ne], dst.at[e], send_0.at[t, d - 1], rsem_0.at[t, e],
                device_id=((e + d) % ne, z, x, c), device_id_type=MESH_ID)
            cp.start()
            sends.append(cp)
    for t, (src, dst) in enumerate(((sent_ref, rbuf), (g_ref, rg))):
        for d in range(1, ne):
            srce = (e + ne - d) % ne
            pltpu.make_async_remote_copy(
                src.at[e], dst.at[srce], send_0.at[t, d - 1], rsem_0.at[t, srce],
                device_id=(srce, z, x, c), device_id_type=MESH_ID).wait_recv()
    for cp in own:
        cp.wait()
    feats = xa.shape[0]
    blk = rbuf.shape[2]
    cols = ne * blk
    for b in range(ne):
        piece = rbuf[b]
        xa[:, b * blk:(b + 1) * blk] = piece[:feats]
        xa[:, cols + b * blk:cols + (b + 1) * blk] = piece[feats:]
        go_ref[:, b * blk:(b + 1) * blk] = rg[b]

    out = xo_ref
    local = pltpu.make_async_copy(xa, out.at[z, x, c], sem_local.at[2])
    local.start()
    for d in range(1, nz):
        cp = pltpu.make_async_remote_copy(
            xa, out.at[z, x, c], send_a.at[d - 1], recv_a.at[d - 1],
            device_id=(e, (z + d) % nz, x, c), device_id_type=MESH_ID)
        cp.start()
        sends.append(cp)

    def forward(src, zz, xs, to_x):
        if to_x:
            for dx in range(1, nx):
                cp = pltpu.make_async_remote_copy(
                    src, out.at[zz, x, c], send_b.at[dx - 1, zz], recv_b.at[dx - 1, zz],
                    device_id=(e, z, (x + dx) % nx, c), device_id_type=MESH_ID)
                cp.start()
                sends.append(cp)
        for dc in range(1, nc):
            cp = pltpu.make_async_remote_copy(
                src, out.at[zz, xs, c], send_c.at[dc - 1, xs, zz], recv_c.at[dc - 1, xs, zz],
                device_id=(e, z, x, (c + dc) % nc), device_id_type=MESH_ID)
            cp.start()
            sends.append(cp)

    forward(xa, z, x, True)
    for d in range(1, nz):
        zs = (z + nz - d) % nz
        pltpu.make_async_remote_copy(
            xa, out.at[zs, x, c], send_a.at[d - 1], recv_a.at[d - 1],
            device_id=(e, zs, x, c), device_id_type=MESH_ID).wait_recv()
        forward(out.at[zs, x, c], zs, x, True)
    for dx in range(1, nx):
        xs = (x + nx - dx) % nx
        for zz in range(nz):
            pltpu.make_async_remote_copy(
                xa, out.at[zz, xs, c], send_b.at[dx - 1, zz], recv_b.at[dx - 1, zz],
                device_id=(e, z, xs, c), device_id_type=MESH_ID).wait_recv()
            forward(out.at[zz, xs, c], zz, xs, False)
    for dc in range(1, nc):
        cs = (c + nc - dc) % nc
        for xx in range(nx):
            for zz in range(nz):
                pltpu.make_async_remote_copy(
                    xa, out.at[zz, xx, cs], send_c.at[dc - 1, xx, zz], recv_c.at[dc - 1, xx, zz],
                    device_id=(e, z, x, cs), device_id_type=MESH_ID).wait_recv()
    local.wait()
    for cp in sends:
        cp.wait_send()


def ep_etp_gather(sent, gsend, nz, nx, nc):
    ne, two_feats, blk = sent.shape
    feats = two_feats // 2
    cols = ne * blk
    vmem = pltpu.VMEM
    dma = pltpu.SemaphoreType.DMA
    shape = jax.ShapeDtypeStruct((nz, nx, nc, feats, 2 * cols), sent.dtype)
    return pl.pallas_call(
        functools.partial(_gather_kernel, ne, nz, nx, nc),
        out_shape=(shape, jax.ShapeDtypeStruct((1, cols), gsend.dtype)),
        in_specs=[pl.BlockSpec(memory_space=vmem)] * 2,
        out_specs=(pl.BlockSpec(memory_space=vmem),) * 2,
        scratch_shapes=[
            pltpu.VMEM((ne, two_feats, blk), sent.dtype),
            pltpu.VMEM((ne, 1, blk), gsend.dtype),
            pltpu.VMEM((feats, 2 * cols), sent.dtype),
            dma((3,)),
            dma((2, max(ne - 1, 1))),
            dma((2, ne)),
            dma((max(nz - 1, 1),)),
            dma((max(nz - 1, 1),)),
            dma((max(nx - 1, 1), nz)),
            dma((max(nx - 1, 1), nz)),
            dma((max(nc - 1, 1), nx, nz)),
            dma((max(nc - 1, 1), nx, nz)),
        ],
        compiler_params=pltpu.CompilerParams(collective_id=0, has_side_effects=True),
    )(sent, gsend)


def _rs_kernel(ne, nz, nx, nc, part_ref, partb_ref, inner_ref, out_ref, recv_c, acc1, acc1b, recv_b, acc2, acc2b,
               recv_a, ir_c, in1, ir_b, in2, ir_a, fin,
               sem_local, send_c, rsem_c, send_b, rsem_b, send_a, rsem_a, send_d, rsem_d):
    e, z, x, c = _coords()
    _barrier(ne, nz, nx, nc, True)
    sends = []

    def exchange(pieces, peers_of, send_sem, recv_sem):
        n = len(peers_of)
        for t, (src_of, dst) in enumerate(pieces):
            for d in range(n):
                cp = pltpu.make_async_remote_copy(
                    src_of(d), dst.at[d], send_sem.at[t, d], recv_sem.at[t, d],
                    device_id=peers_of[d][0], device_id_type=MESH_ID)
                cp.start()
                sends.append(cp)
        for t, (src_of, dst) in enumerate(pieces):
            for d in range(n):
                pltpu.make_async_remote_copy(
                    dst.at[d], dst.at[d], send_sem.at[t, d], recv_sem.at[t, d],
                    device_id=peers_of[d][1], device_id_type=MESH_ID).wait_recv()

    peers = [((e, z, x, (c + d) % nc), (e, z, x, (c + nc - d) % nc)) for d in range(1, nc)]
    exchange([(lambda d: partb_ref.at[:, :, (c + d + 1) % nc], recv_c), (lambda d: inner_ref, ir_c)],
             peers, send_c, rsem_c)

    def sum_c(i, carry):
        zi = i // nx
        xi = i % nx
        total = part_ref[zi, xi, c]
        for d in range(nc - 1):
            total = total + recv_c[d, zi, xi].astype(jnp.float32)
        acc1[zi, xi] = total
        acc1b[zi, xi] = total.astype(acc1b.dtype)
        return carry
    lax.fori_loop(0, nz * nx, sum_c, 0)
    total = inner_ref[...]
    for d in range(nc - 1):
        total = total + ir_c[d]
    in1[...] = total

    peers = [((e, z, (x + d) % nx, c), (e, z, (x + nx - d) % nx, c)) for d in range(1, nx)]
    exchange([(lambda d: acc1b.at[:, (x + d + 1) % nx], recv_b), (lambda d: in1, ir_b)],
             peers, send_b, rsem_b)

    def sum_b(zi, carry):
        total = acc1[zi, x]
        for d in range(nx - 1):
            total = total + recv_b[d, zi].astype(jnp.float32)
        acc2[zi] = total
        acc2b[zi] = total.astype(acc2b.dtype)
        return carry
    lax.fori_loop(0, nz, sum_b, 0)
    total = in1[...]
    for d in range(nx - 1):
        total = total + ir_b[d]
    in2[...] = total

    peers = [((e, (z + d) % nz, x, c), (e, (z + nz - d) % nz, x, c)) for d in range(1, nz)]
    exchange([(lambda d: acc2b.at[(z + d + 1) % nz], recv_a), (lambda d: in2, ir_a)],
             peers, send_a, rsem_a)
    total = acc2[z]
    for d in range(nz - 1):
        total = total + recv_a[d].astype(jnp.float32)
    itotal = in2[...]
    for d in range(nz - 1):
        itotal = itotal + ir_a[d]

    half = total.shape[0]
    feats = 2 * half
    blk = fin.shape[2]
    cols = ne * blk
    for b in range(ne):
        fin[b, :half, :] = total[:, b * blk:(b + 1) * blk]
        fin[b, half:feats, :] = total[:, cols + b * blk:cols + (b + 1) * blk]
        fin[b, feats:feats + 1, :] = itotal[:, b * blk:(b + 1) * blk]
        fin[b, feats + 1:, :] = jnp.zeros((fin.shape[1] - feats - 1, blk), jnp.float32)
    local = pltpu.make_async_copy(fin.at[e], out_ref.at[e], sem_local.at[0])
    local.start()
    for d in range(1, ne):
        cp = pltpu.make_async_remote_copy(
            fin.at[(e + d) % ne], out_ref.at[e], send_d.at[d - 1], rsem_d.at[e],
            device_id=((e + d) % ne, z, x, c), device_id_type=MESH_ID)
        cp.start()
        sends.append(cp)
    for d in range(1, ne):
        src = (e + ne - d) % ne
        pltpu.make_async_remote_copy(
            fin.at[e], out_ref.at[src], send_d.at[d - 1], rsem_d.at[src],
            device_id=(src, z, x, c), device_id_type=MESH_ID).wait_recv()
    local.wait()
    for cp in sends:
        cp.wait_send()


def etp_reduce_scatter(part, inner, ne, blk):
    bf16 = jnp.bfloat16
    nz, nx, nc, feats, cols = part.shape
    pad_rows = -(-(2 * feats + 1) // 8) * 8
    f32 = jnp.float32
    vmem = pltpu.VMEM
    dma = pltpu.SemaphoreType.DMA
    mc, mx, mz = max(nc - 1, 1), max(nx - 1, 1), max(nz - 1, 1)
    return pl.pallas_call(
        functools.partial(_rs_kernel, ne, nz, nx, nc),
        out_shape=jax.ShapeDtypeStruct((ne, pad_rows, blk), f32),
        in_specs=[pl.BlockSpec(memory_space=vmem)] * 3,
        out_specs=pl.BlockSpec(memory_space=vmem),
        scratch_shapes=[
            pltpu.VMEM((mc, nz, nx, feats, cols), bf16),
            pltpu.VMEM((nz, nx, feats, cols), f32),
            pltpu.VMEM((nz, nx, feats, cols), bf16),
            pltpu.VMEM((mx, nz, feats, cols), bf16),
            pltpu.VMEM((nz, feats, cols), f32),
            pltpu.VMEM((nz, feats, cols), bf16),
            pltpu.VMEM((mz, feats, cols), bf16),
            pltpu.VMEM((mc, 1, cols // 2), f32),
            pltpu.VMEM((1, cols // 2), f32),
            pltpu.VMEM((mx, 1, cols // 2), f32),
            pltpu.VMEM((1, cols // 2), f32),
            pltpu.VMEM((mz, 1, cols // 2), f32),
            pltpu.VMEM((ne, pad_rows, blk), f32),
            dma((1,)),
            dma((2, mc)),
            dma((2, mc)),
            dma((2, mx)),
            dma((2, mx)),
            dma((2, mz)),
            dma((2, mz)),
            dma((max(ne - 1, 1),)),
            dma((ne,)),
        ],
        compiler_params=pltpu.CompilerParams(collective_id=1, has_side_effects=True),
    )(part, part.astype(bf16), inner)


def per_device(tokens, routes, route_gates, cotangent, w_gate, w_up, w_down):
    ep_count = lax.axis_size("ep")
    nz, nx, nc = lax.axis_size("z"), lax.axis_size("x"), lax.axis_size("core")
    tok_count, width = tokens.shape
    flat_ids = routes.reshape(-1)
    pair_count = flat_ids.shape[0]
    onehot = (flat_ids[:, None] == jnp.arange(EXPERTS, dtype=jnp.int32)[None, :]).astype(jnp.int32)
    before = jnp.cumsum(onehot, axis=0) - onehot
    slot_id = jnp.sum(before * onehot, axis=1)
    target = flat_ids * CAP + slot_id
    slot_table = (
        jnp.full((EXPERTS * CAP,), pair_count, jnp.int32)
        .at[target]
        .set(jnp.arange(pair_count, dtype=jnp.int32))
    )
    token_of_slot = slot_table // 2
    gate_flat = jnp.concatenate([route_gates.reshape(-1), jnp.zeros((1,), jnp.float32)])
    slot_gate = gate_flat[slot_table]
    xc = jnp.concatenate([tokens, cotangent], axis=1)
    xc_pad = jnp.concatenate([xc, jnp.zeros((1, 2 * width), jnp.bfloat16)], axis=0)
    sent = jnp.transpose(xc_pad[token_of_slot].reshape(ep_count, CAP, 2 * width), (0, 2, 1))
    gsend = slot_gate.reshape(ep_count, 1, CAP)
    rows = ep_count * CAP
    xc_all, gates_recv = ep_etp_gather(sent, gsend, nz, nx, nc)
    feat = nz * nx * nc * width
    xt = xc_all[..., :rows].reshape(feat, rows)
    ct = xc_all[..., rows:].reshape(feat, rows)
    slot_g = gates_recv.reshape(1, rows)
    dyt = (slot_g * ct.astype(jnp.float32)).astype(jnp.bfloat16)
    wg, wu, wd = w_gate[0], w_up[0], w_down[0]
    f32 = jnp.float32

    def dims(a, b):
        return (((a,), (b,)), ((), ()))
    gate_pre = lax.dot_general(xt, wg, dims(0, 0), preferred_element_type=f32)
    up_pre = lax.dot_general(xt, wu, dims(0, 0), preferred_element_type=f32)
    sigma = jax.nn.sigmoid(gate_pre)
    hidden = (jax.nn.silu(gate_pre) * up_pre).astype(jnp.bfloat16)
    out_t = lax.dot_general(wd, hidden, dims(0, 1), preferred_element_type=f32)
    d_hidden = lax.dot_general(dyt, wd, dims(0, 1), preferred_element_type=f32)
    d_up = (d_hidden * jax.nn.silu(gate_pre)).astype(jnp.bfloat16)
    d_gate = (d_hidden * up_pre * sigma * (1.0 + gate_pre * (1.0 - sigma))).astype(jnp.bfloat16)
    grad_down = lax.dot_general(hidden, dyt, dims(0, 1), preferred_element_type=f32)
    grad_gate_w = lax.dot_general(xt, d_gate, dims(1, 0), preferred_element_type=f32)
    grad_up_w = lax.dot_general(xt, d_up, dims(1, 0), preferred_element_type=f32)
    wd_cot = lax.dot_general(wd, ct, dims(1, 0), preferred_element_type=f32)
    inner = jnp.sum(hidden.astype(f32) * wd_cot.T, axis=1)[None, :]
    part = out_t.reshape(nz, nx, nc, width // 2, 2 * rows)
    back = etp_reduce_scatter(part, inner, ep_count, CAP)
    half = width // 2
    feats_back = back[:, :width].reshape(EXPERTS, 2, half, CAP)
    feats_back = jnp.transpose(feats_back, (0, 3, 2, 1)).reshape(EXPERTS * CAP, width)
    inner_back = back[:, width].reshape(EXPERTS * CAP)
    pair_rows = feats_back[target].reshape(tok_count, 2, width)
    mixed = jnp.sum(route_gates[:, :, None] * pair_rows, axis=1).astype(jnp.bfloat16)
    grad_gates = inner_back[target].reshape(tok_count, 2)
    return (
        mixed,
        grad_gates,
        grad_gate_w.astype(jnp.bfloat16)[None],
        grad_up_w.astype(jnp.bfloat16)[None],
        grad_down.astype(jnp.bfloat16)[None],
    )


def solution(mesh):
    ep = mesh.shape["ep"]
    etp = mesh.shape["etp"]
    nz, nx, nc = sub_sizes(etp)
    devs = np.asarray(mesh.devices).reshape(ep, nz, nx, nc)
    mesh2 = Mesh(devs, ("ep",) + SUB)
    in_specs = (
        P("ep", SUB),
        P("ep", None),
        P("ep", None),
        P("ep", SUB),
        P("ep", None, SUB),
        P("ep", None, SUB),
        P("ep", SUB, None),
    )
    out_specs = (
        P("ep", SUB),
        P("ep", None),
        P("ep", None, SUB),
        P("ep", None, SUB),
        P("ep", SUB, None),
    )
    return jax.shard_map(
        per_device, mesh=mesh2, in_specs=in_specs, out_specs=out_specs, check_vma=False
    )
```

```python
import functools

import jax
import jax.numpy as jnp
import numpy as np
from jax import lax
from jax.experimental import pallas as pl
from jax.experimental.pallas import tpu as pltpu
from jax.sharding import Mesh
from jax.sharding import PartitionSpec as P

EXPERTS = 8
CAP = 24
SUB = ("z", "x", "core")
MESH_ID = pl.DeviceIdType.MESH


def sub_sizes(etp):
    if etp % 8 == 0:
        return (etp // 8, 4, 2)
    return (etp, 1, 1)


def _coords():
    return (lax.axis_index("ep"), lax.axis_index("z"), lax.axis_index("x"), lax.axis_index("core"))


def _barrier(ne, nz, nx, nc, with_ep):
    e, z, x, c = _coords()
    barrier = pltpu.get_barrier_semaphore()
    count = 0
    for d in range(1, nz):
        pl.semaphore_signal(barrier, inc=1, device_id=(e, (z + d) % nz, x, c), device_id_type=MESH_ID)
        count += 1
    for d in range(1, nx):
        pl.semaphore_signal(barrier, inc=1, device_id=(e, z, (x + d) % nx, c), device_id_type=MESH_ID)
        count += 1
    for d in range(1, nc):
        pl.semaphore_signal(barrier, inc=1, device_id=(e, z, x, (c + d) % nc), device_id_type=MESH_ID)
        count += 1
    if with_ep:
        for d in range(1, ne):
            pl.semaphore_signal(barrier, inc=1, device_id=((e + d) % ne, z, x, c), device_id_type=MESH_ID)
            count += 1
    pl.semaphore_wait(barrier, count)


def _gather_kernel(ne, nz, nx, nc, sent_ref, g_ref, xo_ref, go_ref, rbuf, rg, xa,
                   sem_local, send_0, rsem_0, send_a, recv_a, send_b, recv_b, send_c, recv_c):
    e, z, x, c = _coords()
    _barrier(ne, nz, nx, nc, True)
    sends = []
    own = [pltpu.make_async_copy(sent_ref.at[e], rbuf.at[e], sem_local.at[0]),
           pltpu.make_async_copy(g_ref.at[e], rg.at[e], sem_local.at[1])]
    for cp in own:
        cp.start()
    for t, (src, dst) in enumerate(((sent_ref, rbuf), (g_ref, rg))):
        for d in range(1, ne):
            cp = pltpu.make_async_remote_copy(
                src.at[(e + d) % ne], dst.at[e], send_0.at[t, d - 1], rsem_0.at[t, e],
                device_id=((e + d) % ne, z, x, c), device_id_type=MESH_ID)
            cp.start()
            sends.append(cp)
    for t, (src, dst) in enumerate(((sent_ref, rbuf), (g_ref, rg))):
        for d in range(1, ne):
            srce = (e + ne - d) % ne
            pltpu.make_async_remote_copy(
                src.at[e], dst.at[srce], send_0.at[t, d - 1], rsem_0.at[t, srce],
                device_id=(srce, z, x, c), device_id_type=MESH_ID).wait_recv()
    for cp in own:
        cp.wait()
    feats = xa.shape[0]
    blk = rbuf.shape[2]
    cols = ne * blk
    for b in range(ne):
        piece = rbuf[b]
        xa[:, b * blk:(b + 1) * blk] = piece[:feats]
        xa[:, cols + b * blk:cols + (b + 1) * blk] = piece[feats:]
        go_ref[:, b * blk:(b + 1) * blk] = rg[b]

    out = xo_ref
    local = pltpu.make_async_copy(xa, out.at[z, x, c], sem_local.at[2])
    local.start()
    for d in range(1, nz):
        cp = pltpu.make_async_remote_copy(
            xa, out.at[z, x, c], send_a.at[d - 1], recv_a.at[d - 1],
            device_id=(e, (z + d) % nz, x, c), device_id_type=MESH_ID)
        cp.start()
        sends.append(cp)

    def forward(src, zz, xs, to_x):
        if to_x:
            for dx in range(1, nx):
                cp = pltpu.make_async_remote_copy(
                    src, out.at[zz, x, c], send_b.at[dx - 1, zz], recv_b.at[dx - 1, zz],
                    device_id=(e, z, (x + dx) % nx, c), device_id_type=MESH_ID)
                cp.start()
                sends.append(cp)
        for dc in range(1, nc):
            cp = pltpu.make_async_remote_copy(
                src, out.at[zz, xs, c], send_c.at[dc - 1, xs, zz], recv_c.at[dc - 1, xs, zz],
                device_id=(e, z, x, (c + dc) % nc), device_id_type=MESH_ID)
            cp.start()
            sends.append(cp)

    forward(xa, z, x, True)
    for d in range(1, nz):
        zs = (z + nz - d) % nz
        pltpu.make_async_remote_copy(
            xa, out.at[zs, x, c], send_a.at[d - 1], recv_a.at[d - 1],
            device_id=(e, zs, x, c), device_id_type=MESH_ID).wait_recv()
        forward(out.at[zs, x, c], zs, x, True)
    for dx in range(1, nx):
        xs = (x + nx - dx) % nx
        for zz in range(nz):
            pltpu.make_async_remote_copy(
                xa, out.at[zz, xs, c], send_b.at[dx - 1, zz], recv_b.at[dx - 1, zz],
                device_id=(e, z, xs, c), device_id_type=MESH_ID).wait_recv()
            forward(out.at[zz, xs, c], zz, xs, False)
    for dc in range(1, nc):
        cs = (c + nc - dc) % nc
        for xx in range(nx):
            for zz in range(nz):
                pltpu.make_async_remote_copy(
                    xa, out.at[zz, xx, cs], send_c.at[dc - 1, xx, zz], recv_c.at[dc - 1, xx, zz],
                    device_id=(e, z, x, cs), device_id_type=MESH_ID).wait_recv()
    local.wait()
    for cp in sends:
        cp.wait_send()


def ep_etp_gather(sent, gsend, nz, nx, nc):
    ne, two_feats, blk = sent.shape
    feats = two_feats // 2
    cols = ne * blk
    vmem = pltpu.VMEM
    dma = pltpu.SemaphoreType.DMA
    shape = jax.ShapeDtypeStruct((nz, nx, nc, feats, 2 * cols), sent.dtype)
    return pl.pallas_call(
        functools.partial(_gather_kernel, ne, nz, nx, nc),
        out_shape=(shape, jax.ShapeDtypeStruct((1, cols), gsend.dtype)),
        in_specs=[pl.BlockSpec(memory_space=vmem)] * 2,
        out_specs=(pl.BlockSpec(memory_space=vmem),) * 2,
        scratch_shapes=[
            pltpu.VMEM((ne, two_feats, blk), sent.dtype),
            pltpu.VMEM((ne, 1, blk), gsend.dtype),
            pltpu.VMEM((feats, 2 * cols), sent.dtype),
            dma((3,)),
            dma((2, max(ne - 1, 1))),
            dma((2, ne)),
            dma((max(nz - 1, 1),)),
            dma((max(nz - 1, 1),)),
            dma((max(nx - 1, 1), nz)),
            dma((max(nx - 1, 1), nz)),
            dma((max(nc - 1, 1), nx, nz)),
            dma((max(nc - 1, 1), nx, nz)),
        ],
        compiler_params=pltpu.CompilerParams(collective_id=0, has_side_effects=True),
    )(sent, gsend)


def _rs_kernel(ne, nz, nx, nc, part_ref, partb_ref, inner_ref, out_ref, recv_c, acc1, acc1b, recv_b, acc2, acc2b,
               recv_a, ir_c, in1, ir_b, in2, ir_a, fin,
               sem_local, send_c, rsem_c, send_b, rsem_b, send_a, rsem_a, send_d, rsem_d):
    e, z, x, c = _coords()
    _barrier(ne, nz, nx, nc, True)
    sends = []

    def exchange(pieces, peers_of, send_sem, recv_sem):
        n = len(peers_of)
        for t, (src_of, dst) in enumerate(pieces):
            for d in range(n):
                cp = pltpu.make_async_remote_copy(
                    src_of(d), dst.at[d], send_sem.at[t, d], recv_sem.at[t, d],
                    device_id=peers_of[d][0], device_id_type=MESH_ID)
                cp.start()
                sends.append(cp)
        for t, (src_of, dst) in enumerate(pieces):
            for d in range(n):
                pltpu.make_async_remote_copy(
                    dst.at[d], dst.at[d], send_sem.at[t, d], recv_sem.at[t, d],
                    device_id=peers_of[d][1], device_id_type=MESH_ID).wait_recv()

    peers = [((e, z, x, (c + d) % nc), (e, z, x, (c + nc - d) % nc)) for d in range(1, nc)]
    exchange([(lambda d: partb_ref.at[:, :, (c + d + 1) % nc], recv_c), (lambda d: inner_ref, ir_c)],
             peers, send_c, rsem_c)

    def sum_c(i, carry):
        zi = i // nx
        xi = i % nx
        total = part_ref[zi, xi, c]
        for d in range(nc - 1):
            total = total + recv_c[d, zi, xi].astype(jnp.float32)
        acc1[zi, xi] = total
        acc1b[zi, xi] = total.astype(acc1b.dtype)
        return carry
    lax.fori_loop(0, nz * nx, sum_c, 0)
    total = inner_ref[...]
    for d in range(nc - 1):
        total = total + ir_c[d]
    in1[...] = total

    peers = [((e, z, (x + d) % nx, c), (e, z, (x + nx - d) % nx, c)) for d in range(1, nx)]
    exchange([(lambda d: acc1b.at[:, (x + d + 1) % nx], recv_b), (lambda d: in1, ir_b)],
             peers, send_b, rsem_b)

    def sum_b(zi, carry):
        total = acc1[zi, x]
        for d in range(nx - 1):
            total = total + recv_b[d, zi].astype(jnp.float32)
        acc2[zi] = total
        acc2b[zi] = total.astype(acc2b.dtype)
        return carry
    lax.fori_loop(0, nz, sum_b, 0)
    total = in1[...]
    for d in range(nx - 1):
        total = total + ir_b[d]
    in2[...] = total

    peers = [((e, (z + d) % nz, x, c), (e, (z + nz - d) % nz, x, c)) for d in range(1, nz)]
    exchange([(lambda d: acc2b.at[(z + d + 1) % nz], recv_a), (lambda d: in2, ir_a)],
             peers, send_a, rsem_a)
    total = acc2[z]
    for d in range(nz - 1):
        total = total + recv_a[d].astype(jnp.float32)
    itotal = in2[...]
    for d in range(nz - 1):
        itotal = itotal + ir_a[d]

    feats = total.shape[0]
    blk = fin.shape[2]
    for b in range(ne):
        fin[b, :feats, :] = total[:, b * blk:(b + 1) * blk]
        fin[b, feats:feats + 1, :] = itotal[:, b * blk:(b + 1) * blk]
        fin[b, feats + 1:, :] = jnp.zeros((fin.shape[1] - feats - 1, blk), jnp.float32)
    local = pltpu.make_async_copy(fin.at[e], out_ref.at[e], sem_local.at[0])
    local.start()
    for d in range(1, ne):
        cp = pltpu.make_async_remote_copy(
            fin.at[(e + d) % ne], out_ref.at[e], send_d.at[d - 1], rsem_d.at[e],
            device_id=((e + d) % ne, z, x, c), device_id_type=MESH_ID)
        cp.start()
        sends.append(cp)
    for d in range(1, ne):
        src = (e + ne - d) % ne
        pltpu.make_async_remote_copy(
            fin.at[e], out_ref.at[src], send_d.at[d - 1], rsem_d.at[src],
            device_id=(src, z, x, c), device_id_type=MESH_ID).wait_recv()
    local.wait()
    for cp in sends:
        cp.wait_send()


def etp_reduce_scatter(part, inner, ne, blk):
    bf16 = jnp.bfloat16
    nz, nx, nc, feats, cols = part.shape
    pad_rows = -(-(feats + 1) // 8) * 8
    f32 = jnp.float32
    vmem = pltpu.VMEM
    dma = pltpu.SemaphoreType.DMA
    mc, mx, mz = max(nc - 1, 1), max(nx - 1, 1), max(nz - 1, 1)
    return pl.pallas_call(
        functools.partial(_rs_kernel, ne, nz, nx, nc),
        out_shape=jax.ShapeDtypeStruct((ne, pad_rows, blk), f32),
        in_specs=[pl.BlockSpec(memory_space=vmem)] * 3,
        out_specs=pl.BlockSpec(memory_space=vmem),
        scratch_shapes=[
            pltpu.VMEM((mc, nz, nx, feats, cols), bf16),
            pltpu.VMEM((nz, nx, feats, cols), f32),
            pltpu.VMEM((nz, nx, feats, cols), bf16),
            pltpu.VMEM((mx, nz, feats, cols), bf16),
            pltpu.VMEM((nz, feats, cols), f32),
            pltpu.VMEM((nz, feats, cols), bf16),
            pltpu.VMEM((mz, feats, cols), bf16),
            pltpu.VMEM((mc, 1, cols), f32),
            pltpu.VMEM((1, cols), f32),
            pltpu.VMEM((mx, 1, cols), f32),
            pltpu.VMEM((1, cols), f32),
            pltpu.VMEM((mz, 1, cols), f32),
            pltpu.VMEM((ne, pad_rows, blk), f32),
            dma((1,)),
            dma((2, mc)),
            dma((2, mc)),
            dma((2, mx)),
            dma((2, mx)),
            dma((2, mz)),
            dma((2, mz)),
            dma((max(ne - 1, 1),)),
            dma((ne,)),
        ],
        compiler_params=pltpu.CompilerParams(collective_id=1, has_side_effects=True),
    )(part, part.astype(bf16), inner)


def per_device(tokens, routes, route_gates, cotangent, w_gate, w_up, w_down):
    ep_count = lax.axis_size("ep")
    nz, nx, nc = lax.axis_size("z"), lax.axis_size("x"), lax.axis_size("core")
    tok_count, width = tokens.shape
    flat_ids = routes.reshape(-1)
    pair_count = flat_ids.shape[0]
    onehot = (flat_ids[:, None] == jnp.arange(EXPERTS, dtype=jnp.int32)[None, :]).astype(jnp.int32)
    before = jnp.cumsum(onehot, axis=0) - onehot
    slot_id = jnp.sum(before * onehot, axis=1)
    target = flat_ids * CAP + slot_id
    slot_table = (
        jnp.full((EXPERTS * CAP,), pair_count, jnp.int32)
        .at[target]
        .set(jnp.arange(pair_count, dtype=jnp.int32))
    )
    token_of_slot = slot_table // 2
    gate_flat = jnp.concatenate([route_gates.reshape(-1), jnp.zeros((1,), jnp.float32)])
    slot_gate = gate_flat[slot_table]
    xc = jnp.concatenate([tokens, cotangent], axis=1)
    xc_pad = jnp.concatenate([xc, jnp.zeros((1, 2 * width), jnp.bfloat16)], axis=0)
    sent = jnp.transpose(xc_pad[token_of_slot].reshape(ep_count, CAP, 2 * width), (0, 2, 1))
    gsend = slot_gate.reshape(ep_count, 1, CAP)
    rows = ep_count * CAP
    xc_all, gates_recv = ep_etp_gather(sent, gsend, nz, nx, nc)
    feat = nz * nx * nc * width
    xt = xc_all[..., :rows].reshape(feat, rows)
    ct = xc_all[..., rows:].reshape(feat, rows)
    slot_g = gates_recv.reshape(1, rows)
    dyt = (slot_g * ct.astype(jnp.float32)).astype(jnp.bfloat16)
    wg, wu, wd = w_gate[0], w_up[0], w_down[0]
    f32 = jnp.float32

    def dims(a, b):
        return (((a,), (b,)), ((), ()))
    gate_pre = lax.dot_general(xt, wg, dims(0, 0), preferred_element_type=f32)
    up_pre = lax.dot_general(xt, wu, dims(0, 0), preferred_element_type=f32)
    sigma = jax.nn.sigmoid(gate_pre)
    hidden = (jax.nn.silu(gate_pre) * up_pre).astype(jnp.bfloat16)
    out_t = lax.dot_general(wd, hidden, dims(0, 1), preferred_element_type=f32)
    d_hidden = lax.dot_general(dyt, wd, dims(0, 1), preferred_element_type=f32)
    d_up = (d_hidden * jax.nn.silu(gate_pre)).astype(jnp.bfloat16)
    d_gate = (d_hidden * up_pre * sigma * (1.0 + gate_pre * (1.0 - sigma))).astype(jnp.bfloat16)
    grad_down = lax.dot_general(hidden, dyt, dims(0, 1), preferred_element_type=f32)
    grad_gate_w = lax.dot_general(xt, d_gate, dims(1, 0), preferred_element_type=f32)
    grad_up_w = lax.dot_general(xt, d_up, dims(1, 0), preferred_element_type=f32)
    wd_cot = lax.dot_general(wd, ct, dims(1, 0), preferred_element_type=f32)
    inner = jnp.sum(hidden.astype(f32) * wd_cot.T, axis=1)[None, :]
    part = out_t.reshape(nz, nx, nc, width, rows)
    back = etp_reduce_scatter(part, inner, ep_count, CAP)
    feats_back = jnp.transpose(back[:, :width], (0, 2, 1)).reshape(EXPERTS * CAP, width)
    inner_back = back[:, width].reshape(EXPERTS * CAP)
    pair_rows = feats_back[target].reshape(tok_count, 2, width)
    mixed = jnp.sum(route_gates[:, :, None] * pair_rows, axis=1).astype(jnp.bfloat16)
    grad_gates = inner_back[target].reshape(tok_count, 2)
    return (
        mixed,
        grad_gates,
        grad_gate_w.astype(jnp.bfloat16)[None],
        grad_up_w.astype(jnp.bfloat16)[None],
        grad_down.astype(jnp.bfloat16)[None],
    )


def solution(mesh):
    ep = mesh.shape["ep"]
    etp = mesh.shape["etp"]
    nz, nx, nc = sub_sizes(etp)
    devs = np.asarray(mesh.devices).reshape(ep, nz, nx, nc)
    mesh2 = Mesh(devs, ("ep",) + SUB)
    in_specs = (
        P("ep", SUB),
        P("ep", None),
        P("ep", None),
        P("ep", SUB),
        P("ep", None, SUB),
        P("ep", None, SUB),
        P("ep", SUB, None),
    )
    out_specs = (
        P("ep", SUB),
        P("ep", None),
        P("ep", None, SUB),
        P("ep", None, SUB),
        P("ep", SUB, None),
    )
    return jax.shard_map(
        per_device, mesh=mesh2, in_specs=in_specs, out_specs=out_specs, check_vma=False
    )
```

```python
import functools

import jax
import jax.numpy as jnp
import numpy as np
from jax import lax
from jax.experimental import pallas as pl
from jax.experimental.pallas import tpu as pltpu
from jax.sharding import Mesh
from jax.sharding import PartitionSpec as P

EXPERTS = 8
CAP = 24
SUB = ("z", "x", "core")
MESH_ID = pl.DeviceIdType.MESH


def sub_sizes(etp):
    if etp % 8 == 0:
        return (etp // 8, 4, 2)
    return (etp, 1, 1)


def _coords():
    return (lax.axis_index("ep"), lax.axis_index("z"), lax.axis_index("x"), lax.axis_index("core"))


def _barrier(ne, nz, nx, nc, with_ep):
    e, z, x, c = _coords()
    barrier = pltpu.get_barrier_semaphore()
    count = 0
    for d in range(1, nz):
        pl.semaphore_signal(barrier, inc=1, device_id=(e, (z + d) % nz, x, c), device_id_type=MESH_ID)
        count += 1
    for d in range(1, nx):
        pl.semaphore_signal(barrier, inc=1, device_id=(e, z, (x + d) % nx, c), device_id_type=MESH_ID)
        count += 1
    for d in range(1, nc):
        pl.semaphore_signal(barrier, inc=1, device_id=(e, z, x, (c + d) % nc), device_id_type=MESH_ID)
        count += 1
    if with_ep:
        for d in range(1, ne):
            pl.semaphore_signal(barrier, inc=1, device_id=((e + d) % ne, z, x, c), device_id_type=MESH_ID)
            count += 1
    pl.semaphore_wait(barrier, count)


def _gather_kernel(ne, nz, nx, nc, sent_ref, g_ref, xo_ref, go_ref, rbuf, rg, xa,
                   sem_local, send_0, rsem_0, send_a, recv_a, send_b, recv_b, send_c, recv_c):
    e, z, x, c = _coords()
    _barrier(ne, nz, nx, nc, True)
    sends = []
    own = [pltpu.make_async_copy(sent_ref.at[e], rbuf.at[e], sem_local.at[0]),
           pltpu.make_async_copy(g_ref.at[e], rg.at[e], sem_local.at[1])]
    for cp in own:
        cp.start()
    for t, (src, dst) in enumerate(((sent_ref, rbuf), (g_ref, rg))):
        for d in range(1, ne):
            cp = pltpu.make_async_remote_copy(
                src.at[(e + d) % ne], dst.at[e], send_0.at[t, d - 1], rsem_0.at[t, e],
                device_id=((e + d) % ne, z, x, c), device_id_type=MESH_ID)
            cp.start()
            sends.append(cp)
    for t, (src, dst) in enumerate(((sent_ref, rbuf), (g_ref, rg))):
        for d in range(1, ne):
            srce = (e + ne - d) % ne
            pltpu.make_async_remote_copy(
                src.at[e], dst.at[srce], send_0.at[t, d - 1], rsem_0.at[t, srce],
                device_id=(srce, z, x, c), device_id_type=MESH_ID).wait_recv()
    for cp in own:
        cp.wait()
    feats = xa.shape[0]
    blk = rbuf.shape[2]
    cols = ne * blk
    for b in range(ne):
        piece = rbuf[b]
        xa[:, b * blk:(b + 1) * blk] = piece[:feats]
        xa[:, cols + b * blk:cols + (b + 1) * blk] = piece[feats:]
        go_ref[:, b * blk:(b + 1) * blk] = rg[b]

    out = xo_ref
    local = pltpu.make_async_copy(xa, out.at[z, x, c], sem_local.at[2])
    local.start()
    for d in range(1, nz):
        cp = pltpu.make_async_remote_copy(
            xa, out.at[z, x, c], send_a.at[d - 1], recv_a.at[d - 1],
            device_id=(e, (z + d) % nz, x, c), device_id_type=MESH_ID)
        cp.start()
        sends.append(cp)

    def forward(src, zz, xs, to_x):
        if to_x:
            for dx in range(1, nx):
                cp = pltpu.make_async_remote_copy(
                    src, out.at[zz, x, c], send_b.at[dx - 1, zz], recv_b.at[dx - 1, zz],
                    device_id=(e, z, (x + dx) % nx, c), device_id_type=MESH_ID)
                cp.start()
                sends.append(cp)
        for dc in range(1, nc):
            cp = pltpu.make_async_remote_copy(
                src, out.at[zz, xs, c], send_c.at[dc - 1, xs, zz], recv_c.at[dc - 1, xs, zz],
                device_id=(e, z, x, (c + dc) % nc), device_id_type=MESH_ID)
            cp.start()
            sends.append(cp)

    forward(xa, z, x, True)
    for d in range(1, nz):
        zs = (z + nz - d) % nz
        pltpu.make_async_remote_copy(
            xa, out.at[zs, x, c], send_a.at[d - 1], recv_a.at[d - 1],
            device_id=(e, zs, x, c), device_id_type=MESH_ID).wait_recv()
        forward(out.at[zs, x, c], zs, x, True)
    for dx in range(1, nx):
        xs = (x + nx - dx) % nx
        for zz in range(nz):
            pltpu.make_async_remote_copy(
                xa, out.at[zz, xs, c], send_b.at[dx - 1, zz], recv_b.at[dx - 1, zz],
                device_id=(e, z, xs, c), device_id_type=MESH_ID).wait_recv()
            forward(out.at[zz, xs, c], zz, xs, False)
    for dc in range(1, nc):
        cs = (c + nc - dc) % nc
        for xx in range(nx):
            for zz in range(nz):
                pltpu.make_async_remote_copy(
                    xa, out.at[zz, xx, cs], send_c.at[dc - 1, xx, zz], recv_c.at[dc - 1, xx, zz],
                    device_id=(e, z, x, cs), device_id_type=MESH_ID).wait_recv()
    local.wait()
    for cp in sends:
        cp.wait_send()


def ep_etp_gather(sent, gsend, nz, nx, nc):
    ne, two_feats, blk = sent.shape
    feats = two_feats // 2
    cols = ne * blk
    vmem = pltpu.VMEM
    dma = pltpu.SemaphoreType.DMA
    shape = jax.ShapeDtypeStruct((nz, nx, nc, feats, 2 * cols), sent.dtype)
    return pl.pallas_call(
        functools.partial(_gather_kernel, ne, nz, nx, nc),
        out_shape=(shape, jax.ShapeDtypeStruct((1, cols), gsend.dtype)),
        in_specs=[pl.BlockSpec(memory_space=vmem)] * 2,
        out_specs=(pl.BlockSpec(memory_space=vmem),) * 2,
        scratch_shapes=[
            pltpu.VMEM((ne, two_feats, blk), sent.dtype),
            pltpu.VMEM((ne, 1, blk), gsend.dtype),
            pltpu.VMEM((feats, 2 * cols), sent.dtype),
            dma((3,)),
            dma((2, max(ne - 1, 1))),
            dma((2, ne)),
            dma((max(nz - 1, 1),)),
            dma((max(nz - 1, 1),)),
            dma((max(nx - 1, 1), nz)),
            dma((max(nx - 1, 1), nz)),
            dma((max(nc - 1, 1), nx, nz)),
            dma((max(nc - 1, 1), nx, nz)),
        ],
        compiler_params=pltpu.CompilerParams(collective_id=0, has_side_effects=True),
    )(sent, gsend)


def _rs_kernel(ne, nz, nx, nc, part_ref, partb_ref, inner_ref, out_ref, recv_c, acc1, acc1b, recv_b, acc2, acc2b,
               recv_a, ir_c, in1, ir_b, in2, ir_a, fin,
               sem_local, send_c, rsem_c, send_b, rsem_b, send_a, rsem_a, send_d, rsem_d):
    e, z, x, c = _coords()
    _barrier(ne, nz, nx, nc, True)
    sends = []

    def exchange(pieces, peers_of, send_sem, recv_sem):
        n = len(peers_of)
        for t, (src_of, dst) in enumerate(pieces):
            for d in range(n):
                cp = pltpu.make_async_remote_copy(
                    src_of(d), dst.at[d], send_sem.at[t, d], recv_sem.at[t, d],
                    device_id=peers_of[d][0], device_id_type=MESH_ID)
                cp.start()
                sends.append(cp)
        for t, (src_of, dst) in enumerate(pieces):
            for d in range(n):
                pltpu.make_async_remote_copy(
                    dst.at[d], dst.at[d], send_sem.at[t, d], recv_sem.at[t, d],
                    device_id=peers_of[d][1], device_id_type=MESH_ID).wait_recv()

    order = [(x + k) % nx for k in range(1, nx)] + [x]
    for d in range(1, nc):
        cpeer = (e, z, x, (c + d) % nc)
        for k, xx in enumerate(order):
            cp = pltpu.make_async_remote_copy(
                partb_ref.at[:, xx, (c + d) % nc], recv_c.at[d - 1, :, xx], send_c.at[d - 1, k], rsem_c.at[d - 1, k],
                device_id=cpeer, device_id_type=MESH_ID)
            cp.start()
            sends.append(cp)
        cp = pltpu.make_async_remote_copy(
            inner_ref, ir_c.at[d - 1], send_c.at[d - 1, nx], rsem_c.at[d - 1, nx],
            device_id=cpeer, device_id_type=MESH_ID)
        cp.start()
        sends.append(cp)
    for k, xx in enumerate(order):
        for d in range(1, nc):
            src_peer = (e, z, x, (c + nc - d) % nc)
            pltpu.make_async_remote_copy(
                recv_c.at[d - 1, :, xx], recv_c.at[d - 1, :, xx], send_c.at[d - 1, k], rsem_c.at[d - 1, k],
                device_id=src_peer, device_id_type=MESH_ID).wait_recv()

        def sum_c(zi, carry, xx=xx):
            total = part_ref[zi, xx, c]
            for d in range(nc - 1):
                total = total + recv_c[d, zi, xx].astype(jnp.float32)
            acc1[zi, xx] = total
            acc1b[zi, xx] = total.astype(acc1b.dtype)
            return carry
        lax.fori_loop(0, nz, sum_c, 0)
        if k < nx - 1:
            cp = pltpu.make_async_remote_copy(
                acc1b.at[:, xx], recv_b.at[k], send_b.at[0, k], rsem_b.at[0, k],
                device_id=(e, z, xx, c), device_id_type=MESH_ID)
            cp.start()
            sends.append(cp)
    for d in range(1, nc):
        pltpu.make_async_remote_copy(
            ir_c.at[d - 1], ir_c.at[d - 1], send_c.at[d - 1, nx], rsem_c.at[d - 1, nx],
            device_id=(e, z, x, (c + nc - d) % nc), device_id_type=MESH_ID).wait_recv()
    total = inner_ref[...]
    for d in range(nc - 1):
        total = total + ir_c[d]
    in1[...] = total

    for k in range(nx - 1):
        cp = pltpu.make_async_remote_copy(
            in1, ir_b.at[k], send_b.at[1, k], rsem_b.at[1, k],
            device_id=(e, z, (x + k + 1) % nx, c), device_id_type=MESH_ID)
        cp.start()
        sends.append(cp)
    for k in range(nx - 1):
        xs = (x + nx - k - 1) % nx
        pltpu.make_async_remote_copy(
            recv_b.at[k], recv_b.at[k], send_b.at[0, k], rsem_b.at[0, k],
            device_id=(e, z, xs, c), device_id_type=MESH_ID).wait_recv()
        pltpu.make_async_remote_copy(
            ir_b.at[k], ir_b.at[k], send_b.at[1, k], rsem_b.at[1, k],
            device_id=(e, z, xs, c), device_id_type=MESH_ID).wait_recv()

    def sum_b(zi, carry):
        total = acc1[zi, x]
        for d in range(nx - 1):
            total = total + recv_b[d, zi].astype(jnp.float32)
        acc2[zi] = total
        acc2b[zi] = total.astype(acc2b.dtype)
        return carry
    lax.fori_loop(0, nz, sum_b, 0)
    total = in1[...]
    for d in range(nx - 1):
        total = total + ir_b[d]
    in2[...] = total

    peers = [((e, (z + d) % nz, x, c), (e, (z + nz - d) % nz, x, c)) for d in range(1, nz)]
    exchange([(lambda d: acc2b.at[(z + d + 1) % nz], recv_a), (lambda d: in2, ir_a)],
             peers, send_a, rsem_a)
    total = acc2[z]
    for d in range(nz - 1):
        total = total + recv_a[d].astype(jnp.float32)
    itotal = in2[...]
    for d in range(nz - 1):
        itotal = itotal + ir_a[d]

    half = total.shape[0]
    feats = 2 * half
    blk = fin.shape[2]
    cols = ne * blk
    for b in range(ne):
        fin[b, :half, :] = total[:, b * blk:(b + 1) * blk]
        fin[b, half:feats, :] = total[:, cols + b * blk:cols + (b + 1) * blk]
        fin[b, feats:feats + 1, :] = itotal[:, b * blk:(b + 1) * blk]
        fin[b, feats + 1:, :] = jnp.zeros((fin.shape[1] - feats - 1, blk), jnp.float32)
    local = pltpu.make_async_copy(fin.at[e], out_ref.at[e], sem_local.at[0])
    local.start()
    for d in range(1, ne):
        cp = pltpu.make_async_remote_copy(
            fin.at[(e + d) % ne], out_ref.at[e], send_d.at[d - 1], rsem_d.at[e],
            device_id=((e + d) % ne, z, x, c), device_id_type=MESH_ID)
        cp.start()
        sends.append(cp)
    for d in range(1, ne):
        src = (e + ne - d) % ne
        pltpu.make_async_remote_copy(
            fin.at[e], out_ref.at[src], send_d.at[d - 1], rsem_d.at[src],
            device_id=(src, z, x, c), device_id_type=MESH_ID).wait_recv()
    local.wait()
    for cp in sends:
        cp.wait_send()


def etp_reduce_scatter(part, inner, ne, blk):
    bf16 = jnp.bfloat16
    nz, nx, nc, feats, cols = part.shape
    pad_rows = -(-(2 * feats + 1) // 8) * 8
    f32 = jnp.float32
    vmem = pltpu.VMEM
    dma = pltpu.SemaphoreType.DMA
    mc, mx, mz = max(nc - 1, 1), max(nx - 1, 1), max(nz - 1, 1)
    return pl.pallas_call(
        functools.partial(_rs_kernel, ne, nz, nx, nc),
        out_shape=jax.ShapeDtypeStruct((ne, pad_rows, blk), f32),
        in_specs=[pl.BlockSpec(memory_space=vmem)] * 3,
        out_specs=pl.BlockSpec(memory_space=vmem),
        scratch_shapes=[
            pltpu.VMEM((mc, nz, nx, feats, cols), bf16),
            pltpu.VMEM((nz, nx, feats, cols), f32),
            pltpu.VMEM((nz, nx, feats, cols), bf16),
            pltpu.VMEM((mx, nz, feats, cols), bf16),
            pltpu.VMEM((nz, feats, cols), f32),
            pltpu.VMEM((nz, feats, cols), bf16),
            pltpu.VMEM((mz, feats, cols), bf16),
            pltpu.VMEM((mc, 1, cols // 2), f32),
            pltpu.VMEM((1, cols // 2), f32),
            pltpu.VMEM((mx, 1, cols // 2), f32),
            pltpu.VMEM((1, cols // 2), f32),
            pltpu.VMEM((mz, 1, cols // 2), f32),
            pltpu.VMEM((ne, pad_rows, blk), f32),
            dma((1,)),
            dma((mc, nx + 1)),
            dma((mc, nx + 1)),
            dma((2, mx)),
            dma((2, mx)),
            dma((2, mz)),
            dma((2, mz)),
            dma((max(ne - 1, 1),)),
            dma((ne,)),
        ],
        compiler_params=pltpu.CompilerParams(collective_id=1, has_side_effects=True),
    )(part, part.astype(bf16), inner)


def per_device(tokens, routes, route_gates, cotangent, w_gate, w_up, w_down):
    ep_count = lax.axis_size("ep")
    nz, nx, nc = lax.axis_size("z"), lax.axis_size("x"), lax.axis_size("core")
    tok_count, width = tokens.shape
    flat_ids = routes.reshape(-1)
    pair_count = flat_ids.shape[0]
    onehot = (flat_ids[:, None] == jnp.arange(EXPERTS, dtype=jnp.int32)[None, :]).astype(jnp.int32)
    before = jnp.cumsum(onehot, axis=0) - onehot
    slot_id = jnp.sum(before * onehot, axis=1)
    target = flat_ids * CAP + slot_id
    slot_table = (
        jnp.full((EXPERTS * CAP,), pair_count, jnp.int32)
        .at[target]
        .set(jnp.arange(pair_count, dtype=jnp.int32))
    )
    token_of_slot = slot_table // 2
    gate_flat = jnp.concatenate([route_gates.reshape(-1), jnp.zeros((1,), jnp.float32)])
    slot_gate = gate_flat[slot_table]
    xc = jnp.concatenate([tokens, cotangent], axis=1)
    xc_pad = jnp.concatenate([xc, jnp.zeros((1, 2 * width), jnp.bfloat16)], axis=0)
    sent = jnp.transpose(xc_pad[token_of_slot].reshape(ep_count, CAP, 2 * width), (0, 2, 1))
    gsend = slot_gate.reshape(ep_count, 1, CAP)
    rows = ep_count * CAP
    xc_all, gates_recv = ep_etp_gather(sent, gsend, nz, nx, nc)
    feat = nz * nx * nc * width
    xt = xc_all[..., :rows].reshape(feat, rows)
    ct = xc_all[..., rows:].reshape(feat, rows)
    slot_g = gates_recv.reshape(1, rows)
    dyt = (slot_g * ct.astype(jnp.float32)).astype(jnp.bfloat16)
    wg, wu, wd = w_gate[0], w_up[0], w_down[0]
    f32 = jnp.float32

    def dims(a, b):
        return (((a,), (b,)), ((), ()))
    gate_pre = lax.dot_general(xt, wg, dims(0, 0), preferred_element_type=f32)
    up_pre = lax.dot_general(xt, wu, dims(0, 0), preferred_element_type=f32)
    sigma = jax.nn.sigmoid(gate_pre)
    hidden = (jax.nn.silu(gate_pre) * up_pre).astype(jnp.bfloat16)
    out_t = lax.dot_general(wd, hidden, dims(0, 1), preferred_element_type=f32)
    d_hidden = lax.dot_general(dyt, wd, dims(0, 1), preferred_element_type=f32)
    d_up = (d_hidden * jax.nn.silu(gate_pre)).astype(jnp.bfloat16)
    d_gate = (d_hidden * up_pre * sigma * (1.0 + gate_pre * (1.0 - sigma))).astype(jnp.bfloat16)
    grad_down = lax.dot_general(hidden, dyt, dims(0, 1), preferred_element_type=f32)
    grad_gate_w = lax.dot_general(xt, d_gate, dims(1, 0), preferred_element_type=f32)
    grad_up_w = lax.dot_general(xt, d_up, dims(1, 0), preferred_element_type=f32)
    wd_cot = lax.dot_general(wd, ct, dims(1, 0), preferred_element_type=f32)
    inner = jnp.sum(hidden.astype(f32) * wd_cot.T, axis=1)[None, :]
    part = out_t.reshape(nz, nx, nc, width // 2, 2 * rows)
    back = etp_reduce_scatter(part, inner, ep_count, CAP)
    half = width // 2
    feats_back = back[:, :width].reshape(EXPERTS, 2, half, CAP)
    feats_back = jnp.transpose(feats_back, (0, 3, 2, 1)).reshape(EXPERTS * CAP, width)
    inner_back = back[:, width].reshape(EXPERTS * CAP)
    pair_rows = feats_back[target].reshape(tok_count, 2, width)
    mixed = jnp.sum(route_gates[:, :, None] * pair_rows, axis=1).astype(jnp.bfloat16)
    grad_gates = inner_back[target].reshape(tok_count, 2)
    return (
        mixed,
        grad_gates,
        grad_gate_w.astype(jnp.bfloat16)[None],
        grad_up_w.astype(jnp.bfloat16)[None],
        grad_down.astype(jnp.bfloat16)[None],
    )


def solution(mesh):
    ep = mesh.shape["ep"]
    etp = mesh.shape["etp"]
    nz, nx, nc = sub_sizes(etp)
    devs = np.asarray(mesh.devices).reshape(ep, nz, nx, nc)
    mesh2 = Mesh(devs, ("ep",) + SUB)
    in_specs = (
        P("ep", SUB),
        P("ep", None),
        P("ep", None),
        P("ep", SUB),
        P("ep", None, SUB),
        P("ep", None, SUB),
        P("ep", SUB, None),
    )
    out_specs = (
        P("ep", SUB),
        P("ep", None),
        P("ep", None, SUB),
        P("ep", None, SUB),
        P("ep", SUB, None),
    )
    return jax.shard_map(
        per_device, mesh=mesh2, in_specs=in_specs, out_specs=out_specs, check_vma=False
    )
```

```python
import functools

import jax
import jax.numpy as jnp
import numpy as np
from jax import lax
from jax.experimental import pallas as pl
from jax.experimental.pallas import tpu as pltpu
from jax.sharding import Mesh
from jax.sharding import PartitionSpec as P

EXPERTS = 8
CAP = 24
SUB = ("z", "x", "core")
MESH_ID = pl.DeviceIdType.MESH


def sub_sizes(etp):
    if etp % 8 == 0:
        return (etp // 8, 4, 2)
    return (etp, 1, 1)


def _coords():
    return (lax.axis_index("ep"), lax.axis_index("z"), lax.axis_index("x"), lax.axis_index("core"))


def _barrier(ne, nz, nx, nc, with_ep):
    e, z, x, c = _coords()
    barrier = pltpu.get_barrier_semaphore()
    count = 0
    for d in range(1, nz):
        pl.semaphore_signal(barrier, inc=1, device_id=(e, (z + d) % nz, x, c), device_id_type=MESH_ID)
        count += 1
    for d in range(1, nx):
        pl.semaphore_signal(barrier, inc=1, device_id=(e, z, (x + d) % nx, c), device_id_type=MESH_ID)
        count += 1
    for d in range(1, nc):
        pl.semaphore_signal(barrier, inc=1, device_id=(e, z, x, (c + d) % nc), device_id_type=MESH_ID)
        count += 1
    if with_ep:
        for d in range(1, ne):
            pl.semaphore_signal(barrier, inc=1, device_id=((e + d) % ne, z, x, c), device_id_type=MESH_ID)
            count += 1
    pl.semaphore_wait(barrier, count)


def _gather_kernel(ne, nz, nx, nc, sent_ref, g_ref, xo_ref, go_ref, rbuf, rg, xa,
                   sem_local, send_0, rsem_0, send_a, recv_a, send_b, recv_b, send_c, recv_c):
    e, z, x, c = _coords()
    _barrier(ne, nz, nx, nc, True)
    sends = []
    own = [pltpu.make_async_copy(sent_ref.at[e], rbuf.at[e], sem_local.at[0]),
           pltpu.make_async_copy(g_ref.at[e], rg.at[e], sem_local.at[1])]
    for cp in own:
        cp.start()
    for t, (src, dst) in enumerate(((sent_ref, rbuf), (g_ref, rg))):
        for d in range(1, ne):
            cp = pltpu.make_async_remote_copy(
                src.at[(e + d) % ne], dst.at[e], send_0.at[t, d - 1], rsem_0.at[t, e],
                device_id=((e + d) % ne, z, x, c), device_id_type=MESH_ID)
            cp.start()
            sends.append(cp)
    for t, (src, dst) in enumerate(((sent_ref, rbuf), (g_ref, rg))):
        for d in range(1, ne):
            srce = (e + ne - d) % ne
            pltpu.make_async_remote_copy(
                src.at[e], dst.at[srce], send_0.at[t, d - 1], rsem_0.at[t, srce],
                device_id=(srce, z, x, c), device_id_type=MESH_ID).wait_recv()
    for cp in own:
        cp.wait()
    feats = xa.shape[0]
    blk = rbuf.shape[2]
    cols = ne * blk
    for b in range(ne):
        piece = rbuf[b]
        xa[:, b * blk:(b + 1) * blk] = piece[:feats]
        xa[:, cols + b * blk:cols + (b + 1) * blk] = piece[feats:]
        go_ref[:, b * blk:(b + 1) * blk] = rg[b]

    out = xo_ref
    local = pltpu.make_async_copy(xa, out.at[z, x, c], sem_local.at[2])
    local.start()
    for d in range(1, nz):
        cp = pltpu.make_async_remote_copy(
            xa, out.at[z, x, c], send_a.at[d - 1], recv_a.at[d - 1],
            device_id=(e, (z + d) % nz, x, c), device_id_type=MESH_ID)
        cp.start()
        sends.append(cp)

    def forward(src, zz, xs, to_x):
        if to_x:
            for dx in range(1, nx):
                cp = pltpu.make_async_remote_copy(
                    src, out.at[zz, x, c], send_b.at[dx - 1, zz], recv_b.at[dx - 1, zz],
                    device_id=(e, z, (x + dx) % nx, c), device_id_type=MESH_ID)
                cp.start()
                sends.append(cp)
        for dc in range(1, nc):
            cp = pltpu.make_async_remote_copy(
                src, out.at[zz, xs, c], send_c.at[dc - 1, xs, zz], recv_c.at[dc - 1, xs, zz],
                device_id=(e, z, x, (c + dc) % nc), device_id_type=MESH_ID)
            cp.start()
            sends.append(cp)

    forward(xa, z, x, True)
    for d in range(1, nz):
        zs = (z + nz - d) % nz
        pltpu.make_async_remote_copy(
            xa, out.at[zs, x, c], send_a.at[d - 1], recv_a.at[d - 1],
            device_id=(e, zs, x, c), device_id_type=MESH_ID).wait_recv()
        forward(out.at[zs, x, c], zs, x, True)
    for dx in range(1, nx):
        xs = (x + nx - dx) % nx
        for zz in range(nz):
            pltpu.make_async_remote_copy(
                xa, out.at[zz, xs, c], send_b.at[dx - 1, zz], recv_b.at[dx - 1, zz],
                device_id=(e, z, xs, c), device_id_type=MESH_ID).wait_recv()
            forward(out.at[zz, xs, c], zz, xs, False)
    for dc in range(1, nc):
        cs = (c + nc - dc) % nc
        for xx in range(nx):
            for zz in range(nz):
                pltpu.make_async_remote_copy(
                    xa, out.at[zz, xx, cs], send_c.at[dc - 1, xx, zz], recv_c.at[dc - 1, xx, zz],
                    device_id=(e, z, x, cs), device_id_type=MESH_ID).wait_recv()
    local.wait()
    for cp in sends:
        cp.wait_send()


def ep_etp_gather(sent, gsend, nz, nx, nc):
    ne, two_feats, blk = sent.shape
    feats = two_feats // 2
    cols = ne * blk
    vmem = pltpu.VMEM
    dma = pltpu.SemaphoreType.DMA
    shape = jax.ShapeDtypeStruct((nz, nx, nc, feats, 2 * cols), sent.dtype)
    return pl.pallas_call(
        functools.partial(_gather_kernel, ne, nz, nx, nc),
        out_shape=(shape, jax.ShapeDtypeStruct((1, cols), gsend.dtype)),
        in_specs=[pl.BlockSpec(memory_space=vmem)] * 2,
        out_specs=(pl.BlockSpec(memory_space=vmem),) * 2,
        scratch_shapes=[
            pltpu.VMEM((ne, two_feats, blk), sent.dtype),
            pltpu.VMEM((ne, 1, blk), gsend.dtype),
            pltpu.VMEM((feats, 2 * cols), sent.dtype),
            dma((3,)),
            dma((2, max(ne - 1, 1))),
            dma((2, ne)),
            dma((max(nz - 1, 1),)),
            dma((max(nz - 1, 1),)),
            dma((max(nx - 1, 1), nz)),
            dma((max(nx - 1, 1), nz)),
            dma((max(nc - 1, 1), nx, nz)),
            dma((max(nc - 1, 1), nx, nz)),
        ],
        compiler_params=pltpu.CompilerParams(collective_id=0, has_side_effects=True),
    )(sent, gsend)


def _rs_kernel(ne, nz, nx, nc, part_ref, partb_ref, inner_ref, out_ref, recv_c, acc1, acc1b, recv_b, acc2, acc2b,
               recv_a, ir_c, in1, ir_b, in2, ir_a, fin,
               sem_local, send_c, rsem_c, send_b, rsem_b, send_a, rsem_a, send_d, rsem_d):
    e, z, x, c = _coords()
    _barrier(ne, nz, nx, nc, True)
    sends = []

    def exchange(pieces, peers_of, send_sem, recv_sem):
        n = len(peers_of)
        for t, (src_of, dst) in enumerate(pieces):
            for d in range(n):
                cp = pltpu.make_async_remote_copy(
                    src_of(d), dst.at[d], send_sem.at[t, d], recv_sem.at[t, d],
                    device_id=peers_of[d][0], device_id_type=MESH_ID)
                cp.start()
                sends.append(cp)
        for t, (src_of, dst) in enumerate(pieces):
            for d in range(n):
                pltpu.make_async_remote_copy(
                    dst.at[d], dst.at[d], send_sem.at[t, d], recv_sem.at[t, d],
                    device_id=peers_of[d][1], device_id_type=MESH_ID).wait_recv()

    order = [(x + k) % nx for k in range(1, nx)] + [x]
    for d in range(1, nc):
        cpeer = (e, z, x, (c + d) % nc)
        for k, xx in enumerate(order):
            cp = pltpu.make_async_remote_copy(
                partb_ref.at[:, xx, (c + d) % nc], recv_c.at[d - 1, :, xx], send_c.at[d - 1, k], rsem_c.at[d - 1, k],
                device_id=cpeer, device_id_type=MESH_ID)
            cp.start()
            sends.append(cp)
        cp = pltpu.make_async_remote_copy(
            inner_ref, ir_c.at[d - 1], send_c.at[d - 1, nx], rsem_c.at[d - 1, nx],
            device_id=cpeer, device_id_type=MESH_ID)
        cp.start()
        sends.append(cp)
    for k, xx in enumerate(order):
        for d in range(1, nc):
            src_peer = (e, z, x, (c + nc - d) % nc)
            pltpu.make_async_remote_copy(
                recv_c.at[d - 1, :, xx], recv_c.at[d - 1, :, xx], send_c.at[d - 1, k], rsem_c.at[d - 1, k],
                device_id=src_peer, device_id_type=MESH_ID).wait_recv()

        def sum_c(zi, carry, xx=xx):
            total = part_ref[zi, xx, c]
            for d in range(nc - 1):
                total = total + recv_c[d, zi, xx].astype(jnp.float32)
            acc1[zi, xx] = total
            acc1b[zi, xx] = total.astype(acc1b.dtype)
            return carry
        lax.fori_loop(0, nz, sum_c, 0)
        if k < nx - 1:
            cp = pltpu.make_async_remote_copy(
                acc1b.at[:, xx], recv_b.at[k], send_b.at[0, k], rsem_b.at[0, k],
                device_id=(e, z, xx, c), device_id_type=MESH_ID)
            cp.start()
            sends.append(cp)
    for d in range(1, nc):
        pltpu.make_async_remote_copy(
            ir_c.at[d - 1], ir_c.at[d - 1], send_c.at[d - 1, nx], rsem_c.at[d - 1, nx],
            device_id=(e, z, x, (c + nc - d) % nc), device_id_type=MESH_ID).wait_recv()
    total = inner_ref[...]
    for d in range(nc - 1):
        total = total + ir_c[d]
    in1[...] = total

    for k in range(nx - 1):
        cp = pltpu.make_async_remote_copy(
            in1, ir_b.at[k], send_b.at[1, k], rsem_b.at[1, k],
            device_id=(e, z, (x + k + 1) % nx, c), device_id_type=MESH_ID)
        cp.start()
        sends.append(cp)
    for k in range(nx - 1):
        xs = (x + nx - k - 1) % nx
        pltpu.make_async_remote_copy(
            recv_b.at[k], recv_b.at[k], send_b.at[0, k], rsem_b.at[0, k],
            device_id=(e, z, xs, c), device_id_type=MESH_ID).wait_recv()
        pltpu.make_async_remote_copy(
            ir_b.at[k], ir_b.at[k], send_b.at[1, k], rsem_b.at[1, k],
            device_id=(e, z, xs, c), device_id_type=MESH_ID).wait_recv()

    def sum_b(zi, carry):
        total = acc1[zi, x]
        for d in range(nx - 1):
            total = total + recv_b[d, zi].astype(jnp.float32)
        acc2[zi] = total
        acc2b[zi] = total.astype(acc2b.dtype)
        return carry
    lax.fori_loop(0, nz, sum_b, 0)
    total = in1[...]
    for d in range(nx - 1):
        total = total + ir_b[d]
    in2[...] = total

    peers = [((e, (z + d) % nz, x, c), (e, (z + nz - d) % nz, x, c)) for d in range(1, nz)]
    exchange([(lambda d: acc2b.at[(z + d + 1) % nz], recv_a), (lambda d: in2, ir_a)],
             peers, send_a, rsem_a)
    total = acc2[z]
    for d in range(nz - 1):
        total = total + recv_a[d].astype(jnp.float32)
    itotal = in2[...]
    for d in range(nz - 1):
        itotal = itotal + ir_a[d]

    half = total.shape[0]
    feats = 2 * half
    blk = fin.shape[2]
    cols = ne * blk
    for b in range(ne):
        fin[b, :half, :] = total[:, b * blk:(b + 1) * blk]
        fin[b, half:feats, :] = total[:, cols + b * blk:cols + (b + 1) * blk]
        fin[b, feats:feats + 1, :] = itotal[:, b * blk:(b + 1) * blk]
        fin[b, feats + 1:, :] = jnp.zeros((fin.shape[1] - feats - 1, blk), jnp.float32)
    local = pltpu.make_async_copy(fin.at[e], out_ref.at[e], sem_local.at[0])
    local.start()
    for d in range(1, ne):
        cp = pltpu.make_async_remote_copy(
            fin.at[(e + d) % ne], out_ref.at[e], send_d.at[d - 1], rsem_d.at[e],
            device_id=((e + d) % ne, z, x, c), device_id_type=MESH_ID)
        cp.start()
        sends.append(cp)
    for d in range(1, ne):
        src = (e + ne - d) % ne
        pltpu.make_async_remote_copy(
            fin.at[e], out_ref.at[src], send_d.at[d - 1], rsem_d.at[src],
            device_id=(src, z, x, c), device_id_type=MESH_ID).wait_recv()
    local.wait()
    for cp in sends:
        cp.wait_send()


def etp_reduce_scatter(part, inner, ne, blk):
    bf16 = jnp.bfloat16
    nz, nx, nc, feats, cols = part.shape
    pad_rows = -(-(2 * feats + 1) // 8) * 8
    f32 = jnp.float32
    vmem = pltpu.VMEM
    dma = pltpu.SemaphoreType.DMA
    mc, mx, mz = max(nc - 1, 1), max(nx - 1, 1), max(nz - 1, 1)
    return pl.pallas_call(
        functools.partial(_rs_kernel, ne, nz, nx, nc),
        out_shape=jax.ShapeDtypeStruct((ne, pad_rows, blk), f32),
        in_specs=[pl.BlockSpec(memory_space=vmem)] * 3,
        out_specs=pl.BlockSpec(memory_space=vmem),
        scratch_shapes=[
            pltpu.VMEM((mc, nz, nx, feats, cols), bf16),
            pltpu.VMEM((nz, nx, feats, cols), f32),
            pltpu.VMEM((nz, nx, feats, cols), bf16),
            pltpu.VMEM((mx, nz, feats, cols), bf16),
            pltpu.VMEM((nz, feats, cols), f32),
            pltpu.VMEM((nz, feats, cols), bf16),
            pltpu.VMEM((mz, feats, cols), bf16),
            pltpu.VMEM((mc, 1, cols // 2), f32),
            pltpu.VMEM((1, cols // 2), f32),
            pltpu.VMEM((mx, 1, cols // 2), f32),
            pltpu.VMEM((1, cols // 2), f32),
            pltpu.VMEM((mz, 1, cols // 2), f32),
            pltpu.VMEM((ne, pad_rows, blk), f32),
            dma((1,)),
            dma((mc, nx + 1)),
            dma((mc, nx + 1)),
            dma((2, mx)),
            dma((2, mx)),
            dma((2, mz)),
            dma((2, mz)),
            dma((max(ne - 1, 1),)),
            dma((ne,)),
        ],
        compiler_params=pltpu.CompilerParams(collective_id=1, has_side_effects=True),
    )(part, part.astype(bf16), inner)


def per_device(tokens, routes, route_gates, cotangent, w_gate, w_up, w_down):
    ep_count = lax.axis_size("ep")
    nz, nx, nc = lax.axis_size("z"), lax.axis_size("x"), lax.axis_size("core")
    tok_count, width = tokens.shape
    flat_ids = routes.reshape(-1)
    pair_count = flat_ids.shape[0]
    onehot = (flat_ids[:, None] == jnp.arange(EXPERTS, dtype=jnp.int32)[None, :]).astype(jnp.int32)
    before = jnp.cumsum(onehot, axis=0) - onehot
    slot_id = jnp.sum(before * onehot, axis=1)
    target = flat_ids * CAP + slot_id
    slot_table = (
        jnp.full((EXPERTS * CAP,), pair_count, jnp.int32)
        .at[target]
        .set(jnp.arange(pair_count, dtype=jnp.int32))
    )
    token_of_slot = slot_table // 2
    gate_flat = jnp.concatenate([route_gates.reshape(-1), jnp.zeros((1,), jnp.float32)])
    slot_gate = gate_flat[slot_table]
    xc = jnp.concatenate([tokens, cotangent], axis=1)
    xc_pad = jnp.concatenate([xc, jnp.zeros((1, 2 * width), jnp.bfloat16)], axis=0)
    sent = jnp.transpose(xc_pad[token_of_slot].reshape(ep_count, CAP, 2 * width), (0, 2, 1))
    gsend = slot_gate.reshape(ep_count, 1, CAP)
    rows = ep_count * CAP
    xc_all, gates_recv = ep_etp_gather(sent, gsend, nz, nx, nc)
    feat = nz * nx * nc * width
    xt = xc_all[..., :rows].reshape(feat, rows)
    ct = xc_all[..., rows:].reshape(feat, rows)
    slot_g = gates_recv.reshape(1, rows)
    dyt = (slot_g * ct.astype(jnp.float32)).astype(jnp.bfloat16)
    wg, wu, wd = w_gate[0], w_up[0], w_down[0]
    f32 = jnp.float32

    def dims(a, b):
        return (((a,), (b,)), ((), ()))
    gate_pre = lax.dot_general(xt, wg, dims(0, 0), preferred_element_type=f32)
    up_pre = lax.dot_general(xt, wu, dims(0, 0), preferred_element_type=f32)
    sigma = jax.nn.sigmoid(gate_pre)
    hidden = (jax.nn.silu(gate_pre) * up_pre).astype(jnp.bfloat16)
    out_t = lax.dot_general(wd, hidden, dims(0, 1), preferred_element_type=f32)
    d_hidden = lax.dot_general(dyt, wd, dims(0, 1), preferred_element_type=f32)
    d_up = (d_hidden * jax.nn.silu(gate_pre)).astype(jnp.bfloat16)
    d_gate = (d_hidden * up_pre * sigma * (1.0 + gate_pre * (1.0 - sigma))).astype(jnp.bfloat16)
    grad_down = lax.dot_general(hidden, dyt, dims(0, 1), preferred_element_type=f32)
    hid = d_gate.shape[1]
    grad_gu = lax.dot_general(xt, jnp.concatenate([d_gate, d_up], axis=1), dims(1, 0), preferred_element_type=f32)
    grad_gate_w = grad_gu[:, :hid]
    grad_up_w = grad_gu[:, hid:]
    wd_cot = lax.dot_general(wd, ct, dims(1, 0), preferred_element_type=f32)
    inner = jnp.sum(hidden.astype(f32) * wd_cot.T, axis=1)[None, :]
    part = out_t.reshape(nz, nx, nc, width // 2, 2 * rows)
    back = etp_reduce_scatter(part, inner, ep_count, CAP)
    half = width // 2
    feats_back = back[:, :width].reshape(EXPERTS, 2, half, CAP)
    feats_back = jnp.transpose(feats_back, (0, 3, 2, 1)).reshape(EXPERTS * CAP, width)
    inner_back = back[:, width].reshape(EXPERTS * CAP)
    pair_rows = feats_back[target].reshape(tok_count, 2, width)
    mixed = jnp.sum(route_gates[:, :, None] * pair_rows, axis=1).astype(jnp.bfloat16)
    grad_gates = inner_back[target].reshape(tok_count, 2)
    return (
        mixed,
        grad_gates,
        grad_gate_w.astype(jnp.bfloat16)[None],
        grad_up_w.astype(jnp.bfloat16)[None],
        grad_down.astype(jnp.bfloat16)[None],
    )


def solution(mesh):
    ep = mesh.shape["ep"]
    etp = mesh.shape["etp"]
    nz, nx, nc = sub_sizes(etp)
    devs = np.asarray(mesh.devices).reshape(ep, nz, nx, nc)
    mesh2 = Mesh(devs, ("ep",) + SUB)
    in_specs = (
        P("ep", SUB),
        P("ep", None),
        P("ep", None),
        P("ep", SUB),
        P("ep", None, SUB),
        P("ep", None, SUB),
        P("ep", SUB, None),
    )
    out_specs = (
        P("ep", SUB),
        P("ep", None),
        P("ep", None, SUB),
        P("ep", None, SUB),
        P("ep", SUB, None),
    )
    return jax.shard_map(
        per_device, mesh=mesh2, in_specs=in_specs, out_specs=out_specs, check_vma=False
    )
```

```python
import functools

import jax
import jax.numpy as jnp
import numpy as np
from jax import lax
from jax.experimental import pallas as pl
from jax.experimental.pallas import tpu as pltpu
from jax.sharding import Mesh
from jax.sharding import PartitionSpec as P

EXPERTS = 8
CAP = 24
SUB = ("z", "x", "core")
MESH_ID = pl.DeviceIdType.MESH


def sub_sizes(etp):
    if etp % 8 == 0:
        return (etp // 8, 4, 2)
    return (etp, 1, 1)


def _coords():
    return (lax.axis_index("ep"), lax.axis_index("z"), lax.axis_index("x"), lax.axis_index("core"))


def _barrier(ne, nz, nx, nc, with_ep):
    e, z, x, c = _coords()
    barrier = pltpu.get_barrier_semaphore()
    count = 0
    for d in range(1, nz):
        pl.semaphore_signal(barrier, inc=1, device_id=(e, (z + d) % nz, x, c), device_id_type=MESH_ID)
        count += 1
    for d in range(1, nx):
        pl.semaphore_signal(barrier, inc=1, device_id=(e, z, (x + d) % nx, c), device_id_type=MESH_ID)
        count += 1
    for d in range(1, nc):
        pl.semaphore_signal(barrier, inc=1, device_id=(e, z, x, (c + d) % nc), device_id_type=MESH_ID)
        count += 1
    if with_ep:
        for d in range(1, ne):
            pl.semaphore_signal(barrier, inc=1, device_id=((e + d) % ne, z, x, c), device_id_type=MESH_ID)
            count += 1
    pl.semaphore_wait(barrier, count)


def _gather_kernel(ne, nz, nx, nc, sent_ref, g_ref, xo_ref, go_ref, rbuf, rg, xa,
                   sem_local, send_0, rsem_0, send_a, recv_a, send_b, recv_b, send_c, recv_c):
    e, z, x, c = _coords()
    _barrier(ne, nz, nx, nc, True)
    sends = []
    own = [pltpu.make_async_copy(sent_ref.at[e], rbuf.at[e], sem_local.at[0]),
           pltpu.make_async_copy(g_ref.at[e], rg.at[e], sem_local.at[1])]
    for cp in own:
        cp.start()
    for t, (src, dst) in enumerate(((sent_ref, rbuf), (g_ref, rg))):
        for d in range(1, ne):
            cp = pltpu.make_async_remote_copy(
                src.at[(e + d) % ne], dst.at[e], send_0.at[t, d - 1], rsem_0.at[t, e],
                device_id=((e + d) % ne, z, x, c), device_id_type=MESH_ID)
            cp.start()
            sends.append(cp)
    for t, (src, dst) in enumerate(((sent_ref, rbuf), (g_ref, rg))):
        for d in range(1, ne):
            srce = (e + ne - d) % ne
            pltpu.make_async_remote_copy(
                src.at[e], dst.at[srce], send_0.at[t, d - 1], rsem_0.at[t, srce],
                device_id=(srce, z, x, c), device_id_type=MESH_ID).wait_recv()
    for cp in own:
        cp.wait()
    feats = xa.shape[0]
    blk = rbuf.shape[2]
    cols = ne * blk
    for b in range(ne):
        piece = rbuf[b]
        xa[:, b * blk:(b + 1) * blk] = piece[:feats]
        xa[:, cols + b * blk:cols + (b + 1) * blk] = piece[feats:]
        go_ref[:, b * blk:(b + 1) * blk] = rg[b]

    out = xo_ref
    local = pltpu.make_async_copy(xa, out.at[z, x, c], sem_local.at[2])
    local.start()
    for d in range(1, nz):
        cp = pltpu.make_async_remote_copy(
            xa, out.at[z, x, c], send_a.at[d - 1], recv_a.at[d - 1],
            device_id=(e, (z + d) % nz, x, c), device_id_type=MESH_ID)
        cp.start()
        sends.append(cp)

    def forward(src, zz, xs, to_x):
        if to_x:
            for dx in range(1, nx):
                cp = pltpu.make_async_remote_copy(
                    src, out.at[zz, x, c], send_b.at[dx - 1, zz], recv_b.at[dx - 1, zz],
                    device_id=(e, z, (x + dx) % nx, c), device_id_type=MESH_ID)
                cp.start()
                sends.append(cp)
        for dc in range(1, nc):
            cp = pltpu.make_async_remote_copy(
                src, out.at[zz, xs, c], send_c.at[dc - 1, xs, zz], recv_c.at[dc - 1, xs, zz],
                device_id=(e, z, x, (c + dc) % nc), device_id_type=MESH_ID)
            cp.start()
            sends.append(cp)

    forward(xa, z, x, True)
    for d in range(1, nz):
        zs = (z + nz - d) % nz
        pltpu.make_async_remote_copy(
            xa, out.at[zs, x, c], send_a.at[d - 1], recv_a.at[d - 1],
            device_id=(e, zs, x, c), device_id_type=MESH_ID).wait_recv()
        forward(out.at[zs, x, c], zs, x, True)
    for dx in range(1, nx):
        xs = (x + nx - dx) % nx
        for zz in range(nz):
            pltpu.make_async_remote_copy(
                xa, out.at[zz, xs, c], send_b.at[dx - 1, zz], recv_b.at[dx - 1, zz],
                device_id=(e, z, xs, c), device_id_type=MESH_ID).wait_recv()
            forward(out.at[zz, xs, c], zz, xs, False)
    for dc in range(1, nc):
        cs = (c + nc - dc) % nc
        for xx in range(nx):
            for zz in range(nz):
                pltpu.make_async_remote_copy(
                    xa, out.at[zz, xx, cs], send_c.at[dc - 1, xx, zz], recv_c.at[dc - 1, xx, zz],
                    device_id=(e, z, x, cs), device_id_type=MESH_ID).wait_recv()
    local.wait()
    for cp in sends:
        cp.wait_send()


def ep_etp_gather(sent, gsend, nz, nx, nc):
    ne, two_feats, blk = sent.shape
    feats = two_feats // 2
    cols = ne * blk
    vmem = pltpu.VMEM
    dma = pltpu.SemaphoreType.DMA
    shape = jax.ShapeDtypeStruct((nz, nx, nc, feats, 2 * cols), sent.dtype)
    return pl.pallas_call(
        functools.partial(_gather_kernel, ne, nz, nx, nc),
        out_shape=(shape, jax.ShapeDtypeStruct((1, cols), gsend.dtype)),
        in_specs=[pl.BlockSpec(memory_space=vmem)] * 2,
        out_specs=(pl.BlockSpec(memory_space=vmem),) * 2,
        scratch_shapes=[
            pltpu.VMEM((ne, two_feats, blk), sent.dtype),
            pltpu.VMEM((ne, 1, blk), gsend.dtype),
            pltpu.VMEM((feats, 2 * cols), sent.dtype),
            dma((3,)),
            dma((2, max(ne - 1, 1))),
            dma((2, ne)),
            dma((max(nz - 1, 1),)),
            dma((max(nz - 1, 1),)),
            dma((max(nx - 1, 1), nz)),
            dma((max(nx - 1, 1), nz)),
            dma((max(nc - 1, 1), nx, nz)),
            dma((max(nc - 1, 1), nx, nz)),
        ],
        compiler_params=pltpu.CompilerParams(collective_id=0, has_side_effects=True),
    )(sent, gsend)


def _rs_kernel(ne, nz, nx, nc, part_ref, partb_ref, inner_ref, out_ref, recv_c, acc1, acc1b, recv_b, acc2, acc2b,
               recv_a, ir_c, in1, ir_b, in2, ir_a, fin,
               sem_local, send_c, rsem_c, send_b, rsem_b, send_a, rsem_a, send_d, rsem_d):
    e, z, x, c = _coords()
    _barrier(ne, nz, nx, nc, True)
    sends = []

    def exchange(pieces, peers_of, send_sem, recv_sem):
        n = len(peers_of)
        for t, (src_of, dst) in enumerate(pieces):
            for d in range(n):
                cp = pltpu.make_async_remote_copy(
                    src_of(d), dst.at[d], send_sem.at[t, d], recv_sem.at[t, d],
                    device_id=peers_of[d][0], device_id_type=MESH_ID)
                cp.start()
                sends.append(cp)
        for t, (src_of, dst) in enumerate(pieces):
            for d in range(n):
                pltpu.make_async_remote_copy(
                    dst.at[d], dst.at[d], send_sem.at[t, d], recv_sem.at[t, d],
                    device_id=peers_of[d][1], device_id_type=MESH_ID).wait_recv()

    order = [(x + k) % nx for k in range(1, nx)] + [x]
    for d in range(1, nc):
        cpeer = (e, z, x, (c + d) % nc)
        for k, xx in enumerate(order):
            cp = pltpu.make_async_remote_copy(
                partb_ref.at[:, xx, (c + d) % nc], recv_c.at[d - 1, :, xx], send_c.at[d - 1, k], rsem_c.at[d - 1, k],
                device_id=cpeer, device_id_type=MESH_ID)
            cp.start()
            sends.append(cp)
        cp = pltpu.make_async_remote_copy(
            inner_ref, ir_c.at[d - 1], send_c.at[d - 1, nx], rsem_c.at[d - 1, nx],
            device_id=cpeer, device_id_type=MESH_ID)
        cp.start()
        sends.append(cp)
    for k, xx in enumerate(order):
        for d in range(1, nc):
            src_peer = (e, z, x, (c + nc - d) % nc)
            pltpu.make_async_remote_copy(
                recv_c.at[d - 1, :, xx], recv_c.at[d - 1, :, xx], send_c.at[d - 1, k], rsem_c.at[d - 1, k],
                device_id=src_peer, device_id_type=MESH_ID).wait_recv()

        def sum_c(zi, carry, xx=xx):
            total = part_ref[zi, xx, c]
            for d in range(nc - 1):
                total = total + recv_c[d, zi, xx].astype(jnp.float32)
            acc1[zi, xx] = total
            acc1b[zi, xx] = total.astype(acc1b.dtype)
            return carry
        lax.fori_loop(0, nz, sum_c, 0)
        if k < nx - 1:
            cp = pltpu.make_async_remote_copy(
                acc1b.at[:, xx], recv_b.at[k], send_b.at[0, k], rsem_b.at[0, k],
                device_id=(e, z, xx, c), device_id_type=MESH_ID)
            cp.start()
            sends.append(cp)
    for d in range(1, nc):
        pltpu.make_async_remote_copy(
            ir_c.at[d - 1], ir_c.at[d - 1], send_c.at[d - 1, nx], rsem_c.at[d - 1, nx],
            device_id=(e, z, x, (c + nc - d) % nc), device_id_type=MESH_ID).wait_recv()
    total = inner_ref[...]
    for d in range(nc - 1):
        total = total + ir_c[d]
    in1[...] = total

    for k in range(nx - 1):
        cp = pltpu.make_async_remote_copy(
            in1, ir_b.at[k], send_b.at[1, k], rsem_b.at[1, k],
            device_id=(e, z, (x + k + 1) % nx, c), device_id_type=MESH_ID)
        cp.start()
        sends.append(cp)
    for k in range(nx - 1):
        xs = (x + nx - k - 1) % nx
        pltpu.make_async_remote_copy(
            recv_b.at[k], recv_b.at[k], send_b.at[0, k], rsem_b.at[0, k],
            device_id=(e, z, xs, c), device_id_type=MESH_ID).wait_recv()
        pltpu.make_async_remote_copy(
            ir_b.at[k], ir_b.at[k], send_b.at[1, k], rsem_b.at[1, k],
            device_id=(e, z, xs, c), device_id_type=MESH_ID).wait_recv()

    def sum_b(zi, carry):
        total = acc1[zi, x]
        for d in range(nx - 1):
            total = total + recv_b[d, zi].astype(jnp.float32)
        acc2[zi] = total
        acc2b[zi] = total.astype(acc2b.dtype)
        return carry
    lax.fori_loop(0, nz, sum_b, 0)
    total = in1[...]
    for d in range(nx - 1):
        total = total + ir_b[d]
    in2[...] = total

    peers = [((e, (z + d) % nz, x, c), (e, (z + nz - d) % nz, x, c)) for d in range(1, nz)]
    exchange([(lambda d: acc2b.at[(z + d + 1) % nz], recv_a), (lambda d: in2, ir_a)],
             peers, send_a, rsem_a)
    total = acc2[z]
    for d in range(nz - 1):
        total = total + recv_a[d].astype(jnp.float32)
    itotal = in2[...]
    for d in range(nz - 1):
        itotal = itotal + ir_a[d]

    half = total.shape[0]
    feats = 2 * half
    blk = fin.shape[2]
    cols = ne * blk
    for b in range(ne):
        fin[b, :half, :] = total[:, b * blk:(b + 1) * blk]
        fin[b, half:feats, :] = total[:, cols + b * blk:cols + (b + 1) * blk]
        fin[b, feats:feats + 1, :] = itotal[:, b * blk:(b + 1) * blk]
        fin[b, feats + 1:, :] = jnp.zeros((fin.shape[1] - feats - 1, blk), jnp.float32)
    local = pltpu.make_async_copy(fin.at[e], out_ref.at[e], sem_local.at[0])
    local.start()
    for d in range(1, ne):
        cp = pltpu.make_async_remote_copy(
            fin.at[(e + d) % ne], out_ref.at[e], send_d.at[d - 1], rsem_d.at[e],
            device_id=((e + d) % ne, z, x, c), device_id_type=MESH_ID)
        cp.start()
        sends.append(cp)
    for d in range(1, ne):
        src = (e + ne - d) % ne
        pltpu.make_async_remote_copy(
            fin.at[e], out_ref.at[src], send_d.at[d - 1], rsem_d.at[src],
            device_id=(src, z, x, c), device_id_type=MESH_ID).wait_recv()
    local.wait()
    for cp in sends:
        cp.wait_send()


def etp_reduce_scatter(part, inner, ne, blk):
    bf16 = jnp.bfloat16
    nz, nx, nc, feats, cols = part.shape
    pad_rows = -(-(2 * feats + 1) // 8) * 8
    f32 = jnp.float32
    vmem = pltpu.VMEM
    dma = pltpu.SemaphoreType.DMA
    mc, mx, mz = max(nc - 1, 1), max(nx - 1, 1), max(nz - 1, 1)
    return pl.pallas_call(
        functools.partial(_rs_kernel, ne, nz, nx, nc),
        out_shape=jax.ShapeDtypeStruct((ne, pad_rows, blk), f32),
        in_specs=[pl.BlockSpec(memory_space=vmem)] * 3,
        out_specs=pl.BlockSpec(memory_space=vmem),
        scratch_shapes=[
            pltpu.VMEM((mc, nz, nx, feats, cols), bf16),
            pltpu.VMEM((nz, nx, feats, cols), f32),
            pltpu.VMEM((nz, nx, feats, cols), bf16),
            pltpu.VMEM((mx, nz, feats, cols), bf16),
            pltpu.VMEM((nz, feats, cols), f32),
            pltpu.VMEM((nz, feats, cols), bf16),
            pltpu.VMEM((mz, feats, cols), bf16),
            pltpu.VMEM((mc, 1, cols // 2), f32),
            pltpu.VMEM((1, cols // 2), f32),
            pltpu.VMEM((mx, 1, cols // 2), f32),
            pltpu.VMEM((1, cols // 2), f32),
            pltpu.VMEM((mz, 1, cols // 2), f32),
            pltpu.VMEM((ne, pad_rows, blk), f32),
            dma((1,)),
            dma((mc, nx + 1)),
            dma((mc, nx + 1)),
            dma((2, mx)),
            dma((2, mx)),
            dma((2, mz)),
            dma((2, mz)),
            dma((max(ne - 1, 1),)),
            dma((ne,)),
        ],
        compiler_params=pltpu.CompilerParams(collective_id=1, has_side_effects=True),
    )(part, part.astype(bf16), inner)


def per_device(tokens, routes, route_gates, cotangent, w_gate, w_up, w_down):
    ep_count = lax.axis_size("ep")
    nz, nx, nc = lax.axis_size("z"), lax.axis_size("x"), lax.axis_size("core")
    tok_count, width = tokens.shape
    flat_ids = routes.reshape(-1)
    pair_count = flat_ids.shape[0]
    onehot = (flat_ids[:, None] == jnp.arange(EXPERTS, dtype=jnp.int32)[None, :]).astype(jnp.int32)
    before = jnp.cumsum(onehot, axis=0) - onehot
    slot_id = jnp.sum(before * onehot, axis=1)
    target = flat_ids * CAP + slot_id
    slot_table = (
        jnp.full((EXPERTS * CAP,), pair_count, jnp.int32)
        .at[target]
        .set(jnp.arange(pair_count, dtype=jnp.int32))
    )
    token_of_slot = slot_table // 2
    gate_flat = jnp.concatenate([route_gates.reshape(-1), jnp.zeros((1,), jnp.float32)])
    slot_gate = gate_flat[slot_table]
    xc = jnp.concatenate([tokens, cotangent], axis=1)
    xc_pad = jnp.concatenate([xc, jnp.zeros((1, 2 * width), jnp.bfloat16)], axis=0)
    sent = jnp.transpose(xc_pad[token_of_slot].reshape(ep_count, CAP, 2 * width), (0, 2, 1))
    gsend = slot_gate.reshape(ep_count, 1, CAP)
    rows = ep_count * CAP
    xc_all, gates_recv = ep_etp_gather(sent, gsend, nz, nx, nc)
    feat = nz * nx * nc * width
    xt = xc_all[..., :rows].reshape(feat, rows)
    ct = xc_all[..., rows:].reshape(feat, rows)
    slot_g = gates_recv.reshape(1, rows)
    dyt = (slot_g * ct.astype(jnp.float32)).astype(jnp.bfloat16)
    wg, wu, wd = w_gate[0], w_up[0], w_down[0]
    f32 = jnp.float32

    def dims(a, b):
        return (((a,), (b,)), ((), ()))
    gu_pre = lax.dot_general(xt, jnp.concatenate([wg, wu], axis=1), dims(0, 0), preferred_element_type=f32)
    gate_pre = gu_pre[:, :wg.shape[1]]
    up_pre = gu_pre[:, wg.shape[1]:]
    sigma = jax.nn.sigmoid(gate_pre)
    hidden = (jax.nn.silu(gate_pre) * up_pre).astype(jnp.bfloat16)
    out_t = lax.dot_general(wd, hidden, dims(0, 1), preferred_element_type=f32)
    d_hidden = lax.dot_general(dyt, wd, dims(0, 1), preferred_element_type=f32)
    d_up = (d_hidden * jax.nn.silu(gate_pre)).astype(jnp.bfloat16)
    d_gate = (d_hidden * up_pre * sigma * (1.0 + gate_pre * (1.0 - sigma))).astype(jnp.bfloat16)
    grad_down = lax.dot_general(hidden, dyt, dims(0, 1), preferred_element_type=f32)
    hid = d_gate.shape[1]
    grad_gu = lax.dot_general(xt, jnp.concatenate([d_gate, d_up], axis=1), dims(1, 0), preferred_element_type=f32)
    grad_gate_w = grad_gu[:, :hid]
    grad_up_w = grad_gu[:, hid:]
    wd_cot = lax.dot_general(wd, ct, dims(1, 0), preferred_element_type=f32)
    inner = jnp.sum(hidden.astype(f32) * wd_cot.T, axis=1)[None, :]
    part = out_t.reshape(nz, nx, nc, width // 2, 2 * rows)
    back = etp_reduce_scatter(part, inner, ep_count, CAP)
    half = width // 2
    feats_back = back[:, :width].reshape(EXPERTS, 2, half, CAP)
    feats_back = jnp.transpose(feats_back, (0, 3, 2, 1)).reshape(EXPERTS * CAP, width)
    inner_back = back[:, width].reshape(EXPERTS * CAP)
    pair_rows = feats_back[target].reshape(tok_count, 2, width)
    mixed = jnp.sum(route_gates[:, :, None] * pair_rows, axis=1).astype(jnp.bfloat16)
    grad_gates = inner_back[target].reshape(tok_count, 2)
    return (
        mixed,
        grad_gates,
        grad_gate_w.astype(jnp.bfloat16)[None],
        grad_up_w.astype(jnp.bfloat16)[None],
        grad_down.astype(jnp.bfloat16)[None],
    )


def solution(mesh):
    ep = mesh.shape["ep"]
    etp = mesh.shape["etp"]
    nz, nx, nc = sub_sizes(etp)
    devs = np.asarray(mesh.devices).reshape(ep, nz, nx, nc)
    mesh2 = Mesh(devs, ("ep",) + SUB)
    in_specs = (
        P("ep", SUB),
        P("ep", None),
        P("ep", None),
        P("ep", SUB),
        P("ep", None, SUB),
        P("ep", None, SUB),
        P("ep", SUB, None),
    )
    out_specs = (
        P("ep", SUB),
        P("ep", None),
        P("ep", None, SUB),
        P("ep", None, SUB),
        P("ep", SUB, None),
    )
    return jax.shard_map(
        per_device, mesh=mesh2, in_specs=in_specs, out_specs=out_specs, check_vma=False
    )
```

```python
import functools

import jax
import jax.numpy as jnp
import numpy as np
from jax import lax
from jax.experimental import pallas as pl
from jax.experimental.pallas import tpu as pltpu
from jax.sharding import Mesh
from jax.sharding import PartitionSpec as P

EXPERTS = 8
CAP = 24
SUB = ("z", "x", "core")
MESH_ID = pl.DeviceIdType.MESH


def sub_sizes(etp):
    if etp % 8 == 0:
        return (etp // 8, 4, 2)
    return (etp, 1, 1)


def _coords():
    return (lax.axis_index("ep"), lax.axis_index("z"), lax.axis_index("x"), lax.axis_index("core"))


def _barrier(ne, nz, nx, nc, with_ep):
    e, z, x, c = _coords()
    barrier = pltpu.get_barrier_semaphore()
    count = 0
    for d in range(1, nz):
        pl.semaphore_signal(barrier, inc=1, device_id=(e, (z + d) % nz, x, c), device_id_type=MESH_ID)
        count += 1
    for d in range(1, nx):
        pl.semaphore_signal(barrier, inc=1, device_id=(e, z, (x + d) % nx, c), device_id_type=MESH_ID)
        count += 1
    for d in range(1, nc):
        pl.semaphore_signal(barrier, inc=1, device_id=(e, z, x, (c + d) % nc), device_id_type=MESH_ID)
        count += 1
    if with_ep:
        for d in range(1, ne):
            pl.semaphore_signal(barrier, inc=1, device_id=((e + d) % ne, z, x, c), device_id_type=MESH_ID)
            count += 1
    pl.semaphore_wait(barrier, count)


def _gather_kernel(ne, nz, nx, nc, sent_ref, g_ref, xo_ref, go_ref, rbuf, rg, xa,
                   sem_local, send_0, rsem_0, send_a, recv_a, send_b, recv_b, send_c, recv_c):
    e, z, x, c = _coords()
    _barrier(ne, nz, nx, nc, True)
    sends = []
    own = [pltpu.make_async_copy(sent_ref.at[e], rbuf.at[e], sem_local.at[0]),
           pltpu.make_async_copy(g_ref.at[e], rg.at[e], sem_local.at[1])]
    for cp in own:
        cp.start()
    for t, (src, dst) in enumerate(((sent_ref, rbuf), (g_ref, rg))):
        for d in range(1, ne):
            cp = pltpu.make_async_remote_copy(
                src.at[(e + d) % ne], dst.at[e], send_0.at[t, d - 1], rsem_0.at[t, e],
                device_id=((e + d) % ne, z, x, c), device_id_type=MESH_ID)
            cp.start()
            sends.append(cp)
    for t, (src, dst) in enumerate(((sent_ref, rbuf), (g_ref, rg))):
        for d in range(1, ne):
            srce = (e + ne - d) % ne
            pltpu.make_async_remote_copy(
                src.at[e], dst.at[srce], send_0.at[t, d - 1], rsem_0.at[t, srce],
                device_id=(srce, z, x, c), device_id_type=MESH_ID).wait_recv()
    for cp in own:
        cp.wait()
    feats = xa.shape[0]
    blk = rbuf.shape[2]
    cols = ne * blk
    for b in range(ne):
        piece = rbuf[b]
        xa[:, b * blk:(b + 1) * blk] = piece[:feats]
        xa[:, cols + b * blk:cols + (b + 1) * blk] = piece[feats:]
        go_ref[:, b * blk:(b + 1) * blk] = rg[b]

    out = xo_ref
    local = pltpu.make_async_copy(xa, out.at[z, x, c], sem_local.at[2])
    local.start()
    for d in range(1, nz):
        cp = pltpu.make_async_remote_copy(
            xa, out.at[z, x, c], send_a.at[d - 1], recv_a.at[d - 1],
            device_id=(e, (z + d) % nz, x, c), device_id_type=MESH_ID)
        cp.start()
        sends.append(cp)

    def forward(src, zz, xs, to_x):
        if to_x:
            for dx in range(1, nx):
                cp = pltpu.make_async_remote_copy(
                    src, out.at[zz, x, c], send_b.at[dx - 1, zz], recv_b.at[dx - 1, zz],
                    device_id=(e, z, (x + dx) % nx, c), device_id_type=MESH_ID)
                cp.start()
                sends.append(cp)
        for dc in range(1, nc):
            cp = pltpu.make_async_remote_copy(
                src, out.at[zz, xs, c], send_c.at[dc - 1, xs, zz], recv_c.at[dc - 1, xs, zz],
                device_id=(e, z, x, (c + dc) % nc), device_id_type=MESH_ID)
            cp.start()
            sends.append(cp)

    forward(xa, z, x, True)
    for d in range(1, nz):
        zs = (z + nz - d) % nz
        pltpu.make_async_remote_copy(
            xa, out.at[zs, x, c], send_a.at[d - 1], recv_a.at[d - 1],
            device_id=(e, zs, x, c), device_id_type=MESH_ID).wait_recv()
        forward(out.at[zs, x, c], zs, x, True)
    for dx in range(1, nx):
        xs = (x + nx - dx) % nx
        for zz in range(nz):
            pltpu.make_async_remote_copy(
                xa, out.at[zz, xs, c], send_b.at[dx - 1, zz], recv_b.at[dx - 1, zz],
                device_id=(e, z, xs, c), device_id_type=MESH_ID).wait_recv()
            forward(out.at[zz, xs, c], zz, xs, False)
    for dc in range(1, nc):
        cs = (c + nc - dc) % nc
        for xx in range(nx):
            for zz in range(nz):
                pltpu.make_async_remote_copy(
                    xa, out.at[zz, xx, cs], send_c.at[dc - 1, xx, zz], recv_c.at[dc - 1, xx, zz],
                    device_id=(e, z, x, cs), device_id_type=MESH_ID).wait_recv()
    local.wait()
    for cp in sends:
        cp.wait_send()


def ep_etp_gather(sent, gsend, nz, nx, nc):
    ne, two_feats, blk = sent.shape
    feats = two_feats // 2
    cols = ne * blk
    vmem = pltpu.VMEM
    dma = pltpu.SemaphoreType.DMA
    shape = jax.ShapeDtypeStruct((nz, nx, nc, feats, 2 * cols), sent.dtype)
    return pl.pallas_call(
        functools.partial(_gather_kernel, ne, nz, nx, nc),
        out_shape=(shape, jax.ShapeDtypeStruct((1, cols), gsend.dtype)),
        in_specs=[pl.BlockSpec(memory_space=vmem)] * 2,
        out_specs=(pl.BlockSpec(memory_space=vmem),) * 2,
        scratch_shapes=[
            pltpu.VMEM((ne, two_feats, blk), sent.dtype),
            pltpu.VMEM((ne, 1, blk), gsend.dtype),
            pltpu.VMEM((feats, 2 * cols), sent.dtype),
            dma((3,)),
            dma((2, max(ne - 1, 1))),
            dma((2, ne)),
            dma((max(nz - 1, 1),)),
            dma((max(nz - 1, 1),)),
            dma((max(nx - 1, 1), nz)),
            dma((max(nx - 1, 1), nz)),
            dma((max(nc - 1, 1), nx, nz)),
            dma((max(nc - 1, 1), nx, nz)),
        ],
        compiler_params=pltpu.CompilerParams(collective_id=0, has_side_effects=True),
    )(sent, gsend)


def _rs_kernel(ne, nz, nx, nc, part_ref, partb_ref, inner_ref, out_ref, recv_c, acc1, acc1b, recv_b, acc2, acc2b,
               recv_a, ir_c, in1, ir_b, in2, ir_a, fin,
               sem_local, send_c, rsem_c, send_b, rsem_b, send_a, rsem_a, send_d, rsem_d):
    e, z, x, c = _coords()
    _barrier(ne, nz, nx, nc, True)
    sends = []

    def exchange(pieces, peers_of, send_sem, recv_sem):
        n = len(peers_of)
        for t, (src_of, dst) in enumerate(pieces):
            for d in range(n):
                cp = pltpu.make_async_remote_copy(
                    src_of(d), dst.at[d], send_sem.at[t, d], recv_sem.at[t, d],
                    device_id=peers_of[d][0], device_id_type=MESH_ID)
                cp.start()
                sends.append(cp)
        for t, (src_of, dst) in enumerate(pieces):
            for d in range(n):
                pltpu.make_async_remote_copy(
                    dst.at[d], dst.at[d], send_sem.at[t, d], recv_sem.at[t, d],
                    device_id=peers_of[d][1], device_id_type=MESH_ID).wait_recv()

    order = [(x + k) % nx for k in range(1, nx)] + [x]
    for d in range(1, nc):
        cpeer = (e, z, x, (c + d) % nc)
        for k, xx in enumerate(order):
            cp = pltpu.make_async_remote_copy(
                partb_ref.at[:, xx, (c + d) % nc], recv_c.at[d - 1, :, xx], send_c.at[d - 1, k], rsem_c.at[d - 1, k],
                device_id=cpeer, device_id_type=MESH_ID)
            cp.start()
            sends.append(cp)
        cp = pltpu.make_async_remote_copy(
            inner_ref, ir_c.at[d - 1], send_c.at[d - 1, nx], rsem_c.at[d - 1, nx],
            device_id=cpeer, device_id_type=MESH_ID)
        cp.start()
        sends.append(cp)
    for k, xx in enumerate(order):
        for d in range(1, nc):
            src_peer = (e, z, x, (c + nc - d) % nc)
            pltpu.make_async_remote_copy(
                recv_c.at[d - 1, :, xx], recv_c.at[d - 1, :, xx], send_c.at[d - 1, k], rsem_c.at[d - 1, k],
                device_id=src_peer, device_id_type=MESH_ID).wait_recv()

        def sum_c(zi, carry, xx=xx):
            total = part_ref[zi, xx, c]
            for d in range(nc - 1):
                total = total + recv_c[d, zi, xx].astype(jnp.float32)
            acc1[zi, xx] = total
            acc1b[zi, xx] = total.astype(acc1b.dtype)
            return carry
        lax.fori_loop(0, nz, sum_c, 0)
        if k < nx - 1:
            cp = pltpu.make_async_remote_copy(
                acc1b.at[:, xx], recv_b.at[k], send_b.at[0, k], rsem_b.at[0, k],
                device_id=(e, z, xx, c), device_id_type=MESH_ID)
            cp.start()
            sends.append(cp)
    for d in range(1, nc):
        pltpu.make_async_remote_copy(
            ir_c.at[d - 1], ir_c.at[d - 1], send_c.at[d - 1, nx], rsem_c.at[d - 1, nx],
            device_id=(e, z, x, (c + nc - d) % nc), device_id_type=MESH_ID).wait_recv()
    total = inner_ref[...]
    for d in range(nc - 1):
        total = total + ir_c[d]
    in1[...] = total

    for k in range(nx - 1):
        cp = pltpu.make_async_remote_copy(
            in1, ir_b.at[k], send_b.at[1, k], rsem_b.at[1, k],
            device_id=(e, z, (x + k + 1) % nx, c), device_id_type=MESH_ID)
        cp.start()
        sends.append(cp)
    for k in range(nx - 1):
        xs = (x + nx - k - 1) % nx
        pltpu.make_async_remote_copy(
            recv_b.at[k], recv_b.at[k], send_b.at[0, k], rsem_b.at[0, k],
            device_id=(e, z, xs, c), device_id_type=MESH_ID).wait_recv()
        pltpu.make_async_remote_copy(
            ir_b.at[k], ir_b.at[k], send_b.at[1, k], rsem_b.at[1, k],
            device_id=(e, z, xs, c), device_id_type=MESH_ID).wait_recv()

    def sum_b(zi, carry):
        total = acc1[zi, x]
        for d in range(nx - 1):
            total = total + recv_b[d, zi].astype(jnp.float32)
        acc2[zi] = total
        acc2b[zi] = total.astype(acc2b.dtype)
        return carry
    lax.fori_loop(0, nz, sum_b, 0)
    total = in1[...]
    for d in range(nx - 1):
        total = total + ir_b[d]
    in2[...] = total

    peers = [((e, (z + d) % nz, x, c), (e, (z + nz - d) % nz, x, c)) for d in range(1, nz)]
    exchange([(lambda d: acc2b.at[(z + d + 1) % nz], recv_a), (lambda d: in2, ir_a)],
             peers, send_a, rsem_a)
    total = acc2[z]
    for d in range(nz - 1):
        total = total + recv_a[d].astype(jnp.float32)
    itotal = in2[...]
    for d in range(nz - 1):
        itotal = itotal + ir_a[d]

    half = total.shape[0]
    feats = 2 * half
    blk = fin.shape[2]
    cols = ne * blk
    for b in range(ne):
        fin[b, :half, :] = total[:, b * blk:(b + 1) * blk]
        fin[b, half:feats, :] = total[:, cols + b * blk:cols + (b + 1) * blk]
        fin[b, feats:feats + 1, :] = itotal[:, b * blk:(b + 1) * blk]
        fin[b, feats + 1:, :] = jnp.zeros((fin.shape[1] - feats - 1, blk), jnp.float32)
    local = pltpu.make_async_copy(fin.at[e], out_ref.at[e], sem_local.at[0])
    local.start()
    for d in range(1, ne):
        cp = pltpu.make_async_remote_copy(
            fin.at[(e + d) % ne], out_ref.at[e], send_d.at[d - 1], rsem_d.at[e],
            device_id=((e + d) % ne, z, x, c), device_id_type=MESH_ID)
        cp.start()
        sends.append(cp)
    for d in range(1, ne):
        src = (e + ne - d) % ne
        pltpu.make_async_remote_copy(
            fin.at[e], out_ref.at[src], send_d.at[d - 1], rsem_d.at[src],
            device_id=(src, z, x, c), device_id_type=MESH_ID).wait_recv()
    local.wait()
    for cp in sends:
        cp.wait_send()


def etp_reduce_scatter(part, inner, ne, blk):
    bf16 = jnp.bfloat16
    nz, nx, nc, feats, cols = part.shape
    pad_rows = -(-(2 * feats + 1) // 8) * 8
    f32 = jnp.float32
    vmem = pltpu.VMEM
    dma = pltpu.SemaphoreType.DMA
    mc, mx, mz = max(nc - 1, 1), max(nx - 1, 1), max(nz - 1, 1)
    return pl.pallas_call(
        functools.partial(_rs_kernel, ne, nz, nx, nc),
        out_shape=jax.ShapeDtypeStruct((ne, pad_rows, blk), f32),
        in_specs=[pl.BlockSpec(memory_space=vmem)] * 3,
        out_specs=pl.BlockSpec(memory_space=vmem),
        scratch_shapes=[
            pltpu.VMEM((mc, nz, nx, feats, cols), bf16),
            pltpu.VMEM((nz, nx, feats, cols), f32),
            pltpu.VMEM((nz, nx, feats, cols), bf16),
            pltpu.VMEM((mx, nz, feats, cols), bf16),
            pltpu.VMEM((nz, feats, cols), f32),
            pltpu.VMEM((nz, feats, cols), bf16),
            pltpu.VMEM((mz, feats, cols), bf16),
            pltpu.VMEM((mc, 1, cols // 2), f32),
            pltpu.VMEM((1, cols // 2), f32),
            pltpu.VMEM((mx, 1, cols // 2), f32),
            pltpu.VMEM((1, cols // 2), f32),
            pltpu.VMEM((mz, 1, cols // 2), f32),
            pltpu.VMEM((ne, pad_rows, blk), f32),
            dma((1,)),
            dma((mc, nx + 1)),
            dma((mc, nx + 1)),
            dma((2, mx)),
            dma((2, mx)),
            dma((2, mz)),
            dma((2, mz)),
            dma((max(ne - 1, 1),)),
            dma((ne,)),
        ],
        compiler_params=pltpu.CompilerParams(collective_id=1, has_side_effects=True),
    )(part, part.astype(bf16), inner)


def per_device(tokens, routes, route_gates, cotangent, w_gate, w_up, w_down):
    ep_count = lax.axis_size("ep")
    nz, nx, nc = lax.axis_size("z"), lax.axis_size("x"), lax.axis_size("core")
    tok_count, width = tokens.shape
    flat_ids = routes.reshape(-1)
    pair_count = flat_ids.shape[0]
    onehot = (flat_ids[:, None] == jnp.arange(EXPERTS, dtype=jnp.int32)[None, :]).astype(jnp.int32)
    before = jnp.cumsum(onehot, axis=0) - onehot
    slot_id = jnp.sum(before * onehot, axis=1)
    target = flat_ids * CAP + slot_id
    slot_table = (
        jnp.full((EXPERTS * CAP,), pair_count, jnp.int32)
        .at[target]
        .set(jnp.arange(pair_count, dtype=jnp.int32))
    )
    token_of_slot = slot_table // 2
    gate_flat = jnp.concatenate([route_gates.reshape(-1), jnp.zeros((1,), jnp.float32)])
    slot_gate = gate_flat[slot_table]
    xc = jnp.concatenate([tokens, cotangent], axis=1)
    xc_pad = jnp.concatenate([xc, jnp.zeros((1, 2 * width), jnp.bfloat16)], axis=0)
    sent = jnp.transpose(xc_pad[token_of_slot].reshape(ep_count, CAP, 2 * width), (0, 2, 1))
    gsend = slot_gate.reshape(ep_count, 1, CAP)
    rows = ep_count * CAP
    xc_all, gates_recv = ep_etp_gather(sent, gsend, nz, nx, nc)
    feat = nz * nx * nc * width
    xt = xc_all[..., :rows].reshape(feat, rows)
    ct = xc_all[..., rows:].reshape(feat, rows)
    slot_g = gates_recv.reshape(1, rows)
    dyt = (slot_g * ct.astype(jnp.float32)).astype(jnp.bfloat16)
    wg, wu, wd = w_gate[0], w_up[0], w_down[0]
    f32 = jnp.float32

    def dims(a, b):
        return (((a,), (b,)), ((), ()))
    gu_pre = lax.dot_general(xt, jnp.concatenate([wg, wu], axis=1), dims(0, 0), preferred_element_type=f32)
    gate_pre = gu_pre[:, :wg.shape[1]]
    up_pre = gu_pre[:, wg.shape[1]:]
    sigma = jax.nn.sigmoid(gate_pre)
    hidden = (jax.nn.silu(gate_pre) * up_pre).astype(jnp.bfloat16)
    out_t = lax.dot_general(wd, hidden, dims(0, 1), preferred_element_type=f32)
    dh_wc = lax.dot_general(jnp.concatenate([dyt, ct], axis=1), wd, dims(0, 1), preferred_element_type=f32)
    d_hidden = dh_wc[:rows]
    d_up = (d_hidden * jax.nn.silu(gate_pre)).astype(jnp.bfloat16)
    d_gate = (d_hidden * up_pre * sigma * (1.0 + gate_pre * (1.0 - sigma))).astype(jnp.bfloat16)
    grad_down = lax.dot_general(hidden, dyt, dims(0, 1), preferred_element_type=f32)
    hid = d_gate.shape[1]
    grad_gu = lax.dot_general(xt, jnp.concatenate([d_gate, d_up], axis=1), dims(1, 0), preferred_element_type=f32)
    grad_gate_w = grad_gu[:, :hid]
    grad_up_w = grad_gu[:, hid:]
    inner = jnp.sum(hidden.astype(f32) * dh_wc[rows:], axis=1)[None, :]
    part = out_t.reshape(nz, nx, nc, width // 2, 2 * rows)
    back = etp_reduce_scatter(part, inner, ep_count, CAP)
    half = width // 2
    feats_back = back[:, :width].reshape(EXPERTS, 2, half, CAP)
    feats_back = jnp.transpose(feats_back, (0, 3, 2, 1)).reshape(EXPERTS * CAP, width)
    inner_back = back[:, width].reshape(EXPERTS * CAP)
    pair_rows = feats_back[target].reshape(tok_count, 2, width)
    mixed = jnp.sum(route_gates[:, :, None] * pair_rows, axis=1).astype(jnp.bfloat16)
    grad_gates = inner_back[target].reshape(tok_count, 2)
    return (
        mixed,
        grad_gates,
        grad_gate_w.astype(jnp.bfloat16)[None],
        grad_up_w.astype(jnp.bfloat16)[None],
        grad_down.astype(jnp.bfloat16)[None],
    )


def solution(mesh):
    ep = mesh.shape["ep"]
    etp = mesh.shape["etp"]
    nz, nx, nc = sub_sizes(etp)
    devs = np.asarray(mesh.devices).reshape(ep, nz, nx, nc)
    mesh2 = Mesh(devs, ("ep",) + SUB)
    in_specs = (
        P("ep", SUB),
        P("ep", None),
        P("ep", None),
        P("ep", SUB),
        P("ep", None, SUB),
        P("ep", None, SUB),
        P("ep", SUB, None),
    )
    out_specs = (
        P("ep", SUB),
        P("ep", None),
        P("ep", None, SUB),
        P("ep", None, SUB),
        P("ep", SUB, None),
    )
    return jax.shard_map(
        per_device, mesh=mesh2, in_specs=in_specs, out_specs=out_specs, check_vma=False
    )
```

```python
import functools

import jax
import jax.numpy as jnp
import numpy as np
from jax import lax
from jax.experimental import pallas as pl
from jax.experimental.pallas import tpu as pltpu
from jax.sharding import Mesh
from jax.sharding import PartitionSpec as P

EXPERTS = 8
CAP = 24
SUB = ("z", "x", "core")
MESH_ID = pl.DeviceIdType.MESH


def sub_sizes(etp):
    if etp % 8 == 0:
        return (etp // 8, 4, 2)
    return (etp, 1, 1)


def _coords():
    return (lax.axis_index("ep"), lax.axis_index("z"), lax.axis_index("x"), lax.axis_index("core"))


def _barrier(ne, nz, nx, nc, with_ep):
    e, z, x, c = _coords()
    barrier = pltpu.get_barrier_semaphore()
    count = 0
    for d in range(1, nz):
        pl.semaphore_signal(barrier, inc=1, device_id=(e, (z + d) % nz, x, c), device_id_type=MESH_ID)
        count += 1
    for d in range(1, nx):
        pl.semaphore_signal(barrier, inc=1, device_id=(e, z, (x + d) % nx, c), device_id_type=MESH_ID)
        count += 1
    for d in range(1, nc):
        pl.semaphore_signal(barrier, inc=1, device_id=(e, z, x, (c + d) % nc), device_id_type=MESH_ID)
        count += 1
    if with_ep:
        for d in range(1, ne):
            pl.semaphore_signal(barrier, inc=1, device_id=((e + d) % ne, z, x, c), device_id_type=MESH_ID)
            count += 1
    pl.semaphore_wait(barrier, count)


def _gather_kernel(ne, nz, nx, nc, sent_ref, g_ref, xo_ref, go_ref, rbuf, rg, xa,
                   sem_local, send_0, rsem_0, send_a, recv_a, send_b, recv_b, send_c, recv_c):
    e, z, x, c = _coords()
    _barrier(ne, nz, nx, nc, True)
    sends = []
    own = [pltpu.make_async_copy(sent_ref.at[e], rbuf.at[e], sem_local.at[0]),
           pltpu.make_async_copy(g_ref.at[e], rg.at[e], sem_local.at[1])]
    for cp in own:
        cp.start()
    for t, (src, dst) in enumerate(((sent_ref, rbuf), (g_ref, rg))):
        for d in range(1, ne):
            cp = pltpu.make_async_remote_copy(
                src.at[(e + d) % ne], dst.at[e], send_0.at[t, d - 1], rsem_0.at[t, e],
                device_id=((e + d) % ne, z, x, c), device_id_type=MESH_ID)
            cp.start()
            sends.append(cp)
    for t, (src, dst) in enumerate(((sent_ref, rbuf), (g_ref, rg))):
        for d in range(1, ne):
            srce = (e + ne - d) % ne
            pltpu.make_async_remote_copy(
                src.at[e], dst.at[srce], send_0.at[t, d - 1], rsem_0.at[t, srce],
                device_id=(srce, z, x, c), device_id_type=MESH_ID).wait_recv()
    for cp in own:
        cp.wait()
    feats = xa.shape[0]
    blk = rbuf.shape[2]
    cols = ne * blk
    for b in range(ne):
        piece = rbuf[b]
        xa[:, b * blk:(b + 1) * blk] = piece[:feats]
        xa[:, cols + b * blk:cols + (b + 1) * blk] = piece[feats:]
        go_ref[:, b * blk:(b + 1) * blk] = rg[b]

    out = xo_ref
    local = pltpu.make_async_copy(xa, out.at[z, x, c], sem_local.at[2])
    local.start()
    for d in range(1, nz):
        cp = pltpu.make_async_remote_copy(
            xa, out.at[z, x, c], send_a.at[d - 1], recv_a.at[d - 1],
            device_id=(e, (z + d) % nz, x, c), device_id_type=MESH_ID)
        cp.start()
        sends.append(cp)

    def forward(src, zz, xs, to_x):
        for dc in range(1, nc):
            cp = pltpu.make_async_remote_copy(
                src, out.at[zz, xs, c], send_c.at[dc - 1, xs, zz], recv_c.at[dc - 1, xs, zz],
                device_id=(e, z, x, (c + dc) % nc), device_id_type=MESH_ID)
            cp.start()
            sends.append(cp)
        if to_x:
            for dx in range(1, nx):
                cp = pltpu.make_async_remote_copy(
                    src, out.at[zz, x, c], send_b.at[dx - 1, zz], recv_b.at[dx - 1, zz],
                    device_id=(e, z, (x + dx) % nx, c), device_id_type=MESH_ID)
                cp.start()
                sends.append(cp)

    forward(xa, z, x, True)
    for d in range(1, nz):
        zs = (z + nz - d) % nz
        pltpu.make_async_remote_copy(
            xa, out.at[zs, x, c], send_a.at[d - 1], recv_a.at[d - 1],
            device_id=(e, zs, x, c), device_id_type=MESH_ID).wait_recv()
        forward(out.at[zs, x, c], zs, x, True)
    for dx in range(1, nx):
        xs = (x + nx - dx) % nx
        for zz in range(nz):
            pltpu.make_async_remote_copy(
                xa, out.at[zz, xs, c], send_b.at[dx - 1, zz], recv_b.at[dx - 1, zz],
                device_id=(e, z, xs, c), device_id_type=MESH_ID).wait_recv()
            forward(out.at[zz, xs, c], zz, xs, False)
    for dc in range(1, nc):
        cs = (c + nc - dc) % nc
        for xx in range(nx):
            for zz in range(nz):
                pltpu.make_async_remote_copy(
                    xa, out.at[zz, xx, cs], send_c.at[dc - 1, xx, zz], recv_c.at[dc - 1, xx, zz],
                    device_id=(e, z, x, cs), device_id_type=MESH_ID).wait_recv()
    local.wait()
    for cp in sends:
        cp.wait_send()


def ep_etp_gather(sent, gsend, nz, nx, nc):
    ne, two_feats, blk = sent.shape
    feats = two_feats // 2
    cols = ne * blk
    vmem = pltpu.VMEM
    dma = pltpu.SemaphoreType.DMA
    shape = jax.ShapeDtypeStruct((nz, nx, nc, feats, 2 * cols), sent.dtype)
    return pl.pallas_call(
        functools.partial(_gather_kernel, ne, nz, nx, nc),
        out_shape=(shape, jax.ShapeDtypeStruct((1, cols), gsend.dtype)),
        in_specs=[pl.BlockSpec(memory_space=vmem)] * 2,
        out_specs=(pl.BlockSpec(memory_space=vmem),) * 2,
        scratch_shapes=[
            pltpu.VMEM((ne, two_feats, blk), sent.dtype),
            pltpu.VMEM((ne, 1, blk), gsend.dtype),
            pltpu.VMEM((feats, 2 * cols), sent.dtype),
            dma((3,)),
            dma((2, max(ne - 1, 1))),
            dma((2, ne)),
            dma((max(nz - 1, 1),)),
            dma((max(nz - 1, 1),)),
            dma((max(nx - 1, 1), nz)),
            dma((max(nx - 1, 1), nz)),
            dma((max(nc - 1, 1), nx, nz)),
            dma((max(nc - 1, 1), nx, nz)),
        ],
        compiler_params=pltpu.CompilerParams(collective_id=0, has_side_effects=True),
    )(sent, gsend)


def _rs_kernel(ne, nz, nx, nc, part_ref, partb_ref, inner_ref, out_ref, recv_c, acc1, acc1b, recv_b, acc2, acc2b,
               recv_a, ir_c, in1, ir_b, in2, ir_a, fin,
               sem_local, send_c, rsem_c, send_b, rsem_b, send_a, rsem_a, send_d, rsem_d):
    e, z, x, c = _coords()
    _barrier(ne, nz, nx, nc, True)
    sends = []

    def exchange(pieces, peers_of, send_sem, recv_sem):
        n = len(peers_of)
        for t, (src_of, dst) in enumerate(pieces):
            for d in range(n):
                cp = pltpu.make_async_remote_copy(
                    src_of(d), dst.at[d], send_sem.at[t, d], recv_sem.at[t, d],
                    device_id=peers_of[d][0], device_id_type=MESH_ID)
                cp.start()
                sends.append(cp)
        for t, (src_of, dst) in enumerate(pieces):
            for d in range(n):
                pltpu.make_async_remote_copy(
                    dst.at[d], dst.at[d], send_sem.at[t, d], recv_sem.at[t, d],
                    device_id=peers_of[d][1], device_id_type=MESH_ID).wait_recv()

    order = [(x + k) % nx for k in range(1, nx)] + [x]
    for d in range(1, nc):
        cpeer = (e, z, x, (c + d) % nc)
        for k, xx in enumerate(order):
            cp = pltpu.make_async_remote_copy(
                partb_ref.at[:, xx, (c + d) % nc], recv_c.at[d - 1, :, xx], send_c.at[d - 1, k], rsem_c.at[d - 1, k],
                device_id=cpeer, device_id_type=MESH_ID)
            cp.start()
            sends.append(cp)
        cp = pltpu.make_async_remote_copy(
            inner_ref, ir_c.at[d - 1], send_c.at[d - 1, nx], rsem_c.at[d - 1, nx],
            device_id=cpeer, device_id_type=MESH_ID)
        cp.start()
        sends.append(cp)
    for k, xx in enumerate(order):
        for d in range(1, nc):
            src_peer = (e, z, x, (c + nc - d) % nc)
            pltpu.make_async_remote_copy(
                recv_c.at[d - 1, :, xx], recv_c.at[d - 1, :, xx], send_c.at[d - 1, k], rsem_c.at[d - 1, k],
                device_id=src_peer, device_id_type=MESH_ID).wait_recv()

        def sum_c(zi, carry, xx=xx):
            total = part_ref[zi, xx, c]
            for d in range(nc - 1):
                total = total + recv_c[d, zi, xx].astype(jnp.float32)
            acc1[zi, xx] = total
            acc1b[zi, xx] = total.astype(acc1b.dtype)
            return carry
        lax.fori_loop(0, nz, sum_c, 0)
        if k < nx - 1:
            cp = pltpu.make_async_remote_copy(
                acc1b.at[:, xx], recv_b.at[k], send_b.at[0, k], rsem_b.at[0, k],
                device_id=(e, z, xx, c), device_id_type=MESH_ID)
            cp.start()
            sends.append(cp)
    for d in range(1, nc):
        pltpu.make_async_remote_copy(
            ir_c.at[d - 1], ir_c.at[d - 1], send_c.at[d - 1, nx], rsem_c.at[d - 1, nx],
            device_id=(e, z, x, (c + nc - d) % nc), device_id_type=MESH_ID).wait_recv()
    total = inner_ref[...]
    for d in range(nc - 1):
        total = total + ir_c[d]
    in1[...] = total

    for k in range(nx - 1):
        cp = pltpu.make_async_remote_copy(
            in1, ir_b.at[k], send_b.at[1, k], rsem_b.at[1, k],
            device_id=(e, z, (x + k + 1) % nx, c), device_id_type=MESH_ID)
        cp.start()
        sends.append(cp)
    for k in range(nx - 1):
        xs = (x + nx - k - 1) % nx
        pltpu.make_async_remote_copy(
            recv_b.at[k], recv_b.at[k], send_b.at[0, k], rsem_b.at[0, k],
            device_id=(e, z, xs, c), device_id_type=MESH_ID).wait_recv()
        pltpu.make_async_remote_copy(
            ir_b.at[k], ir_b.at[k], send_b.at[1, k], rsem_b.at[1, k],
            device_id=(e, z, xs, c), device_id_type=MESH_ID).wait_recv()

    def sum_b(zi, carry):
        total = acc1[zi, x]
        for d in range(nx - 1):
            total = total + recv_b[d, zi].astype(jnp.float32)
        acc2[zi] = total
        acc2b[zi] = total.astype(acc2b.dtype)
        return carry
    lax.fori_loop(0, nz, sum_b, 0)
    total = in1[...]
    for d in range(nx - 1):
        total = total + ir_b[d]
    in2[...] = total

    peers = [((e, (z + d) % nz, x, c), (e, (z + nz - d) % nz, x, c)) for d in range(1, nz)]
    exchange([(lambda d: acc2b.at[(z + d + 1) % nz], recv_a), (lambda d: in2, ir_a)],
             peers, send_a, rsem_a)
    total = acc2[z]
    for d in range(nz - 1):
        total = total + recv_a[d].astype(jnp.float32)
    itotal = in2[...]
    for d in range(nz - 1):
        itotal = itotal + ir_a[d]

    half = total.shape[0]
    feats = 2 * half
    blk = fin.shape[2]
    cols = ne * blk
    for b in range(ne):
        fin[b, :half, :] = total[:, b * blk:(b + 1) * blk]
        fin[b, half:feats, :] = total[:, cols + b * blk:cols + (b + 1) * blk]
        fin[b, feats:feats + 1, :] = itotal[:, b * blk:(b + 1) * blk]
        fin[b, feats + 1:, :] = jnp.zeros((fin.shape[1] - feats - 1, blk), jnp.float32)
    local = pltpu.make_async_copy(fin.at[e], out_ref.at[e], sem_local.at[0])
    local.start()
    for d in range(1, ne):
        cp = pltpu.make_async_remote_copy(
            fin.at[(e + d) % ne], out_ref.at[e], send_d.at[d - 1], rsem_d.at[e],
            device_id=((e + d) % ne, z, x, c), device_id_type=MESH_ID)
        cp.start()
        sends.append(cp)
    for d in range(1, ne):
        src = (e + ne - d) % ne
        pltpu.make_async_remote_copy(
            fin.at[e], out_ref.at[src], send_d.at[d - 1], rsem_d.at[src],
            device_id=(src, z, x, c), device_id_type=MESH_ID).wait_recv()
    local.wait()
    for cp in sends:
        cp.wait_send()


def etp_reduce_scatter(part, inner, ne, blk):
    bf16 = jnp.bfloat16
    nz, nx, nc, feats, cols = part.shape
    pad_rows = -(-(2 * feats + 1) // 8) * 8
    f32 = jnp.float32
    vmem = pltpu.VMEM
    dma = pltpu.SemaphoreType.DMA
    mc, mx, mz = max(nc - 1, 1), max(nx - 1, 1), max(nz - 1, 1)
    return pl.pallas_call(
        functools.partial(_rs_kernel, ne, nz, nx, nc),
        out_shape=jax.ShapeDtypeStruct((ne, pad_rows, blk), f32),
        in_specs=[pl.BlockSpec(memory_space=vmem)] * 3,
        out_specs=pl.BlockSpec(memory_space=vmem),
        scratch_shapes=[
            pltpu.VMEM((mc, nz, nx, feats, cols), bf16),
            pltpu.VMEM((nz, nx, feats, cols), f32),
            pltpu.VMEM((nz, nx, feats, cols), bf16),
            pltpu.VMEM((mx, nz, feats, cols), bf16),
            pltpu.VMEM((nz, feats, cols), f32),
            pltpu.VMEM((nz, feats, cols), bf16),
            pltpu.VMEM((mz, feats, cols), bf16),
            pltpu.VMEM((mc, 1, cols // 2), f32),
            pltpu.VMEM((1, cols // 2), f32),
            pltpu.VMEM((mx, 1, cols // 2), f32),
            pltpu.VMEM((1, cols // 2), f32),
            pltpu.VMEM((mz, 1, cols // 2), f32),
            pltpu.VMEM((ne, pad_rows, blk), f32),
            dma((1,)),
            dma((mc, nx + 1)),
            dma((mc, nx + 1)),
            dma((2, mx)),
            dma((2, mx)),
            dma((2, mz)),
            dma((2, mz)),
            dma((max(ne - 1, 1),)),
            dma((ne,)),
        ],
        compiler_params=pltpu.CompilerParams(collective_id=1, has_side_effects=True),
    )(part, part.astype(bf16), inner)


def per_device(tokens, routes, route_gates, cotangent, w_gate, w_up, w_down):
    ep_count = lax.axis_size("ep")
    nz, nx, nc = lax.axis_size("z"), lax.axis_size("x"), lax.axis_size("core")
    tok_count, width = tokens.shape
    flat_ids = routes.reshape(-1)
    pair_count = flat_ids.shape[0]
    onehot = (flat_ids[:, None] == jnp.arange(EXPERTS, dtype=jnp.int32)[None, :]).astype(jnp.int32)
    before = jnp.cumsum(onehot, axis=0) - onehot
    slot_id = jnp.sum(before * onehot, axis=1)
    target = flat_ids * CAP + slot_id
    slot_table = (
        jnp.full((EXPERTS * CAP,), pair_count, jnp.int32)
        .at[target]
        .set(jnp.arange(pair_count, dtype=jnp.int32))
    )
    token_of_slot = slot_table // 2
    gate_flat = jnp.concatenate([route_gates.reshape(-1), jnp.zeros((1,), jnp.float32)])
    slot_gate = gate_flat[slot_table]
    xc = jnp.concatenate([tokens, cotangent], axis=1)
    xc_pad = jnp.concatenate([xc, jnp.zeros((1, 2 * width), jnp.bfloat16)], axis=0)
    sent = jnp.transpose(xc_pad[token_of_slot].reshape(ep_count, CAP, 2 * width), (0, 2, 1))
    gsend = slot_gate.reshape(ep_count, 1, CAP)
    rows = ep_count * CAP
    xc_all, gates_recv = ep_etp_gather(sent, gsend, nz, nx, nc)
    feat = nz * nx * nc * width
    xt = xc_all[..., :rows].reshape(feat, rows)
    ct = xc_all[..., rows:].reshape(feat, rows)
    slot_g = gates_recv.reshape(1, rows)
    dyt = (slot_g * ct.astype(jnp.float32)).astype(jnp.bfloat16)
    wg, wu, wd = w_gate[0], w_up[0], w_down[0]
    f32 = jnp.float32

    def dims(a, b):
        return (((a,), (b,)), ((), ()))
    gu_pre = lax.dot_general(xt, jnp.concatenate([wg, wu], axis=1), dims(0, 0), preferred_element_type=f32)
    gate_pre = gu_pre[:, :wg.shape[1]]
    up_pre = gu_pre[:, wg.shape[1]:]
    sigma = jax.nn.sigmoid(gate_pre)
    hidden = (jax.nn.silu(gate_pre) * up_pre).astype(jnp.bfloat16)
    out_t = lax.dot_general(wd, hidden, dims(0, 1), preferred_element_type=f32)
    dh_wc = lax.dot_general(jnp.concatenate([dyt, ct], axis=1), wd, dims(0, 1), preferred_element_type=f32)
    d_hidden = dh_wc[:rows]
    d_up = (d_hidden * jax.nn.silu(gate_pre)).astype(jnp.bfloat16)
    d_gate = (d_hidden * up_pre * sigma * (1.0 + gate_pre * (1.0 - sigma))).astype(jnp.bfloat16)
    grad_down = lax.dot_general(hidden, dyt, dims(0, 1), preferred_element_type=f32)
    hid = d_gate.shape[1]
    grad_gu = lax.dot_general(xt, jnp.concatenate([d_gate, d_up], axis=1), dims(1, 0), preferred_element_type=f32)
    grad_gate_w = grad_gu[:, :hid]
    grad_up_w = grad_gu[:, hid:]
    inner = jnp.sum(hidden.astype(f32) * dh_wc[rows:], axis=1)[None, :]
    part = out_t.reshape(nz, nx, nc, width // 2, 2 * rows)
    back = etp_reduce_scatter(part, inner, ep_count, CAP)
    half = width // 2
    feats_back = back[:, :width].reshape(EXPERTS, 2, half, CAP)
    feats_back = jnp.transpose(feats_back, (0, 3, 2, 1)).reshape(EXPERTS * CAP, width)
    inner_back = back[:, width].reshape(EXPERTS * CAP)
    pair_rows = feats_back[target].reshape(tok_count, 2, width)
    mixed = jnp.sum(route_gates[:, :, None] * pair_rows, axis=1).astype(jnp.bfloat16)
    grad_gates = inner_back[target].reshape(tok_count, 2)
    return (
        mixed,
        grad_gates,
        grad_gate_w.astype(jnp.bfloat16)[None],
        grad_up_w.astype(jnp.bfloat16)[None],
        grad_down.astype(jnp.bfloat16)[None],
    )


def solution(mesh):
    ep = mesh.shape["ep"]
    etp = mesh.shape["etp"]
    nz, nx, nc = sub_sizes(etp)
    devs = np.asarray(mesh.devices).reshape(ep, nz, nx, nc)
    mesh2 = Mesh(devs, ("ep",) + SUB)
    in_specs = (
        P("ep", SUB),
        P("ep", None),
        P("ep", None),
        P("ep", SUB),
        P("ep", None, SUB),
        P("ep", None, SUB),
        P("ep", SUB, None),
    )
    out_specs = (
        P("ep", SUB),
        P("ep", None),
        P("ep", None, SUB),
        P("ep", None, SUB),
        P("ep", SUB, None),
    )
    return jax.shard_map(
        per_device, mesh=mesh2, in_specs=in_specs, out_specs=out_specs, check_vma=False
    )
```

```python
import functools

import jax
import jax.numpy as jnp
import numpy as np
from jax import lax
from jax.experimental import pallas as pl
from jax.experimental.pallas import tpu as pltpu
from jax.sharding import Mesh
from jax.sharding import PartitionSpec as P

EXPERTS = 8
CAP = 24
SUB = ("z", "x", "core")
MESH_ID = pl.DeviceIdType.MESH


def sub_sizes(etp):
    if etp % 8 == 0:
        return (etp // 8, 4, 2)
    return (etp, 1, 1)


def _coords():
    return (lax.axis_index("ep"), lax.axis_index("z"), lax.axis_index("x"), lax.axis_index("core"))


def _barrier(ne, nz, nx, nc, with_ep):
    e, z, x, c = _coords()
    barrier = pltpu.get_barrier_semaphore()
    count = 0
    for d in range(1, nz):
        pl.semaphore_signal(barrier, inc=1, device_id=(e, (z + d) % nz, x, c), device_id_type=MESH_ID)
        count += 1
    for d in range(1, nx):
        pl.semaphore_signal(barrier, inc=1, device_id=(e, z, (x + d) % nx, c), device_id_type=MESH_ID)
        count += 1
    for d in range(1, nc):
        pl.semaphore_signal(barrier, inc=1, device_id=(e, z, x, (c + d) % nc), device_id_type=MESH_ID)
        count += 1
    if with_ep:
        for d in range(1, ne):
            pl.semaphore_signal(barrier, inc=1, device_id=((e + d) % ne, z, x, c), device_id_type=MESH_ID)
            count += 1
    pl.semaphore_wait(barrier, count)


def _gather_kernel(ne, nz, nx, nc, sent_ref, g_ref, xo_ref, go_ref, rbuf, rg, xa,
                   sem_local, send_0, rsem_0, send_a, recv_a, send_b, recv_b, send_c, recv_c):
    e, z, x, c = _coords()
    _barrier(ne, nz, nx, nc, True)
    sends = []
    own = [pltpu.make_async_copy(sent_ref.at[e], rbuf.at[e], sem_local.at[0]),
           pltpu.make_async_copy(g_ref.at[e], rg.at[e], sem_local.at[1])]
    for cp in own:
        cp.start()
    for t, (src, dst) in enumerate(((sent_ref, rbuf), (g_ref, rg))):
        for d in range(1, ne):
            cp = pltpu.make_async_remote_copy(
                src.at[(e + d) % ne], dst.at[e], send_0.at[t, d - 1], rsem_0.at[t, e],
                device_id=((e + d) % ne, z, x, c), device_id_type=MESH_ID)
            cp.start()
            sends.append(cp)
    for t, (src, dst) in enumerate(((sent_ref, rbuf), (g_ref, rg))):
        for d in range(1, ne):
            srce = (e + ne - d) % ne
            pltpu.make_async_remote_copy(
                src.at[e], dst.at[srce], send_0.at[t, d - 1], rsem_0.at[t, srce],
                device_id=(srce, z, x, c), device_id_type=MESH_ID).wait_recv()
    for cp in own:
        cp.wait()
    feats = xa.shape[0]
    blk = rbuf.shape[2]
    cols = ne * blk
    for b in range(ne):
        piece = rbuf[b]
        xa[:, b * blk:(b + 1) * blk] = piece[:feats]
        xa[:, cols + b * blk:cols + (b + 1) * blk] = piece[feats:]
        go_ref[:, b * blk:(b + 1) * blk] = rg[b]

    out = xo_ref
    local = pltpu.make_async_copy(xa, out.at[z, x, c], sem_local.at[2])
    local.start()
    for d in range(1, nz):
        cp = pltpu.make_async_remote_copy(
            xa, out.at[z, x, c], send_a.at[d - 1], recv_a.at[d - 1],
            device_id=(e, (z + d) % nz, x, c), device_id_type=MESH_ID)
        cp.start()
        sends.append(cp)

    def forward(src, zz, xs, to_x):
        if to_x:
            for dx in range(1, nx):
                cp = pltpu.make_async_remote_copy(
                    src, out.at[zz, x, c], send_b.at[dx - 1, zz], recv_b.at[dx - 1, zz],
                    device_id=(e, z, (x + dx) % nx, c), device_id_type=MESH_ID)
                cp.start()
                sends.append(cp)
        for dc in range(1, nc):
            cp = pltpu.make_async_remote_copy(
                src, out.at[zz, xs, c], send_c.at[dc - 1, xs, zz], recv_c.at[dc - 1, xs, zz],
                device_id=(e, z, x, (c + dc) % nc), device_id_type=MESH_ID)
            cp.start()
            sends.append(cp)

    forward(xa, z, x, True)
    for d in range(1, nz):
        zs = (z + nz - d) % nz
        pltpu.make_async_remote_copy(
            xa, out.at[zs, x, c], send_a.at[d - 1], recv_a.at[d - 1],
            device_id=(e, zs, x, c), device_id_type=MESH_ID).wait_recv()
        forward(out.at[zs, x, c], zs, x, True)
    for dx in range(1, nx):
        xs = (x + nx - dx) % nx
        for zz in range(nz):
            pltpu.make_async_remote_copy(
                xa, out.at[zz, xs, c], send_b.at[dx - 1, zz], recv_b.at[dx - 1, zz],
                device_id=(e, z, xs, c), device_id_type=MESH_ID).wait_recv()
            forward(out.at[zz, xs, c], zz, xs, False)
    for dc in range(1, nc):
        cs = (c + nc - dc) % nc
        for xx in range(nx):
            for zz in range(nz):
                pltpu.make_async_remote_copy(
                    xa, out.at[zz, xx, cs], send_c.at[dc - 1, xx, zz], recv_c.at[dc - 1, xx, zz],
                    device_id=(e, z, x, cs), device_id_type=MESH_ID).wait_recv()
    local.wait()
    for cp in sends:
        cp.wait_send()


def ep_etp_gather(sent, gsend, nz, nx, nc):
    ne, two_feats, blk = sent.shape
    feats = two_feats // 2
    cols = ne * blk
    vmem = pltpu.VMEM
    dma = pltpu.SemaphoreType.DMA
    shape = jax.ShapeDtypeStruct((nz, nx, nc, feats, 2 * cols), sent.dtype)
    return pl.pallas_call(
        functools.partial(_gather_kernel, ne, nz, nx, nc),
        out_shape=(shape, jax.ShapeDtypeStruct((1, cols), gsend.dtype)),
        in_specs=[pl.BlockSpec(memory_space=vmem)] * 2,
        out_specs=(pl.BlockSpec(memory_space=vmem),) * 2,
        scratch_shapes=[
            pltpu.VMEM((ne, two_feats, blk), sent.dtype),
            pltpu.VMEM((ne, 1, blk), gsend.dtype),
            pltpu.VMEM((feats, 2 * cols), sent.dtype),
            dma((3,)),
            dma((2, max(ne - 1, 1))),
            dma((2, ne)),
            dma((max(nz - 1, 1),)),
            dma((max(nz - 1, 1),)),
            dma((max(nx - 1, 1), nz)),
            dma((max(nx - 1, 1), nz)),
            dma((max(nc - 1, 1), nx, nz)),
            dma((max(nc - 1, 1), nx, nz)),
        ],
        compiler_params=pltpu.CompilerParams(collective_id=0, has_side_effects=True),
    )(sent, gsend)


def _rs_kernel(ne, nz, nx, nc, part_ref, inner_ref, out_ref, partb_ref, recv_c, acc1, acc1b, recv_b, acc2, acc2b,
               recv_a, ir_c, in1, ir_b, in2, ir_a, fin,
               sem_local, send_c, rsem_c, send_b, rsem_b, send_a, rsem_a, send_d, rsem_d):
    e, z, x, c = _coords()
    _barrier(ne, nz, nx, nc, True)
    sends = []

    def exchange(pieces, peers_of, send_sem, recv_sem):
        n = len(peers_of)
        for t, (src_of, dst) in enumerate(pieces):
            for d in range(n):
                cp = pltpu.make_async_remote_copy(
                    src_of(d), dst.at[d], send_sem.at[t, d], recv_sem.at[t, d],
                    device_id=peers_of[d][0], device_id_type=MESH_ID)
                cp.start()
                sends.append(cp)
        for t, (src_of, dst) in enumerate(pieces):
            for d in range(n):
                pltpu.make_async_remote_copy(
                    dst.at[d], dst.at[d], send_sem.at[t, d], recv_sem.at[t, d],
                    device_id=peers_of[d][1], device_id_type=MESH_ID).wait_recv()

    order = [(x + k) % nx for k in range(1, nx)] + [x]

    def cast_partner(i, carry):
        zi = i // nx
        xi = i % nx
        for d in range(1, nc):
            partb_ref[d - 1, zi, xi] = part_ref[zi, xi, (c + d) % nc].astype(partb_ref.dtype)
        return carry
    lax.fori_loop(0, nz * nx, cast_partner, 0)
    for d in range(1, nc):
        cpeer = (e, z, x, (c + d) % nc)
        for k, xx in enumerate(order):
            cp = pltpu.make_async_remote_copy(
                partb_ref.at[d - 1, :, xx], recv_c.at[d - 1, :, xx], send_c.at[d - 1, k], rsem_c.at[d - 1, k],
                device_id=cpeer, device_id_type=MESH_ID)
            cp.start()
            sends.append(cp)
        cp = pltpu.make_async_remote_copy(
            inner_ref, ir_c.at[d - 1], send_c.at[d - 1, nx], rsem_c.at[d - 1, nx],
            device_id=cpeer, device_id_type=MESH_ID)
        cp.start()
        sends.append(cp)
    for k, xx in enumerate(order):
        for d in range(1, nc):
            src_peer = (e, z, x, (c + nc - d) % nc)
            pltpu.make_async_remote_copy(
                recv_c.at[d - 1, :, xx], recv_c.at[d - 1, :, xx], send_c.at[d - 1, k], rsem_c.at[d - 1, k],
                device_id=src_peer, device_id_type=MESH_ID).wait_recv()

        def sum_c(zi, carry, xx=xx):
            total = part_ref[zi, xx, c]
            for d in range(nc - 1):
                total = total + recv_c[d, zi, xx].astype(jnp.float32)
            acc1[zi, xx] = total
            acc1b[zi, xx] = total.astype(acc1b.dtype)
            return carry
        lax.fori_loop(0, nz, sum_c, 0)
        if k < nx - 1:
            cp = pltpu.make_async_remote_copy(
                acc1b.at[:, xx], recv_b.at[k], send_b.at[0, k], rsem_b.at[0, k],
                device_id=(e, z, xx, c), device_id_type=MESH_ID)
            cp.start()
            sends.append(cp)
    for d in range(1, nc):
        pltpu.make_async_remote_copy(
            ir_c.at[d - 1], ir_c.at[d - 1], send_c.at[d - 1, nx], rsem_c.at[d - 1, nx],
            device_id=(e, z, x, (c + nc - d) % nc), device_id_type=MESH_ID).wait_recv()
    total = inner_ref[...]
    for d in range(nc - 1):
        total = total + ir_c[d]
    in1[...] = total

    for k in range(nx - 1):
        cp = pltpu.make_async_remote_copy(
            in1, ir_b.at[k], send_b.at[1, k], rsem_b.at[1, k],
            device_id=(e, z, (x + k + 1) % nx, c), device_id_type=MESH_ID)
        cp.start()
        sends.append(cp)
    for k in range(nx - 1):
        xs = (x + nx - k - 1) % nx
        pltpu.make_async_remote_copy(
            recv_b.at[k], recv_b.at[k], send_b.at[0, k], rsem_b.at[0, k],
            device_id=(e, z, xs, c), device_id_type=MESH_ID).wait_recv()
        pltpu.make_async_remote_copy(
            ir_b.at[k], ir_b.at[k], send_b.at[1, k], rsem_b.at[1, k],
            device_id=(e, z, xs, c), device_id_type=MESH_ID).wait_recv()

    def sum_b(zi, carry):
        total = acc1[zi, x]
        for d in range(nx - 1):
            total = total + recv_b[d, zi].astype(jnp.float32)
        acc2[zi] = total
        acc2b[zi] = total.astype(acc2b.dtype)
        return carry
    lax.fori_loop(0, nz, sum_b, 0)
    total = in1[...]
    for d in range(nx - 1):
        total = total + ir_b[d]
    in2[...] = total

    peers = [((e, (z + d) % nz, x, c), (e, (z + nz - d) % nz, x, c)) for d in range(1, nz)]
    exchange([(lambda d: acc2b.at[(z + d + 1) % nz], recv_a), (lambda d: in2, ir_a)],
             peers, send_a, rsem_a)
    total = acc2[z]
    for d in range(nz - 1):
        total = total + recv_a[d].astype(jnp.float32)
    itotal = in2[...]
    for d in range(nz - 1):
        itotal = itotal + ir_a[d]

    half = total.shape[0]
    feats = 2 * half
    blk = fin.shape[2]
    cols = ne * blk
    for b in range(ne):
        fin[b, :half, :] = total[:, b * blk:(b + 1) * blk]
        fin[b, half:feats, :] = total[:, cols + b * blk:cols + (b + 1) * blk]
        fin[b, feats:feats + 1, :] = itotal[:, b * blk:(b + 1) * blk]
        fin[b, feats + 1:, :] = jnp.zeros((fin.shape[1] - feats - 1, blk), jnp.float32)
    local = pltpu.make_async_copy(fin.at[e], out_ref.at[e], sem_local.at[0])
    local.start()
    for d in range(1, ne):
        cp = pltpu.make_async_remote_copy(
            fin.at[(e + d) % ne], out_ref.at[e], send_d.at[d - 1], rsem_d.at[e],
            device_id=((e + d) % ne, z, x, c), device_id_type=MESH_ID)
        cp.start()
        sends.append(cp)
    for d in range(1, ne):
        src = (e + ne - d) % ne
        pltpu.make_async_remote_copy(
            fin.at[e], out_ref.at[src], send_d.at[d - 1], rsem_d.at[src],
            device_id=(src, z, x, c), device_id_type=MESH_ID).wait_recv()
    local.wait()
    for cp in sends:
        cp.wait_send()


def etp_reduce_scatter(part, inner, ne, blk):
    bf16 = jnp.bfloat16
    nz, nx, nc, feats, cols = part.shape
    pad_rows = -(-(2 * feats + 1) // 8) * 8
    f32 = jnp.float32
    vmem = pltpu.VMEM
    dma = pltpu.SemaphoreType.DMA
    mc, mx, mz = max(nc - 1, 1), max(nx - 1, 1), max(nz - 1, 1)
    return pl.pallas_call(
        functools.partial(_rs_kernel, ne, nz, nx, nc),
        out_shape=jax.ShapeDtypeStruct((ne, pad_rows, blk), f32),
        in_specs=[pl.BlockSpec(memory_space=vmem)] * 2,
        out_specs=pl.BlockSpec(memory_space=vmem),
        scratch_shapes=[
            pltpu.VMEM((mc, nz, nx, feats, cols), bf16),
            pltpu.VMEM((mc, nz, nx, feats, cols), bf16),
            pltpu.VMEM((nz, nx, feats, cols), f32),
            pltpu.VMEM((nz, nx, feats, cols), bf16),
            pltpu.VMEM((mx, nz, feats, cols), bf16),
            pltpu.VMEM((nz, feats, cols), f32),
            pltpu.VMEM((nz, feats, cols), bf16),
            pltpu.VMEM((mz, feats, cols), bf16),
            pltpu.VMEM((mc, 1, cols // 2), f32),
            pltpu.VMEM((1, cols // 2), f32),
            pltpu.VMEM((mx, 1, cols // 2), f32),
            pltpu.VMEM((1, cols // 2), f32),
            pltpu.VMEM((mz, 1, cols // 2), f32),
            pltpu.VMEM((ne, pad_rows, blk), f32),
            dma((1,)),
            dma((mc, nx + 1)),
            dma((mc, nx + 1)),
            dma((2, mx)),
            dma((2, mx)),
            dma((2, mz)),
            dma((2, mz)),
            dma((max(ne - 1, 1),)),
            dma((ne,)),
        ],
        compiler_params=pltpu.CompilerParams(collective_id=1, has_side_effects=True),
    )(part, inner)


def per_device(tokens, routes, route_gates, cotangent, w_gate, w_up, w_down):
    ep_count = lax.axis_size("ep")
    nz, nx, nc = lax.axis_size("z"), lax.axis_size("x"), lax.axis_size("core")
    tok_count, width = tokens.shape
    flat_ids = routes.reshape(-1)
    pair_count = flat_ids.shape[0]
    onehot = (flat_ids[:, None] == jnp.arange(EXPERTS, dtype=jnp.int32)[None, :]).astype(jnp.int32)
    before = jnp.cumsum(onehot, axis=0) - onehot
    slot_id = jnp.sum(before * onehot, axis=1)
    target = flat_ids * CAP + slot_id
    slot_table = (
        jnp.full((EXPERTS * CAP,), pair_count, jnp.int32)
        .at[target]
        .set(jnp.arange(pair_count, dtype=jnp.int32))
    )
    token_of_slot = slot_table // 2
    gate_flat = jnp.concatenate([route_gates.reshape(-1), jnp.zeros((1,), jnp.float32)])
    slot_gate = gate_flat[slot_table]
    xc = jnp.concatenate([tokens, cotangent], axis=1)
    xc_pad = jnp.concatenate([xc, jnp.zeros((1, 2 * width), jnp.bfloat16)], axis=0)
    sent = jnp.transpose(xc_pad[token_of_slot].reshape(ep_count, CAP, 2 * width), (0, 2, 1))
    gsend = slot_gate.reshape(ep_count, 1, CAP)
    rows = ep_count * CAP
    xc_all, gates_recv = ep_etp_gather(sent, gsend, nz, nx, nc)
    feat = nz * nx * nc * width
    xt = xc_all[..., :rows].reshape(feat, rows)
    ct = xc_all[..., rows:].reshape(feat, rows)
    slot_g = gates_recv.reshape(1, rows)
    dyt = (slot_g * ct.astype(jnp.float32)).astype(jnp.bfloat16)
    wg, wu, wd = w_gate[0], w_up[0], w_down[0]
    f32 = jnp.float32

    def dims(a, b):
        return (((a,), (b,)), ((), ()))
    gu_pre = lax.dot_general(xt, jnp.concatenate([wg, wu], axis=1), dims(0, 0), preferred_element_type=f32)
    gate_pre = gu_pre[:, :wg.shape[1]]
    up_pre = gu_pre[:, wg.shape[1]:]
    sigma = jax.nn.sigmoid(gate_pre)
    hidden = (jax.nn.silu(gate_pre) * up_pre).astype(jnp.bfloat16)
    out_t = lax.dot_general(wd, hidden, dims(0, 1), preferred_element_type=f32)
    dh_wc = lax.dot_general(jnp.concatenate([dyt, ct], axis=1), wd, dims(0, 1), preferred_element_type=f32)
    d_hidden = dh_wc[:rows]
    d_up = (d_hidden * jax.nn.silu(gate_pre)).astype(jnp.bfloat16)
    d_gate = (d_hidden * up_pre * sigma * (1.0 + gate_pre * (1.0 - sigma))).astype(jnp.bfloat16)
    grad_down = lax.dot_general(hidden, dyt, dims(0, 1), preferred_element_type=f32)
    hid = d_gate.shape[1]
    grad_gu = lax.dot_general(xt, jnp.concatenate([d_gate, d_up], axis=1), dims(1, 0), preferred_element_type=f32)
    grad_gate_w = grad_gu[:, :hid]
    grad_up_w = grad_gu[:, hid:]
    inner = jnp.sum(hidden.astype(f32) * dh_wc[rows:], axis=1)[None, :]
    part = out_t.reshape(nz, nx, nc, width // 2, 2 * rows)
    back = etp_reduce_scatter(part, inner, ep_count, CAP)
    half = width // 2
    feats_back = back[:, :width].reshape(EXPERTS, 2, half, CAP)
    feats_back = jnp.transpose(feats_back, (0, 3, 2, 1)).reshape(EXPERTS * CAP, width)
    inner_back = back[:, width].reshape(EXPERTS * CAP)
    pair_rows = feats_back[target].reshape(tok_count, 2, width)
    mixed = jnp.sum(route_gates[:, :, None] * pair_rows, axis=1).astype(jnp.bfloat16)
    grad_gates = inner_back[target].reshape(tok_count, 2)
    return (
        mixed,
        grad_gates,
        grad_gate_w.astype(jnp.bfloat16)[None],
        grad_up_w.astype(jnp.bfloat16)[None],
        grad_down.astype(jnp.bfloat16)[None],
    )


def solution(mesh):
    ep = mesh.shape["ep"]
    etp = mesh.shape["etp"]
    nz, nx, nc = sub_sizes(etp)
    devs = np.asarray(mesh.devices).reshape(ep, nz, nx, nc)
    mesh2 = Mesh(devs, ("ep",) + SUB)
    in_specs = (
        P("ep", SUB),
        P("ep", None),
        P("ep", None),
        P("ep", SUB),
        P("ep", None, SUB),
        P("ep", None, SUB),
        P("ep", SUB, None),
    )
    out_specs = (
        P("ep", SUB),
        P("ep", None),
        P("ep", None, SUB),
        P("ep", None, SUB),
        P("ep", SUB, None),
    )
    return jax.shard_map(
        per_device, mesh=mesh2, in_specs=in_specs, out_specs=out_specs, check_vma=False
    )
```
